128 devices in a mesh: dp: 16 (over x, y), mp: 8 (over z, core).
Axes of the slice: x: 4, y: 4, z: 4, core: 2. Of those that a mesh axis runs over, the one named last changes fastest.
Arguments:
- samples: bfloat16 [128, 55, 128], P('dp'), may hold values from -6 to 6
- targets: bfloat16 [128, 53, 128], P('dp'), may hold values from -6 to 6
- counts: int32 [16], P('dp'), may hold values from 1 to 7, as said below
- weight_in: float32 [55, 2048], P(None, ('mp', 'dp')), may hold values from -0.875 to 0.875
- weight_mid: float32 [2048, 2048], P('mp', 'dp'), may hold values from -0.125 to 0.125
- weight_top: float32 [2048, 2048], P('dp', 'mp'), may hold values from -0.125 to 0.125
- weight_out: float32 [2048, 53], P(('mp', 'dp')), may hold values from -0.125 to 0.125
- moment_in: float32 [55, 2048], P(None, ('mp', 'dp')), may hold values from -0.15625 to 0.15625
- moment_mid: float32 [2048, 2048], P('mp', 'dp'), may hold values from -0.15625 to 0.15625
- moment_top: float32 [2048, 2048], P('dp', 'mp'), may hold values from -0.15625 to 0.15625
- moment_out: float32 [2048, 53], P(('mp', 'dp')), may hold values from -0.15625 to 0.15625
Outputs:
- new_in: float32 [55, 2048], P(None, ('mp', 'dp'))
- new_mid: float32 [2048, 2048], P('mp', 'dp')
- new_top: float32 [2048, 2048], P('dp', 'mp')
- new_out: float32 [2048, 53], P(('mp', 'dp'))
- mom_in: float32 [55, 2048], P(None, ('mp', 'dp'))
- mom_mid: float32 [2048, 2048], P('mp', 'dp')
- mom_top: float32 [2048, 2048], P('dp', 'mp')
- mom_out: float32 [2048, 53], P(('mp', 'dp'))
The draws below stay inside these ranges and needn't reach their ends.
Inputs may be any that keep to these rules, and one draw needn't show every extreme that they name: Partition p and partition (p + 8) mod 16 form a matched pair whose counts sum to at most 8; some partition has 7.
All inputs are finite; a program needn't handle non-finite values.
Results may differ from the reference program's by a relative error of at most 0.011.
Values may be sent and summed in bfloat16 or wider, within the bound.
A program may use at most 64 MiB of HBM per device.

```python
import math
import jax
import jax.numpy as jnp
from jax import lax

IN = 55
OUT = 53
H = 2048
BLOCK = 128
BLK_DEV = 8
CAP = 4
NBLK = 128
N_DP = 16
N_MP = 8


def draw_counts(key, part):
    pairs = N_DP // 2
    totals = jax.random.randint(jax.random.fold_in(key, 12), (pairs,), 2, 2 * CAP + 1)
    totals = totals.at[0].set(2 * CAP)
    spread = totals // 2
    lower = (totals + 1) // 2
    picks = jax.random.randint(jax.random.fold_in(key, 13), (pairs,), 0, 1 << 20)
    heavy = lower + picks % spread
    heavy = heavy.at[0].set(2 * CAP - 1)
    light = totals - heavy
    flips = jax.random.randint(jax.random.fold_in(key, 14), (pairs,), 0, 2)
    low_half = jnp.where(flips == 1, heavy, light)
    high_half = jnp.where(flips == 1, light, heavy)
    return jnp.concatenate([low_half, high_half]).astype(jnp.int32)


def steps_of(rng, shape, split, smallest, largest):
    level = 1.0
    for axis_at, shards_of in split:
        draws = jax.random.uniform(jax.random.fold_in(jax.random.fold_in(rng, 6), axis_at), (shards_of,), jnp.float32, smallest / len(split), largest / len(split))
        level = level * jnp.repeat(jnp.exp(draws), shape[axis_at] // shards_of).reshape((-1,) + (1,) * (len(shape) - 1 - axis_at))
    return level


def scatter_about(rng, dims, scale, bound, pieces=(), kind=jnp.bfloat16):
    result = jax.random.normal(rng, dims, jnp.float32) * scale
    if len(pieces) > 0:
        result = steps_of(rng, dims, pieces, -0.22, 0.18) * result
    return jnp.clip(result, min=-bound, max=bound).astype(kind)


def setup_inputs(seed: int = 0) -> dict:
    splits = jax.random.split(jax.random.key(seed), 12)
    return {
        "samples": scatter_about(splits[0], (NBLK, IN, BLOCK), 1.0, 6.0, ((0, 16),)),
        "targets": scatter_about(splits[1], (NBLK, OUT, BLOCK), 1.0, 6.0, ((0, 16),)),
        "counts": draw_counts(jax.random.fold_in(splits[11], 71), 0),
        "weight_in": scatter_about(splits[3], (IN, H), IN ** -0.5, 0.875, ((1, 128),), jnp.float32),
        "weight_mid": scatter_about(splits[4], (H, H), H ** -0.5, 0.125, ((0, 8), (1, 16)), jnp.float32),
        "weight_top": scatter_about(splits[5], (H, H), H ** -0.5, 0.125, ((0, 16), (1, 8)), jnp.float32),
        "weight_out": scatter_about(splits[6], (H, OUT), H ** -0.5, 0.125, ((0, 128),), jnp.float32),
        "moment_in": scatter_about(splits[7], (IN, H), 0.01, 0.15625, ((1, 128),), jnp.float32),
        "moment_mid": scatter_about(splits[8], (H, H), 0.01, 0.15625, ((0, 8), (1, 16)), jnp.float32),
        "moment_top": scatter_about(splits[9], (H, H), 0.01, 0.15625, ((0, 16), (1, 8)), jnp.float32),
        "moment_out": scatter_about(splits[10], (H, OUT), 0.01, 0.15625, ((0, 128),), jnp.float32),
    }


momentum_decay = 0.9
learn_rate = 0.05

def gelu_act(value):
    return 0.5 * value * (1.0 + jax.scipy.special.erf(value / math.sqrt(2.0)))

def gelu_slope(value):
    return 0.5 * (1.0 + jax.scipy.special.erf(value / math.sqrt(2.0))) + value * jnp.exp(-0.5 * value * value) / math.sqrt(2.0 * math.pi)

def split_sum(left, right):
    width = left.shape[1] // N_MP
    summed = jnp.zeros((left.shape[0], right.shape[1]), jnp.float32)
    for group in range(N_MP):
        part = jnp.dot(left[:, group * width:(group + 1) * width], right[group * width:(group + 1) * width], preferred_element_type=jnp.float32)
        rounded = lax.optimization_barrier(part.astype(jnp.bfloat16))
        summed = summed + rounded.astype(jnp.float32)
    return summed

def reference(samples, targets, counts, weight_in, weight_mid, weight_top, weight_out, moment_in, moment_mid, moment_top, moment_out):
    inputs = jnp.transpose(samples, (0, 2, 1)).reshape(-1, IN)
    wanted = jnp.transpose(targets, (0, 2, 1)).reshape(-1, OUT).astype(jnp.float32)
    slots = jnp.arange(NBLK, dtype=jnp.int32)
    live = (slots % BLK_DEV < jnp.repeat(counts, BLK_DEV)).astype(jnp.float32)
    row_live = jnp.repeat(live, BLOCK)
    total = jnp.sum(counts).astype(jnp.float32) * BLOCK
    first = weight_in.astype(jnp.bfloat16)
    second = weight_mid.astype(jnp.bfloat16)
    third = weight_top.astype(jnp.bfloat16)
    fourth = weight_out.astype(jnp.bfloat16)
    pre_one = jnp.dot(inputs, first, preferred_element_type=jnp.float32)
    act_one = gelu_act(pre_one).astype(jnp.bfloat16)
    pre_two = split_sum(act_one, second)
    act_two = gelu_act(pre_two).astype(jnp.bfloat16)
    pre_three = jnp.dot(act_two, third, preferred_element_type=jnp.float32)
    act_three = gelu_act(pre_three).astype(jnp.bfloat16)
    predicted = split_sum(act_three, fourth)
    grad_pred = (2.0 / total * (predicted - wanted) * row_live[:, None]).astype(jnp.bfloat16)
    grad_four = jnp.dot(act_three.T, grad_pred, preferred_element_type=jnp.float32)
    delta_three = (jnp.dot(grad_pred, fourth.T, preferred_element_type=jnp.float32) * gelu_slope(pre_three)).astype(jnp.bfloat16)
    grad_three = jnp.dot(act_two.T, delta_three, preferred_element_type=jnp.float32)
    delta_two = (split_sum(delta_three, third.T) * gelu_slope(pre_two)).astype(jnp.bfloat16)
    grad_two = jnp.dot(act_one.T, delta_two, preferred_element_type=jnp.float32)
    delta_one = (jnp.dot(delta_two, second.T, preferred_element_type=jnp.float32) * gelu_slope(pre_one)).astype(jnp.bfloat16)
    grad_one = jnp.dot(inputs.T, delta_one, preferred_element_type=jnp.float32)
    mom_in = momentum_decay * moment_in + grad_one
    mom_mid = momentum_decay * moment_mid + grad_two
    mom_top = momentum_decay * moment_top + grad_three
    mom_out = momentum_decay * moment_out + grad_four
    return (weight_in - learn_rate * mom_in, weight_mid - learn_rate * mom_mid, weight_top - learn_rate * mom_top, weight_out - learn_rate * mom_out, mom_in, mom_mid, mom_top, mom_out)
```

```python
import math

import jax
import jax.numpy as jnp
from jax import lax
from jax.experimental import pallas as pl
from jax.experimental.pallas import tpu as pltpu
from jax.sharding import PartitionSpec as P

momentum_decay = 0.9
learn_rate = 0.05
MESH = pl.DeviceIdType.MESH
f32, bf16 = jnp.float32, jnp.bfloat16
NSEM = 192
HALF = 256


def gelu_act(value):
    return 0.5 * value * (1.0 + lax.erf(value * (1.0 / math.sqrt(2.0))))


def gelu_slope(value):
    return 0.5 * (1.0 + lax.erf(value * (1.0 / math.sqrt(2.0)))) + value * jnp.exp(
        -0.5 * value * value
    ) * (1.0 / math.sqrt(2.0 * math.pi))


def dot(left, right, a, b):
    return lax.dot_general(left, right, (((a,), (b,)), ((), ())), preferred_element_type=f32)


def adv(*tasks):
    for task in tasks:
        next(task, None)


def fin(*tasks):
    tasks = list(tasks)
    while tasks:
        tasks = [t for t in tasks if next(t, "end") != "end"]


def kernel(
    x_ref, y_ref, tile_ref, w2_ref, w3_ref,
    g2_ref, g3_ref, gs_ref,
    xr, yr, cw, ct, w3b, xt, xrow, xtb, h1, a1, d1, a2, a3, h2f, h3, d3, d2, d2t,
    psend, pp, psum, pr, et, erow,
    s2b, s2p, s2a, s2r, s2l,
    g3b, g3a, g3x, g2b, g2a, g2x, gtb, gta, gtx, z2, zt,
    ssem, rsem, lsem,
):
    d, m = lax.axis_index("dp"), lax.axis_index("mp")
    x, y = lax.div(d, 4), lax.rem(d, 4)
    z, core = lax.div(m, 2), lax.rem(m, 2)

    def ring(v, k):
        return lax.rem(v + k, 4)

    def dp_dev(xx, yy):
        return (xx * 4 + yy, m)

    def mp_dev(mm):
        return (d, mm)

    partner = mp_dev(z * 2 + 1 - core)
    zdev = {k: mp_dev(ring(z, k) * 2 + core) for k in (1, 2, 3)}
    mdev = {k: lax.rem(m + k, 8) for k in range(1, 8)}
    pair = dp_dev(ring(x, 2), y)

    count = [0]
    sent = []

    def send(src, dst, dev):
        k = count[0]
        count[0] += 1
        assert k < NSEM
        copy = pltpu.make_async_remote_copy(
            src_ref=src, dst_ref=dst, send_sem=ssem.at[k], recv_sem=rsem.at[k],
            device_id=dev, device_id_type=MESH,
        )
        copy.start()
        sent.append(copy)
        return copy

    barrier = pltpu.get_barrier_semaphore()
    peers = [mp_dev(mdev[k]) for k in range(1, 8)]
    peers += [dp_dev(ring(x, k), y) for k in (1, 2, 3)]
    peers += [dp_dev(x, ring(y, k)) for k in (1, 3)]
    for dev in peers:
        pl.semaphore_signal(barrier, inc=1, device_id=dev, device_id_type=MESH)
    pl.semaphore_wait(barrier, len(peers))

    def gather(buf, part):
        lo = 4 * part
        for phase in (0, 1):
            axis = (phase + part) % 2
            pos = x if axis == 0 else y

            def view(s, a, n):
                ms = slice(lo + a, lo + a + n)
                if axis == 0:
                    return buf.at[s, y, ms] if phase == 0 else buf.at[s, :, ms]
                return buf.at[x, s, ms] if phase == 0 else buf.at[:, s, ms]

            def dev(k):
                return dp_dev(ring(x, k), y) if axis == 0 else dp_dev(x, ring(y, k))

            right, left = dev(1), dev(3)
            own = view(pos, 0, 4)
            a_r = send(own, own, right)
            a_l = send(own, own, left)
            yield
            a_r.wait_recv()
            h0 = view(ring(pos, 3), 0, 2)
            b_r = send(h0, h0, right)
            a_l.wait_recv()
            h1_ = view(ring(pos, 1), 2, 2)
            b_l = send(h1_, h1_, left)
            yield
            b_r.wait_recv()
            b_l.wait_recv()

    def scatter(buf, part, abuf, xbuf, finish):
        lo = 4 * part
        for phase in (0, 1):
            axis = (1 - part) if phase == 0 else part
            pos = x if axis == 0 else y

            def at(t, a, n):
                ms = slice(lo + a, lo + a + n)
                if axis == 0:
                    return (t, y, ms) if phase == 1 else (t, slice(None), ms)
                return (x, t, ms) if phase == 1 else (slice(None), t, ms)

            def dev(k):
                return dp_dev(ring(x, k), y) if axis == 0 else dp_dev(x, ring(y, k))

            def rbuf(i, a, n):
                if phase == 0:
                    return (part, i, slice(None), slice(a, a + n))
                return (part, i, slice(a, a + n))

            rb = abuf if phase == 0 else xbuf
            right, left = dev(1), dev(3)
            a_r = send(buf.at[at(ring(pos, 2), 0, 2)], rb.at[rbuf(0, 0, 2)], right)
            a_l = send(buf.at[at(ring(pos, 2), 2, 2)], rb.at[rbuf(0, 2, 2)], left)
            yield
            a_r.wait_recv()
            i1 = at(ring(pos, 1), 0, 2)
            buf[i1] = (buf[i1].astype(f32) + rb[rbuf(0, 0, 2)].astype(f32)).astype(bf16)
            b_r = send(buf.at[at(ring(pos, 1), 0, 4)], rb.at[rbuf(1, 0, 4)], right)
            a_l.wait_recv()
            i3 = at(ring(pos, 3), 2, 2)
            buf[i3] = (buf[i3].astype(f32) + rb[rbuf(0, 2, 2)].astype(f32)).astype(bf16)
            b_l = send(buf.at[at(ring(pos, 3), 0, 4)], rb.at[rbuf(2, 0, 4)], left)
            yield
            b_r.wait_recv()
            b_l.wait_recv()
            i0 = at(pos, 0, 4)
            total = (
                buf[i0].astype(f32)
                + rb[rbuf(1, 0, 4)].astype(f32)
                + rb[rbuf(2, 0, 4)].astype(f32)
            )
            if phase == 0:
                buf[i0] = total.astype(bf16)
            else:
                finish(lo, total)

    locs = [
        pltpu.make_async_copy(w3_ref, w3b.at[x, y], lsem.at[0]),
        pltpu.make_async_copy(tile_ref, ct.at[x, y, m], lsem.at[1]),
        pltpu.make_async_copy(w2_ref.at[m], cw.at[x, y, m], lsem.at[2]),
    ]
    for c in locs:
        c.start()
    tile_copies = [send(tile_ref, ct.at[x, y, m], mp_dev(mdev[k])) for k in range(1, 8)]
    w2_copies = [send(w2_ref.at[mdev[k]], cw.at[x, y, m], mp_dev(mdev[k])) for k in range(1, 8)]
    x_copy = send(x_ref.at[4:7], xr, pair)
    for c in locs:
        c.wait()
    for c in tile_copies:
        c.wait_recv()
    t_ct = [gather(ct, 0), gather(ct, 1)]
    adv(*t_ct)
    for c in w2_copies:
        c.wait_recv()
    t_cw = [gather(cw, 0), gather(cw, 1)]
    adv(*t_cw)
    t_w3 = [gather(w3b, 0), gather(w3b, 1)]
    for _ in range(3):
        adv(*t_ct)
        adv(*t_cw)
    fin(*t_ct)
    y_copy = send(y_ref.at[4:7], yr, pair)
    adv(*t_w3)

    lane = ct[:, :, 0].reshape(256, 128).astype(f32)[:, 127:128]
    scale = 2.0 / (jnp.sum(lane, axis=0, keepdims=True) * (1.0 / 16.0) * 128.0)
    mine = ct[x, y, 0].astype(f32)[0:1, 127:128]
    theirs = ct[ring(x, 2), y, 0].astype(f32)[0:1, 127:128]

    def pick(ref, recv, q):
        value = ref[q].astype(f32)
        for k in range(3):
            if q - k < 1:
                continue
            take = jnp.broadcast_to(mine, value.shape) == float(q - k)
            value = jnp.where(take, recv[k].astype(f32), value)
        return value

    x_copy.wait_recv()
    xt[...] = jnp.zeros_like(xt)
    for q in range(4):
        xt[q, 0:55] = pick(x_ref, xr, q)
    for q in range(4):
        xtb[:, q * 128:(q + 1) * 128] = xt[q, 0:64].astype(bf16)
        xrow[q * 128:(q + 1) * 128] = jnp.transpose(xt[q]).astype(bf16)

    def rows_of(r):
        return slice(r * HALF, (r + 1) * HALF)

    def chunks(body, n=HALF, step=32):
        lax.fori_loop(0, n // step, lambda i, c: (body(pl.multiple_of(i * step, step)), c)[1], 0)

    def layer_one(r):
        xv = xrow[rows_of(r)]

        def body(k, carry):
            a1[k, rows_of(r)] = dot(xv, ct[:, :, k].reshape(256, 128), 1, 1)

            def act(i):
                rr = pl.ds(r * HALF + i, 32)
                h1[k, rr] = gelu_act(a1[k, rr]).astype(bf16)

            chunks(act)
            return carry

        lax.fori_loop(0, 8, body, 0)

    def slope_one(r, k0, k1):
        def body(k, carry):
            def act(i):
                rr = pl.ds(r * HALF + i, 32)
                a1[k, rr] = gelu_slope(a1[k, rr])

            chunks(act)
            return carry

        lax.fori_loop(k0, k1, body, 0)

    layer_one(0)
    adv(*t_w3)
    layer_one(1)
    fin(*t_cw)

    def layer_two(r):
        total = jnp.zeros((HALF, 256), f32)
        for k in range(8):
            total = total + dot(h1[k, rows_of(r)], cw[:, :, k].reshape(256, 256), 1, 1)
        a2[rows_of(r)] = total

        def act(i):
            rr = pl.ds(r * HALF + i, 32)
            h2f[m, rr] = gelu_act(a2[rr]).astype(bf16)

        chunks(act)

    def h2_task(r):
        def blk(k, cc):
            return h2f.at[ring(z, k) * 2 + cc, rows_of(r)]

        own = blk(0, core)
        a_r = send(own, own, zdev[1])
        a_l = send(own, own, zdev[3])
        waits = [send(own, own, partner)]
        yield
        a_r.wait_recv()
        from_left = blk(3, core)
        if r == 0:
            b = send(from_left, from_left, zdev[1])
        waits.append(send(from_left, from_left, partner))
        a_l.wait_recv()
        from_right = blk(1, core)
        if r == 1:
            b = send(from_right, from_right, zdev[3])
        waits.append(send(from_right, from_right, partner))
        yield
        b.wait_recv()
        far = blk(2, core)
        waits.append(send(far, far, partner))
        yield
        for c in waits:
            c.wait_recv()

    layer_two(0)
    t_h2 = [h2_task(0), h2_task(1)]
    adv(t_h2[0])
    layer_two(1)
    adv(t_h2[1])
    slope_one(0, 0, 4)
    adv(*t_h2)
    adv(*t_w3)
    slope_one(0, 4, 8)
    adv(*t_h2)
    fin(*t_w3)
    slope_one(1, 0, 4)
    fin(t_h2[0])

    tm = ct[:, :, m].reshape(256, 128)

    def layer_three(r):
        total = jnp.zeros((HALF, 256), f32)
        for k in range(8):
            total = total + dot(h2f[k, rows_of(r)], w3b[:, :, k].reshape(256, 256), 1, 0)
        a3[rows_of(r)] = total

        def act(i):
            rr = pl.ds(r * HALF + i, 32)
            v = a3[rr]
            h3[rr] = gelu_act(v).astype(bf16)
            a3[rr] = gelu_slope(v)

        chunks(act)
        part = dot(h3[rows_of(r)], tm, 1, 0)
        psend[r] = jnp.transpose(part)[64:128].astype(bf16)

    def p_task(r):
        c = send(psend.at[r], pp.at[r], partner)
        yield
        c.wait_recv()
        psum[r] = (psend[r].astype(f32) + pp[r].astype(f32)).astype(bf16)
        cs = [send(psum.at[r], pr.at[r, k - 1], zdev[k]) for k in (1, 2, 3)]
        yield
        for c in cs:
            c.wait_recv()

    layer_three(0)
    t_p = [p_task(0), p_task(1)]
    adv(t_p[0])
    fin(t_h2[1])
    adv(t_p[0])
    layer_three(1)
    adv(t_p[1])
    slope_one(1, 4, 8)
    adv(t_p[1])

    def slope_two(r):
        def act(i):
            rr = pl.ds(r * HALF + i, 32)
            a2[rr] = gelu_slope(a2[rr])

        chunks(act)

    slope_two(0)
    y_copy.wait_recv()
    fin(t_p[0])

    sub = lax.broadcasted_iota(jnp.int32, (64, 128), 0)

    def error(r):
        for h in range(2):
            q = 2 * r + h
            ls = slice(h * 128, (h + 1) * 128)
            want = jnp.concatenate([pick(y_ref, yr, q), jnp.zeros((11, 128), f32)], axis=0)
            own_n = jnp.broadcast_to(mine, (64, 128))
            pair_n = jnp.broadcast_to(theirs, (64, 128))
            live = (own_n > float(q)) | (4.0 + float(q) - own_n < pair_n)
            predicted = psum[r, :, ls].astype(f32)
            for k in range(3):
                predicted = predicted + pr[r, k, :, ls].astype(f32)
            value = jnp.broadcast_to(scale, (64, 128)) * (predicted - want)
            value = jnp.where(live & (sub < 53), value, 0.0)
            et[:, q * 128:(q + 1) * 128] = value.astype(bf16)
            tall = jnp.concatenate([jnp.zeros((64, 128), f32), value], axis=0)
            erow[q * 128:(q + 1) * 128] = jnp.transpose(tall).astype(bf16)

    def delta_three(r):
        d3[rows_of(r)] = (dot(erow[rows_of(r)], tm, 1, 1) * a3[rows_of(r)]).astype(bf16)

    s2_p = [{}, {}]

    def s2_part(r):
        dv = d3[rows_of(r)]
        for k in (2, 1, 3, 0):
            zz = ring(z, k)
            for own in (False, True):
                c = zz * 2 + (core if own else 1 - core)
                s2b[c, rows_of(r)] = dot(dv, w3b[:, :, c].reshape(256, 256), 1, 1).astype(bf16)
                if not own:
                    s2_p[r][k] = send(s2b.at[c, rows_of(r)], s2p.at[zz, rows_of(r)], partner)

    def s2_task(r):
        rr = rows_of(r)

        def join(k):
            s2_p[r][k].wait_recv()
            zz = ring(z, k)
            c = zz * 2 + core
            s2b[c, rr] = (s2b[c, rr].astype(f32) + s2p[zz, rr].astype(f32)).astype(bf16)

        join(2)
        a = send(s2b.at[ring(z, 2) * 2 + core, rr], s2a.at[r], zdev[1] if r == 0 else zdev[3])
        join(1)
        join(3)
        yield
        a.wait_recv()
        c = ring(z, 1 if r == 0 else 3) * 2 + core
        s2b[c, rr] = (s2b[c, rr].astype(f32) + s2a[r].astype(f32)).astype(bf16)
        b_r = send(s2b.at[ring(z, 1) * 2 + core, rr], s2r.at[rr], zdev[1])
        b_l = send(s2b.at[ring(z, 3) * 2 + core, rr], s2l.at[rr], zdev[3])
        yield
        s2_p[r][0].wait_recv()
        b_r.wait_recv()
        b_l.wait_recv()
        total = (
            s2b[m, rr].astype(f32) + s2p[z, rr].astype(f32)
            + s2r[rr].astype(f32) + s2l[rr].astype(f32)
        )
        a2[rr] = total * a2[rr]

    error(0)
    delta_three(0)
    s2_part(0)
    t_s2 = [s2_task(0), s2_task(1)]
    adv(t_s2[0])
    slope_two(1)
    fin(t_p[1])
    error(1)
    delta_three(1)
    s2_part(1)
    adv(t_s2[1])
    adv(t_s2[0])

    def grad_three(k, carry):
        g3b[:, :, k] = dot(h2f[k], d3[...], 0, 0).astype(bf16).reshape(4, 4, 16, 256)
        return carry

    lax.fori_loop(0, 8, grad_three, 0)

    def finish_three(lo, total):
        g3_ref[lo:lo + 4] = total

    t_g3 = [scatter(g3b, p, g3a, g3x, finish_three) for p in range(2)]
    adv(*t_g3)
    g4 = dot(et[...], h3[...], 1, 0)
    adv(t_s2[1])
    fin(t_s2[0])
    fin(t_s2[1])
    d2[...] = a2[...].astype(bf16)
    d2t[...] = jnp.transpose(a2[...]).astype(bf16)
    adv(*t_g3)

    def grad_two(k, carry):
        g2b[:, :, k] = dot(d2t[...], h1[k], 1, 0).astype(bf16).reshape(4, 4, 16, 256)
        return carry

    lax.fori_loop(0, 8, grad_two, 0)

    def finish_two(lo, total):
        g2b[x, y, lo:lo + 4] = total.astype(bf16)

    t_g2 = [scatter(g2b, p, g2a, g2x, finish_two) for p in range(2)]
    adv(*t_g2)

    def delta_one(k, carry):
        d1[...] = (dot(d2[...], cw[:, :, k].reshape(256, 256), 1, 0) * a1[k]).astype(bf16)
        low = dot(xtb[...], d1[...], 1, 0)
        own = jnp.where(jnp.full((64, 256), k, jnp.int32) == m, g4, 0.0)
        tall = jnp.transpose(jnp.concatenate([low, own], axis=0))
        gtb[:, :, k] = tall.astype(bf16).reshape(4, 4, 16, 128)
        return carry

    lax.fori_loop(0, 8, delta_one, 0)
    adv(*t_g2)

    def finish_tile(lo, total):
        gtb[x, y, lo:lo + 4] = total.astype(bf16)

    t_gt = [scatter(gtb, p, gta, gtx, finish_tile) for p in range(2)]
    adv(*t_gt)
    fin(*t_g3)
    fin(*t_g2)
    g2_copies = [send(g2b.at[x, y, mdev[k]], z2.at[m], mp_dev(mdev[k])) for k in range(1, 8)]
    fin(*t_gt)
    gt_copies = [send(gtb.at[x, y, mdev[k]], zt.at[m], mp_dev(mdev[k])) for k in range(1, 8)]
    z2[m] = g2b[x, y, m]
    zt[m] = gtb[x, y, m]
    for c in g2_copies:
        c.wait_recv()
    g2_ref[...] = jnp.transpose(z2[...].astype(f32).reshape(128, 256))
    for c in gt_copies:
        c.wait_recv()
    gs_ref[...] = jnp.sum(zt[...].astype(f32), axis=0)
    for c in sent:
        c.wait_send()


def run_kernel(samples, targets, tile, w2t, w3):
    vm = pltpu.VMEM
    scratch = [
        vm((3, 55, 128), bf16), vm((3, 53, 128), bf16),
        vm((4, 4, 8, 16, 256), bf16), vm((4, 4, 8, 16, 128), bf16), vm((4, 4, 8, 16, 256), bf16),
        vm((4, 128, 128), f32), vm((512, 128), bf16), vm((64, 512), bf16),
        vm((8, 512, 256), bf16), vm((8, 512, 256), f32), vm((512, 256), bf16),
        vm((512, 256), f32), vm((512, 256), f32),
        vm((8, 512, 256), bf16), vm((512, 256), bf16), vm((512, 256), bf16),
        vm((512, 256), bf16), vm((256, 512), bf16),
        vm((2, 64, 256), bf16), vm((2, 64, 256), bf16), vm((2, 64, 256), bf16),
        vm((2, 3, 64, 256), bf16), vm((64, 512), bf16), vm((512, 128), bf16),
        vm((8, 512, 256), bf16), vm((4, 512, 256), bf16), vm((2, 256, 256), bf16),
        vm((512, 256), bf16), vm((512, 256), bf16),
        vm((4, 4, 8, 16, 256), bf16), vm((2, 3, 4, 4, 16, 256), bf16), vm((2, 3, 4, 16, 256), bf16),
        vm((4, 4, 8, 16, 256), bf16), vm((2, 3, 4, 4, 16, 256), bf16), vm((2, 3, 4, 16, 256), bf16),
        vm((4, 4, 8, 16, 128), bf16), vm((2, 3, 4, 4, 16, 128), bf16), vm((2, 3, 4, 16, 128), bf16),
        vm((8, 16, 256), bf16), vm((8, 16, 128), bf16),
        pltpu.SemaphoreType.DMA((NSEM,)), pltpu.SemaphoreType.DMA((NSEM,)),
        pltpu.SemaphoreType.DMA((3,)),
    ]
    spec = pl.BlockSpec(memory_space=pltpu.VMEM)
    return pl.pallas_call(
        kernel,
        out_shape=(
            jax.ShapeDtypeStruct((256, 128), f32),
            jax.ShapeDtypeStruct((8, 16, 256), f32),
            jax.ShapeDtypeStruct((16, 128), f32),
        ),
        in_specs=[spec] * 5,
        out_specs=[spec] * 3,
        scratch_shapes=scratch,
        compiler_params=pltpu.CompilerParams(
            collective_id=0, has_side_effects=True, vmem_limit_bytes=60 * 1024 * 1024
        ),
        name="train_step",
    )(samples, targets, tile, w2t, w3)


def on_device(
    samples, targets, counts,
    weight_in, weight_mid, weight_top, weight_out,
    moment_in, moment_mid, moment_top, moment_out,
):
    tile = jnp.concatenate(
        [
            weight_in.T, jnp.zeros((16, 9), f32),
            weight_out, jnp.zeros((16, 10), f32),
            jnp.broadcast_to(counts.astype(f32)[None, :], (16, 1)),
        ],
        axis=1,
    ).astype(bf16)
    w2t = weight_mid.T.astype(bf16).reshape(8, 16, 256)
    w3 = weight_top.astype(bf16).reshape(8, 16, 256)
    g_mid, g_top, g_small = run_kernel(samples, targets, tile, w2t, w3)
    g_top = g_top.reshape(128, 256)
    mom_in = momentum_decay * moment_in + g_small[:, :55].T
    mom_mid = momentum_decay * moment_mid + g_mid
    mom_top = momentum_decay * moment_top + g_top
    mom_out = momentum_decay * moment_out + g_small[:, 64:117]
    return (
        weight_in - learn_rate * mom_in,
        weight_mid - learn_rate * mom_mid,
        weight_top - learn_rate * mom_top,
        weight_out - learn_rate * mom_out,
        mom_in,
        mom_mid,
        mom_top,
        mom_out,
    )


def solution(mesh):
    weights = (P(None, ("mp", "dp")), P("mp", "dp"), P("dp", "mp"), P(("mp", "dp"), None))
    in_specs = (P("dp", None, None), P("dp", None, None), P("dp")) + weights + weights
    return jax.shard_map(
        on_device, mesh=mesh, in_specs=in_specs, out_specs=weights + weights, check_vma=False
    )
```

```python
import math

import jax
import jax.numpy as jnp
from jax import lax
from jax.experimental import pallas as pl
from jax.experimental.pallas import tpu as pltpu
from jax.sharding import PartitionSpec as P

momentum_decay = 0.9
learn_rate = 0.05
MESH = pl.DeviceIdType.MESH
f32, bf16 = jnp.float32, jnp.bfloat16
NSEM = 256
HALF = 256


def gelu_act(value):
    return 0.5 * value * (1.0 + lax.erf(value * (1.0 / math.sqrt(2.0))))


def gelu_slope(value):
    return 0.5 * (1.0 + lax.erf(value * (1.0 / math.sqrt(2.0)))) + value * jnp.exp(
        -0.5 * value * value
    ) * (1.0 / math.sqrt(2.0 * math.pi))


def dot(left, right, a, b):
    return lax.dot_general(left, right, (((a,), (b,)), ((), ())), preferred_element_type=f32)


def adv(*tasks):
    for task in tasks:
        next(task, None)


def fin(*tasks):
    tasks = list(tasks)
    while tasks:
        tasks = [t for t in tasks if next(t, "end") != "end"]


def kernel(
    x_ref, y_ref, n_ref, win_ref, wmid_ref, wtop_ref, wout_ref,
    g2_ref, g3_ref, gs_ref,
    xf, yf, xs, ys, xr, yr, wide, w2s, cw, ct, w3b, xrow, xtb,
    h1, a1, d1, a2, a3, h2f, h3, d3, d2, d2t,
    psend, pp, psum, pr, et, erow,
    s2b, s2p, s2z,
    g3b, g3a, g3x, g2b, g2a, g2x, gtb, gtp, gtz, gto, gtx, z2,
    ssem, rsem,
):
    d, m = lax.axis_index("dp"), lax.axis_index("mp")
    x, y = lax.div(d, 4), lax.rem(d, 4)
    z, core = lax.div(m, 2), lax.rem(m, 2)

    def ring(v, k):
        return lax.rem(v + k, 4)

    def dp_dev(xx, yy):
        return (xx * 4 + yy, m)

    def mp_dev(mm):
        return (d, mm)

    partner = mp_dev(z * 2 + 1 - core)
    zdev = {k: mp_dev(ring(z, k) * 2 + core) for k in (1, 2, 3)}
    mdev = {k: lax.rem(m + k, 8) for k in range(1, 8)}
    plane = [(i, j) for i in range(4) for j in range(4) if i or j]
    plane.sort(key=lambda t: -((t[0] % 2) + (t[0] == 2) * 2 + (t[1] % 2) + (t[1] == 2) * 2))
    pair = dp_dev(ring(x, 2), y)

    count = [0]
    sent = []

    def send(src, dst, dev):
        k = count[0]
        count[0] += 1
        assert k < NSEM
        copy = pltpu.make_async_remote_copy(
            src_ref=src, dst_ref=dst, send_sem=ssem.at[k], recv_sem=rsem.at[k],
            device_id=dev, device_id_type=MESH,
        )
        copy.start()
        sent.append(copy)
        return copy

    barrier = pltpu.get_barrier_semaphore()
    peers = [dp_dev(ring(x, i), ring(y, j)) for i, j in plane]
    peers += [mp_dev(mdev[k]) for k in range(1, 8)]
    for dev in peers:
        pl.semaphore_signal(barrier, inc=1, device_id=dev, device_id_type=MESH)

    lanes = lax.broadcasted_iota(jnp.int32, (16, 128), 1)
    wide[...] = jnp.zeros_like(wide)
    wide[0, :, 0:55] = win_ref[...]
    wide[1, :, 0:53] = wout_ref[...]
    tile = wide[0] + pltpu.roll(wide[1], 64, 1)
    tile = jnp.where(lanes == 127, jnp.full((16, 128), n_ref[0], jnp.int32).astype(f32), tile)
    ct[m, x, y] = tile.astype(bf16)
    w2s[...] = jnp.transpose(wmid_ref[...]).astype(bf16).reshape(8, 16, 256)
    w3b[x, y] = wtop_ref[...].astype(bf16).reshape(8, 16, 256)
    cw[x, y, m] = w2s[m]
    xf[...] = jnp.zeros_like(xf)
    yf[...] = jnp.zeros_like(yf)
    xf[:, 0:55] = jnp.transpose(x_ref[...].astype(f32), (1, 0, 2))
    yf[:, 0:53] = jnp.transpose(y_ref[...].astype(f32), (1, 0, 2))
    for q in range(3):
        xs[q] = xf[4 + q, 0:64].astype(bf16)
        ys[q] = yf[4 + q].astype(bf16)
    pl.semaphore_wait(barrier, len(peers))

    def gather(buf, part):
        ms = slice(4 * part, 4 * part + 4)
        pos = (x, y) if part == 0 else (y, x)

        def at(a, b):
            return buf.at[a, b, ms] if part == 0 else buf.at[b, a, ms]

        def dev(a, b):
            return dp_dev(a, b) if part == 0 else dp_dev(b, a)

        own = at(pos[0], pos[1])
        first = {k: send(own, own, dev(ring(pos[0], k), pos[1])) for k in (2, 1, 3)}
        waits = [send(own, own, dev(pos[0], ring(pos[1], k))) for k in (2, 1, 3)]
        yield
        for k in (1, 3, 2):
            first[k].wait_recv()
            got = at(ring(pos[0], 4 - k), pos[1])
            waits += [send(got, got, dev(pos[0], ring(pos[1], j))) for j in (2, 1, 3)]
            yield
        for c in waits:
            c.wait_recv()

    def scatter(buf, part, abuf, xbuf, finish):
        lo = 4 * part
        ms = slice(lo, lo + 4)
        up, ap = (x, y) if part == 0 else (y, x)

        def at(u, a):
            return (u, a, ms) if part == 0 else (a, u, ms)

        def dev(u, a):
            return dp_dev(u, a) if part == 0 else dp_dev(a, u)

        first = {}
        for j in (2, 1, 3, 0):
            u = ring(up, j)
            for k in (2, 1, 3):
                first[j, k] = send(
                    buf.at[at(u, ring(ap, k))], abuf.at[part, k - 1, u], dev(up, ring(ap, k))
                )
        yield
        second = {}
        for j in (2, 1, 3, 0):
            u = ring(up, j)
            for k in (2, 1, 3):
                first[j, k].wait_recv()
            total = buf[at(u, ap)].astype(f32)
            for k in (1, 2, 3):
                total = total + abuf[part, k - 1, u].astype(f32)
            if j:
                buf[at(u, ap)] = total.astype(bf16)
                second[j] = send(buf.at[at(u, ap)], xbuf.at[part, j - 1], dev(u, ap))
                yield
        for j in (1, 3, 2):
            second[j].wait_recv()
            total = total + xbuf[part, j - 1].astype(f32)
        finish(lo, total)

    own_tile = ct.at[m, x, y]
    tile_copies = [send(own_tile, own_tile, dp_dev(ring(x, i), ring(y, j))) for i, j in plane]
    w2_copies = [send(w2s.at[mdev[k]], cw.at[x, y, m], mp_dev(mdev[k])) for k in range(1, 8)]
    x_copy = send(xs, xr, pair)
    t_w3 = [gather(w3b, 0), gather(w3b, 1)]
    adv(*t_w3)
    for c in tile_copies:
        c.wait_recv()
    own_block = ct.at[m]
    block_copies = {k: send(own_block, own_block, zdev[k]) for k in (2, 1, 3)}
    partner_blocks = {0: send(own_block, own_block, partner)}
    for c in w2_copies:
        c.wait_recv()
    t_cw = [gather(cw, 0), gather(cw, 1)]
    adv(*t_cw)

    lane = ct[m].reshape(256, 128).astype(f32)[:, 127:128]
    scale = 2.0 / (jnp.sum(lane, axis=0, keepdims=True) * (1.0 / 16.0) * 128.0)
    mine = ct[m, x, y].astype(f32)[0:1, 127:128]
    theirs = ct[m, ring(x, 2), y].astype(f32)[0:1, 127:128]

    def pick(ref, recv, q):
        value = ref[q, 0:64]
        for k in range(3):
            if q - k < 1:
                continue
            take = jnp.broadcast_to(mine, value.shape) == float(q - k)
            value = jnp.where(take, recv[k].astype(f32), value)
        return value

    x_copy.wait_recv()
    for q in range(4):
        value = pick(xf, xr, q)
        xtb[:, q * 128:(q + 1) * 128] = value.astype(bf16)
        tall = jnp.concatenate([value, jnp.zeros((64, 128), f32)], axis=0)
        xrow[q * 128:(q + 1) * 128] = jnp.transpose(tall).astype(bf16)

    def rows_of(r):
        return slice(r * HALF, (r + 1) * HALF)

    def chunks(body, lo=0, n=HALF, step=32):
        lax.fori_loop(0, n // step, lambda i, c: (body(pl.ds(pl.multiple_of(lo + i * step, step), step)), c)[1], 0)

    def layer_one(k):
        a1[k] = dot(xrow[...], ct[k].reshape(256, 128), 1, 1)

        def act(rr):
            h1[k, rr] = gelu_act(a1[k, rr]).astype(bf16)

        chunks(act, 0, 512)

    def slope_one(lo, hi):
        def body(k, carry):
            def act(rr):
                a1[k, rr] = gelu_slope(a1[k, rr])

            chunks(act, 0, 512)
            return carry

        lax.fori_loop(lo, hi, body, 0)

    layer_one(m)
    partner_blocks[0].wait_recv()
    layer_one(z * 2 + 1 - core)
    adv(*t_cw)
    for k in (1, 3, 2):
        block_copies[k].wait_recv()
        blk = ring(z, 4 - k) * 2 + core
        partner_blocks[k] = send(ct.at[blk], ct.at[blk], partner)
        layer_one(blk)
        adv(*t_cw)
    for k in (1, 3, 2):
        partner_blocks[k].wait_recv()
        layer_one(ring(z, 4 - k) * 2 + 1 - core)
        if k != 1:
            adv(*t_w3)
    fin(*t_cw)
    y_copy = send(ys, yr, pair)

    def layer_two(r):
        total = jnp.zeros((HALF, 256), f32)
        for k in range(8):
            total = total + dot(h1[k, rows_of(r)], cw[:, :, k].reshape(256, 256), 1, 1)
        a2[rows_of(r)] = total

        def act(rr):
            h2f[m, rr] = gelu_act(a2[rr]).astype(bf16)

        chunks(act, r * HALF)

    h2_z, h2_p = [{}, {}], [{}, {}]

    def h2_send(r):
        own = h2f.at[m, rows_of(r)]
        for k in (2, 1, 3):
            h2_z[r][k] = send(own, own, zdev[k])
        h2_p[r][0] = send(own, own, partner)

    layer_two(0)
    h2_send(0)
    adv(*t_w3)
    layer_two(1)
    h2_send(1)
    fin(*t_w3)
    slope_one(0, 4)

    tm = ct[m].reshape(256, 128)

    def layer_three(r):
        rows = rows_of(r)

        def part(k):
            return dot(h2f[k, rows], w3b[:, :, k].reshape(256, 256), 1, 0)

        a3[rows] = part(m)
        h2_p[r][0].wait_recv()
        a3[rows] += part(z * 2 + 1 - core)
        for k in (1, 3, 2):
            h2_z[r][k].wait_recv()
            blk = ring(z, 4 - k) * 2 + core
            view = h2f.at[blk, rows]
            h2_p[r][k] = send(view, view, partner)
            a3[rows] += part(blk)
        for k in (1, 3, 2):
            h2_p[r][k].wait_recv()
            a3[rows] += part(ring(z, 4 - k) * 2 + 1 - core)

        def act(rr):
            v = a3[rr]
            h3[rr] = gelu_act(v).astype(bf16)

        chunks(act, r * HALF)
        psend[r] = jnp.transpose(dot(h3[rows], tm, 1, 0))[64:128].astype(bf16)

    def slope_three(r):
        def act(rr):
            a3[rr] = gelu_slope(a3[rr])

        chunks(act, r * HALF)

    def slope_two(r):
        def act(rr):
            a2[rr] = gelu_slope(a2[rr])

        chunks(act, r * HALF)

    def p_task(r):
        c = send(psend.at[r], pp.at[r], partner)
        yield
        c.wait_recv()
        psum[r] = (psend[r].astype(f32) + pp[r].astype(f32)).astype(bf16)
        cs = [send(psum.at[r], pr.at[r, k - 1], zdev[k]) for k in (2, 1, 3)]
        yield
        for c in cs:
            c.wait_recv()

    t_p = [p_task(0), p_task(1)]
    layer_three(0)
    adv(t_p[0])
    slope_three(0)
    adv(t_p[0])
    layer_three(1)
    adv(t_p[1])
    slope_two(0)
    adv(t_p[1])
    y_copy.wait_recv()
    fin(t_p[0])

    sub = lax.broadcasted_iota(jnp.int32, (64, 128), 0)

    def error(r):
        for h in range(2):
            q = 2 * r + h
            ls = slice(h * 128, (h + 1) * 128)
            want = pick(yf, yr, q)
            own_n = jnp.broadcast_to(mine, (64, 128))
            pair_n = jnp.broadcast_to(theirs, (64, 128))
            live = (own_n > float(q)) | (4.0 + float(q) - own_n < pair_n)
            predicted = psum[r, :, ls].astype(f32)
            for k in range(3):
                predicted = predicted + pr[r, k, :, ls].astype(f32)
            value = jnp.broadcast_to(scale, (64, 128)) * (predicted - want)
            value = jnp.where(live & (sub < 53), value, 0.0)
            et[:, q * 128:(q + 1) * 128] = value.astype(bf16)
            tall = jnp.concatenate([jnp.zeros((64, 128), f32), value], axis=0)
            erow[q * 128:(q + 1) * 128] = jnp.transpose(tall).astype(bf16)

    def delta_three(r):
        d3[rows_of(r)] = (dot(erow[rows_of(r)], tm, 1, 1) * a3[rows_of(r)]).astype(bf16)

    s2_d, s2_s = [{}, {}], [{}, {}]

    def s2_part(r):
        dv = d3[rows_of(r)]
        for own in (False, True):
            for k in (2, 1, 3, 0):
                zz = ring(z, k)
                c = zz * 2 + (core if own else 1 - core)
                s2b[c, rows_of(r)] = dot(dv, w3b[:, :, c].reshape(256, 256), 1, 1).astype(bf16)
                if not own:
                    s2_d[r][k] = send(s2b.at[c, rows_of(r)], s2p.at[zz, rows_of(r)], partner)

    def s2_join(r):
        rr = rows_of(r)
        for k in (2, 1, 3):
            s2_d[r][k].wait_recv()
            zz = ring(z, k)
            c = zz * 2 + core
            s2b[c, rr] = (s2b[c, rr].astype(f32) + s2p[zz, rr].astype(f32)).astype(bf16)
            s2_s[r][k] = send(s2b.at[c, rr], s2z.at[k - 1, rr], zdev[k])

    def s2_end(r):
        rr = rows_of(r)
        s2_d[r][0].wait_recv()
        for k in (1, 3, 2):
            s2_s[r][k].wait_recv()
        total = s2b[m, rr].astype(f32) + s2p[z, rr].astype(f32)
        for k in range(3):
            total = total + s2z[k, rr].astype(f32)
        a2[rr] = total * a2[rr]
        d2[rr] = a2[rr].astype(bf16)
        d2t[:, rr] = jnp.transpose(a2[rr]).astype(bf16)

    error(0)
    delta_three(0)
    s2_part(0)
    slope_three(1)
    s2_join(0)
    slope_two(1)
    fin(t_p[1])
    error(1)
    delta_three(1)
    s2_part(1)

    def grad_three(k, carry):
        g3b[:, :, k] = dot(h2f[k], d3[...], 0, 0).astype(bf16).reshape(4, 4, 16, 256)
        return carry

    def finish_three(lo, total):
        g3_ref[lo * 16:(lo + 4) * 16] = total.reshape(64, 256)

    t_g3 = [scatter(g3b, p, g3a, g3x, finish_three) for p in range(2)]
    lax.fori_loop(0, 2, grad_three, 0)
    s2_join(1)
    lax.fori_loop(2, 4, grad_three, 0)
    adv(t_g3[0])
    lax.fori_loop(4, 8, grad_three, 0)
    adv(t_g3[1])
    slope_one(4, 8)
    g4 = dot(et[...], h3[...], 1, 0)
    adv(*t_g3)
    s2_end(0)
    adv(*t_g3)
    s2_end(1)
    adv(*t_g3)

    def grad_two(k, carry):
        g2b[:, :, k] = dot(d2t[...], h1[k], 1, 0).astype(bf16).reshape(4, 4, 16, 256)
        return carry

    def finish_two(lo, total):
        g2b[x, y, lo:lo + 4] = total.astype(bf16)

    t_g2 = [scatter(g2b, p, g2a, g2x, finish_two) for p in range(2)]
    lax.fori_loop(0, 4, grad_two, 0)
    adv(t_g2[0])
    lax.fori_loop(4, 8, grad_two, 0)
    adv(t_g2[1])
    fin(*t_g3)

    def delta_one(k, carry):
        d1[...] = (dot(d2[...], cw[:, :, k].reshape(256, 256), 1, 0) * a1[k]).astype(bf16)
        low = dot(xtb[...], d1[...], 1, 0)
        own = jnp.where(jnp.full((64, 256), k, jnp.int32) == m, g4, 0.0)
        tall = jnp.transpose(jnp.concatenate([low, own], axis=0))
        gtb[lax.div(k, 2), lax.rem(k, 2)] = tall.astype(bf16).reshape(4, 4, 16, 128)
        return carry

    lax.fori_loop(0, 4, delta_one, 0)
    adv(*t_g2)
    lax.fori_loop(4, 8, delta_one, 0)
    gt_d = send(gtb.at[:, 1 - core], gtp, partner)
    adv(*t_g2)
    gt_d.wait_recv()
    gt_z = {}
    for k in (2, 1, 3):
        zz = ring(z, k)
        gtb[zz, core] = (gtb[zz, core].astype(f32) + gtp[zz].astype(f32)).astype(bf16)
        gt_z[k] = send(gtb.at[zz, core], gtz.at[k - 1], zdev[k])
    adv(*t_g2)
    total = gtb[z, core].astype(f32) + gtp[z].astype(f32)
    for k in (1, 3, 2):
        gt_z[k].wait_recv()
        total = total + gtz[k - 1].astype(f32)
    gto[...] = total.astype(bf16)
    gt_x = [
        send(gto.at[ring(x, i), ring(y, j)], gtx.at[n], dp_dev(ring(x, i), ring(y, j)))
        for n, (i, j) in enumerate(plane)
    ]
    fin(*t_g2)
    g2_copies = [send(g2b.at[x, y, mdev[k]], z2.at[m], mp_dev(mdev[k])) for k in range(1, 8)]
    z2[m] = g2b[x, y, m]
    small = gto[x, y].astype(f32)
    for n, c in enumerate(gt_x):
        c.wait_recv()
        small = small + gtx[n].astype(f32)
    gs_ref[...] = small
    for c in g2_copies:
        c.wait_recv()
    g2_ref[...] = jnp.transpose(z2[...].astype(f32).reshape(128, 256))
    for c in sent:
        c.wait_send()


def run_kernel(*args):
    vm = pltpu.VMEM
    grad = [
        vm((4, 4, 8, 16, 256), bf16), vm((2, 3, 4, 4, 16, 256), bf16), vm((2, 3, 4, 16, 256), bf16),
    ]
    scratch = [
        vm((8, 128, 128), f32), vm((8, 64, 128), f32), vm((3, 64, 128), bf16),
        vm((3, 64, 128), bf16), vm((3, 64, 128), bf16), vm((3, 64, 128), bf16),
        vm((2, 16, 128), f32), vm((8, 16, 256), bf16),
        vm((4, 4, 8, 16, 256), bf16), vm((8, 4, 4, 16, 128), bf16), vm((4, 4, 8, 16, 256), bf16),
        vm((512, 128), bf16), vm((64, 512), bf16),
        vm((8, 512, 256), bf16), vm((8, 512, 256), f32), vm((512, 256), bf16),
        vm((512, 256), f32), vm((512, 256), f32),
        vm((8, 512, 256), bf16), vm((512, 256), bf16), vm((512, 256), bf16),
        vm((512, 256), bf16), vm((256, 512), bf16),
        vm((2, 64, 256), bf16), vm((2, 64, 256), bf16), vm((2, 64, 256), bf16),
        vm((2, 3, 64, 256), bf16), vm((64, 512), bf16), vm((512, 128), bf16),
        vm((8, 512, 256), bf16), vm((4, 512, 256), bf16), vm((3, 512, 256), bf16),
        *grad, *grad,
        vm((4, 2, 4, 4, 16, 128), bf16), vm((4, 4, 4, 16, 128), bf16), vm((3, 4, 4, 16, 128), bf16),
        vm((4, 4, 16, 128), bf16), vm((15, 16, 128), bf16), vm((8, 16, 256), bf16),
        pltpu.SemaphoreType.DMA((NSEM,)), pltpu.SemaphoreType.DMA((NSEM,)),
    ]
    spec = pl.BlockSpec(memory_space=pltpu.VMEM)
    return pl.pallas_call(
        kernel,
        out_shape=(
            jax.ShapeDtypeStruct((256, 128), f32),
            jax.ShapeDtypeStruct((128, 256), f32),
            jax.ShapeDtypeStruct((16, 128), f32),
        ),
        in_specs=[spec] * 2 + [pl.BlockSpec(memory_space=pltpu.SMEM)] + [spec] * 4,
        out_specs=[spec] * 3,
        scratch_shapes=scratch,
        compiler_params=pltpu.CompilerParams(
            collective_id=0, has_side_effects=True, vmem_limit_bytes=60 * 1024 * 1024
        ),
        name="train_step",
    )(*args)


def update_kernel(
    g2, g3, gs, w_in, w_mid, w_top, w_out, m_in, m_mid, m_top, m_out,
    nw_in, nw_mid, nw_top, nw_out, nm_in, nm_mid, nm_top, nm_out,
):
    small = gs[...]
    grads = (small[:, 0:55], g2[...], g3[...], pltpu.roll(small, 64, 1)[:, 0:53])
    for grad, w, mo, nw, nm in zip(
        grads, (w_in, w_mid, w_top, w_out), (m_in, m_mid, m_top, m_out),
        (nw_in, nw_mid, nw_top, nw_out), (nm_in, nm_mid, nm_top, nm_out),
    ):
        value = momentum_decay * mo[...] + grad
        nm[...] = value
        nw[...] = w[...] - learn_rate * value


def on_device(
    samples, targets, counts,
    weight_in, weight_mid, weight_top, weight_out,
    moment_in, moment_mid, moment_top, moment_out,
):
    g_mid, g_top, g_small = run_kernel(
        jnp.transpose(samples, (1, 0, 2)), jnp.transpose(targets, (1, 0, 2)), counts,
        weight_in.T, weight_mid, weight_top, weight_out,
    )
    spec = pl.BlockSpec(memory_space=pltpu.VMEM)
    shapes = [(16, 55), (256, 128), (128, 256), (16, 53)] * 2
    out = pl.pallas_call(
        update_kernel,
        out_shape=[jax.ShapeDtypeStruct(s, f32) for s in shapes],
        in_specs=[spec] * 11,
        out_specs=[spec] * 8,
        name="update",
    )(
        g_mid, g_top, g_small, weight_in.T, weight_mid, weight_top, weight_out,
        moment_in.T, moment_mid, moment_top, moment_out,
    )
    return (out[0].T, *out[1:4], out[4].T, *out[5:])


def solution(mesh):
    weights = (P(None, ("mp", "dp")), P("mp", "dp"), P("dp", "mp"), P(("mp", "dp"), None))
    in_specs = (P("dp", None, None), P("dp", None, None), P("dp")) + weights + weights
    return jax.shard_map(
        on_device, mesh=mesh, in_specs=in_specs, out_specs=weights + weights, check_vma=False
    )
```

```python
import math

import jax
import jax.numpy as jnp
from jax import lax
from jax.experimental import pallas as pl
from jax.experimental.pallas import tpu as pltpu
from jax.sharding import PartitionSpec as P

momentum_decay = 0.9
learn_rate = 0.05
MESH = pl.DeviceIdType.MESH
f32, bf16 = jnp.float32, jnp.bfloat16
NSEM = 256
NROW = 4
ROWS = 512 // NROW


def gelu_act(value):
    return 0.5 * value * (1.0 + lax.erf(value * (1.0 / math.sqrt(2.0))))


def gelu_slope(value):
    return 0.5 * (1.0 + lax.erf(value * (1.0 / math.sqrt(2.0)))) + value * jnp.exp(
        -0.5 * value * value
    ) * (1.0 / math.sqrt(2.0 * math.pi))


def dot(left, right, a, b):
    return lax.dot_general(left, right, (((a,), (b,)), ((), ())), preferred_element_type=f32)


def adv(*tasks):
    for task in tasks:
        next(task, None)


def fin(*tasks):
    tasks = list(tasks)
    while tasks:
        tasks = [t for t in tasks if next(t, "end") != "end"]


def kernel(
    x_ref, y_ref, n_ref, win_ref, wmid_ref, wtop_ref, wout_ref,
    g2_ref, g3_ref, gs_ref,
    xf, yf, xs, ys, xr, yr, wide, w2s, cw, ct, w3b, xrow, xtb,
    h1, a1, d1, a2, a3, h2f, h3, d3, d2, d2t,
    psend, pp, psum, pr, et, erow,
    s2b, s2p, s2z,
    g3b, g3a, g3x, g2b, g2a, g2x, g2f, g1f, gtb, gtp, gtz, gto, gtx, z2,
    ssem, rsem,
):
    d, m = lax.axis_index("dp"), lax.axis_index("mp")
    x, y = lax.div(d, 4), lax.rem(d, 4)
    z, core = lax.div(m, 2), lax.rem(m, 2)

    def ring(v, k):
        return lax.rem(v + k, 4)

    def dp_dev(xx, yy):
        return (xx * 4 + yy, m)

    def mp_dev(mm):
        return (d, mm)

    partner = mp_dev(z * 2 + 1 - core)
    zdev = {k: mp_dev(ring(z, k) * 2 + core) for k in (1, 2, 3)}
    mdev = {k: lax.rem(m + k, 8) for k in range(1, 8)}
    plane = [(i, j) for i in range(4) for j in range(4) if i or j]
    plane.sort(key=lambda t: -((t[0] % 2) + (t[0] == 2) * 2 + (t[1] % 2) + (t[1] == 2) * 2))
    pair = dp_dev(ring(x, 2), y)

    count = [0]
    sent = []

    def send(src, dst, dev):
        k = count[0]
        count[0] += 1
        assert k < NSEM
        copy = pltpu.make_async_remote_copy(
            src_ref=src, dst_ref=dst, send_sem=ssem.at[k], recv_sem=rsem.at[k],
            device_id=dev, device_id_type=MESH,
        )
        copy.start()
        sent.append(copy)
        return copy

    barrier = pltpu.get_barrier_semaphore()
    peers = [dp_dev(ring(x, i), ring(y, j)) for i, j in plane]
    peers += [mp_dev(mdev[k]) for k in range(1, 8)]
    for dev in peers:
        pl.semaphore_signal(barrier, inc=1, device_id=dev, device_id_type=MESH)

    lanes = lax.broadcasted_iota(jnp.int32, (16, 128), 1)
    wide[...] = jnp.zeros_like(wide)
    wide[0, :, 0:55] = win_ref[...]
    wide[1, :, 0:53] = wout_ref[...]
    tile = wide[0] + pltpu.roll(wide[1], 64, 1)
    tile = jnp.where(lanes == 127, jnp.full((16, 128), n_ref[0], jnp.int32).astype(f32), tile)
    ct[m, x, y] = tile.astype(bf16)
    w2s[...] = jnp.transpose(wmid_ref[...]).astype(bf16).reshape(8, 16, 256)
    w3b[x, y] = wtop_ref[...].astype(bf16).reshape(8, 16, 256)
    cw[x, y, m] = w2s[m]
    xf[...] = jnp.zeros_like(xf)
    yf[...] = jnp.zeros_like(yf)
    xf[:, 0:55] = jnp.transpose(x_ref[...].astype(f32), (1, 0, 2))
    yf[:, 0:53] = jnp.transpose(y_ref[...].astype(f32), (1, 0, 2))
    for q in range(3):
        xs[q] = xf[4 + q, 0:64].astype(bf16)
        ys[q] = yf[4 + q].astype(bf16)
    pl.semaphore_wait(barrier, len(peers))

    def gather(buf, part):
        ms = slice(4 * part, 4 * part + 4)
        pos = (x, y) if part == 0 else (y, x)

        def at(a, b):
            return buf.at[a, b, ms] if part == 0 else buf.at[b, a, ms]

        def dev(a, b):
            return dp_dev(a, b) if part == 0 else dp_dev(b, a)

        own = at(pos[0], pos[1])
        first = {k: send(own, own, dev(ring(pos[0], k), pos[1])) for k in (2, 1, 3)}
        yield
        waits = [send(own, own, dev(pos[0], ring(pos[1], k))) for k in (2, 1, 3)]
        yield
        for k in (1, 3, 2):
            first[k].wait_recv()
            got = at(ring(pos[0], 4 - k), pos[1])
            waits += [send(got, got, dev(pos[0], ring(pos[1], j))) for j in (2, 1, 3)]
            yield
        for c in waits:
            c.wait_recv()

    def scatter(buf, part, abuf, xbuf, finish):
        lo = 4 * part
        ms = slice(lo, lo + 4)
        up, ap = (x, y) if part == 0 else (y, x)

        def at(u, a):
            return (u, a, ms) if part == 0 else (a, u, ms)

        def dev(u, a):
            return dp_dev(u, a) if part == 0 else dp_dev(a, u)

        first = {}
        for j in (2, 1, 3, 0):
            u = ring(up, j)
            for k in (2, 1, 3):
                first[j, k] = send(
                    buf.at[at(u, ring(ap, k))], abuf.at[part, k - 1, u], dev(up, ring(ap, k))
                )
        yield
        second = {}
        for j in (2, 1, 3, 0):
            u = ring(up, j)
            for k in (2, 1, 3):
                first[j, k].wait_recv()
            total = buf[at(u, ap)].astype(f32)
            for k in (1, 2, 3):
                total = total + abuf[part, k - 1, u].astype(f32)
            if j:
                buf[at(u, ap)] = total.astype(bf16)
                second[j] = send(buf.at[at(u, ap)], xbuf.at[part, j - 1], dev(u, ap))
                yield
        for j in (1, 3, 2):
            second[j].wait_recv()
            total = total + xbuf[part, j - 1].astype(f32)
        finish(lo, total)

    own_tile = ct.at[m, x, y]
    tile_copies = [send(own_tile, own_tile, dp_dev(ring(x, i), ring(y, j))) for i, j in plane]
    w2_copies = [send(w2s.at[mdev[k]], cw.at[x, y, m], mp_dev(mdev[k])) for k in range(1, 8)]
    x_copy = send(xs, xr, pair)
    for c in tile_copies:
        c.wait_recv()
    own_block = ct.at[m]
    block_copies = {k: send(own_block, own_block, zdev[k]) for k in (2, 1, 3)}
    partner_blocks = {0: send(own_block, own_block, partner)}
    for c in w2_copies:
        c.wait_recv()
    t_cw = [gather(cw, 0), gather(cw, 1)]
    t_w3 = [gather(w3b, 0), gather(w3b, 1)]
    adv(*t_cw, *t_cw)
    adv(*t_w3, *t_w3)

    lane = ct[m].reshape(256, 128).astype(f32)[:, 127:128]
    scale = 2.0 / (jnp.sum(lane, axis=0, keepdims=True) * (1.0 / 16.0) * 128.0)
    mine = ct[m, x, y].astype(f32)[0:1, 127:128]
    theirs = ct[m, ring(x, 2), y].astype(f32)[0:1, 127:128]

    def pick(ref, recv, q):
        value = ref[q, 0:64]
        for k in range(3):
            if q - k < 1:
                continue
            take = jnp.broadcast_to(mine, value.shape) == float(q - k)
            value = jnp.where(take, recv[k].astype(f32), value)
        return value

    x_copy.wait_recv()
    for q in range(4):
        value = pick(xf, xr, q)
        xtb[:, q * 128:(q + 1) * 128] = value.astype(bf16)
        tall = jnp.concatenate([value, jnp.zeros((64, 128), f32)], axis=0)
        xrow[q * 128:(q + 1) * 128] = jnp.transpose(tall).astype(bf16)

    def rows_of(r):
        return slice(r * ROWS, (r + 1) * ROWS)

    def chunks(body, lo=0, n=ROWS, step=32):
        lax.fori_loop(0, n // step, lambda i, c: (body(pl.ds(pl.multiple_of(lo + i * step, step), step)), c)[1], 0)

    def layer_one(k):
        a1[k] = dot(xrow[...], ct[k].reshape(256, 128), 1, 1)

        def act(rr):
            h1[k, rr] = gelu_act(a1[k, rr]).astype(bf16)

        chunks(act, 0, 512)

    def slope_one(lo, hi):
        def body(k, carry):
            def act(rr):
                a1[k, rr] = gelu_slope(a1[k, rr])

            chunks(act, 0, 512)
            return carry

        lax.fori_loop(lo, hi, body, 0)

    layer_one(m)
    partner_blocks[0].wait_recv()
    layer_one(z * 2 + 1 - core)
    for _ in range(3):
        adv(*t_cw)
    for k in (1, 3, 2):
        block_copies[k].wait_recv()
        blk = ring(z, 4 - k) * 2 + core
        partner_blocks[k] = send(ct.at[blk], ct.at[blk], partner)
        layer_one(blk)
    for _ in range(3):
        adv(*t_w3)
    y_copy = send(ys, yr, pair)
    for k in (1, 3, 2):
        partner_blocks[k].wait_recv()
        layer_one(ring(z, 4 - k) * 2 + 1 - core)
    slope_one(0, 2)
    fin(*t_cw)

    def layer_two(r):
        total = jnp.zeros((ROWS, 256), f32)
        for k in range(8):
            total = total + dot(h1[k, rows_of(r)], cw[:, :, k].reshape(256, 256), 1, 1)
        a2[rows_of(r)] = total

        def act(rr):
            h2f[m, rr] = gelu_act(a2[rr]).astype(bf16)

        chunks(act, r * ROWS)

    h2_z, h2_p = ([{} for _ in range(NROW)] for _ in range(2))

    def h2_send(r):
        own = h2f.at[m, rows_of(r)]
        for k in (2, 1, 3):
            h2_z[r][k] = send(own, own, zdev[k])
        h2_p[r][0] = send(own, own, partner)

    for r in range(NROW):
        layer_two(r)
        h2_send(r)
    slope_one(2, 4)
    fin(*t_w3)

    tm = ct[m].reshape(256, 128)

    def layer_three(r):
        rows = rows_of(r)

        def part(k):
            return dot(h2f[k, rows], w3b[:, :, k].reshape(256, 256), 1, 0)

        a3[rows] = part(m)
        h2_p[r][0].wait_recv()
        a3[rows] += part(z * 2 + 1 - core)
        for k in (1, 3, 2):
            h2_z[r][k].wait_recv()
            blk = ring(z, 4 - k) * 2 + core
            view = h2f.at[blk, rows]
            h2_p[r][k] = send(view, view, partner)
            a3[rows] += part(blk)
        for k in (1, 3, 2):
            h2_p[r][k].wait_recv()
            a3[rows] += part(ring(z, 4 - k) * 2 + 1 - core)

        def act(rr):
            v = a3[rr]
            h3[rr] = gelu_act(v).astype(bf16)

        chunks(act, r * ROWS)
        psend[r] = jnp.transpose(dot(h3[rows], tm, 1, 0))[64:128].astype(bf16)

    def slope_three(r):
        def act(rr):
            a3[rr] = gelu_slope(a3[rr])

        chunks(act, r * ROWS)

    def slope_two(r):
        def act(rr):
            a2[rr] = gelu_slope(a2[rr])

        chunks(act, r * ROWS)

    def p_task(r):
        c = send(psend.at[r], pp.at[r], partner)
        yield
        c.wait_recv()
        psum[r] = (psend[r].astype(f32) + pp[r].astype(f32)).astype(bf16)
        cs = [send(psum.at[r], pr.at[r, k - 1], zdev[k]) for k in (2, 1, 3)]
        yield
        for c in cs:
            c.wait_recv()

    t_p = [p_task(r) for r in range(NROW)]
    for r in range(NROW):
        layer_three(r)
        adv(t_p[r])
        slope_three(r)
        slope_two(r)
        if r < NROW - 1:
            slope_one(4 + r, 5 + r)
            adv(t_p[r])
    y_copy.wait_recv()

    sub = lax.broadcasted_iota(jnp.int32, (64, 128), 0)

    def error(r):
        for h in range(4 // NROW):
            q = (4 // NROW) * r + h
            ls = slice(h * 128, (h + 1) * 128)
            want = pick(yf, yr, q)
            own_n = jnp.broadcast_to(mine, (64, 128))
            pair_n = jnp.broadcast_to(theirs, (64, 128))
            live = (own_n > float(q)) | (4.0 + float(q) - own_n < pair_n)
            predicted = psum[r, :, ls].astype(f32)
            for k in range(3):
                predicted = predicted + pr[r, k, :, ls].astype(f32)
            value = jnp.broadcast_to(scale, (64, 128)) * (predicted - want)
            value = jnp.where(live & (sub < 53), value, 0.0)
            et[:, q * 128:(q + 1) * 128] = value.astype(bf16)
            tall = jnp.concatenate([jnp.zeros((64, 128), f32), value], axis=0)
            erow[q * 128:(q + 1) * 128] = jnp.transpose(tall).astype(bf16)

    def delta_three(r):
        d3[rows_of(r)] = (dot(erow[rows_of(r)], tm, 1, 1) * a3[rows_of(r)]).astype(bf16)

    s2_d, s2_s = ([{} for _ in range(NROW)] for _ in range(2))

    def s2_part(r):
        dv = d3[rows_of(r)]
        for own in (False, True):
            for k in (2, 1, 3, 0):
                zz = ring(z, k)
                c = zz * 2 + (core if own else 1 - core)
                s2b[c, rows_of(r)] = dot(dv, w3b[:, :, c].reshape(256, 256), 1, 1).astype(bf16)
                if not own:
                    s2_d[r][k] = send(s2b.at[c, rows_of(r)], s2p.at[zz, rows_of(r)], partner)

    def s2_join(r):
        rr = rows_of(r)
        for k in (2, 1, 3):
            s2_d[r][k].wait_recv()
            zz = ring(z, k)
            c = zz * 2 + core
            s2b[c, rr] = (s2b[c, rr].astype(f32) + s2p[zz, rr].astype(f32)).astype(bf16)
            s2_s[r][k] = send(s2b.at[c, rr], s2z.at[k - 1, rr], zdev[k])

    def s2_end(r):
        rr = rows_of(r)
        s2_d[r][0].wait_recv()
        for k in (1, 3, 2):
            s2_s[r][k].wait_recv()
        total = s2b[m, rr].astype(f32) + s2p[z, rr].astype(f32)
        for k in range(3):
            total = total + s2z[k, rr].astype(f32)
        a2[rr] = total * a2[rr]
        d2[rr] = a2[rr].astype(bf16)
        d2t[:, rr] = jnp.transpose(a2[rr]).astype(bf16)

    for r in range(NROW):
        fin(t_p[r])
        error(r)
        delta_three(r)
        s2_part(r)
        if r == 0:
            adv(t_p[NROW - 1])
        else:
            s2_join(r - 1)

    def grad_three(k, carry):
        g3b[:, :, k] = dot(h2f[k], d3[...], 0, 0).astype(bf16).reshape(4, 4, 16, 256)
        return carry

    def finish_three(lo, total):
        g3_ref[lo * 16:(lo + 4) * 16] = total.reshape(64, 256)

    t_g3 = [scatter(g3b, p, g3a, g3x, finish_three) for p in range(2)]
    lax.fori_loop(0, 4, grad_three, 0)
    s2_join(NROW - 1)
    adv(t_g3[0])
    lax.fori_loop(4, 8, grad_three, 0)
    adv(t_g3[1])
    slope_one(7, 8)
    g4 = dot(et[...], h3[...], 1, 0)

    def finish_two(lo, total):
        g2b[x, y, lo:lo + 4] = total.astype(bf16)

    t_g2 = [scatter(g2b, p, g2a, g2x, finish_two) for p in range(2)]

    upper, lower = slice(0, 256), slice(256, 512)

    def grad_two_a(k, carry):
        g2f[k] = dot(d2t[:, upper], h1[k, upper], 1, 0)
        return carry

    def grad_two_b(k, carry):
        total = g2f[k] + dot(d2t[:, lower], h1[k, lower], 1, 0)
        g2b[:, :, k] = total.astype(bf16).reshape(4, 4, 16, 256)
        return carry

    def grad_one(k, half):
        back = dot(d2[half], cw[:, :, k].reshape(256, 256), 1, 0)
        d1[...] = (back * a1[k, half]).astype(bf16)
        return dot(xtb[:, half], d1[...], 1, 0)

    def delta_one_a(k, carry):
        g1f[k] = grad_one(k, upper)
        return carry

    def delta_one_b(side):
        def body(i, carry):
            k = 2 * i + side
            low = g1f[k] + grad_one(k, lower)
            own = jnp.where(jnp.full((64, 256), k, jnp.int32) == m, g4, 0.0)
            tall = jnp.transpose(jnp.concatenate([low, own], axis=0))
            gtb[i, side] = tall.astype(bf16).reshape(4, 4, 16, 128)
            return carry

        lax.fori_loop(0, 4, body, 0)

    for r in range(NROW // 2):
        s2_end(r)
    adv(*t_g3)
    lax.fori_loop(0, 8, grad_two_a, 0)
    adv(*t_g3)
    lax.fori_loop(0, 8, delta_one_a, 0)
    adv(*t_g3)
    for r in range(NROW // 2, NROW):
        s2_end(r)
    lax.fori_loop(0, 4, grad_two_b, 0)
    adv(t_g2[0])
    lax.fori_loop(4, 8, grad_two_b, 0)
    adv(t_g2[1])
    delta_one_b(1 - core)
    gt_d = send(gtb.at[:, 1 - core], gtp, partner)
    delta_one_b(core)
    fin(*t_g3)
    gt_d.wait_recv()
    gt_z = {}
    for k in (2, 1, 3):
        zz = ring(z, k)
        gtb[zz, core] = (gtb[zz, core].astype(f32) + gtp[zz].astype(f32)).astype(bf16)
        gt_z[k] = send(gtb.at[zz, core], gtz.at[k - 1], zdev[k])
    for _ in range(3):
        adv(*t_g2)
    total = gtb[z, core].astype(f32) + gtp[z].astype(f32)
    for k in (1, 3, 2):
        gt_z[k].wait_recv()
        total = total + gtz[k - 1].astype(f32)
    gto[...] = total.astype(bf16)
    gt_x = [
        send(gto.at[ring(x, i), ring(y, j)], gtx.at[n], dp_dev(ring(x, i), ring(y, j)))
        for n, (i, j) in enumerate(plane)
    ]
    fin(*t_g2)
    g2_copies = [send(g2b.at[x, y, mdev[k]], z2.at[m], mp_dev(mdev[k])) for k in range(1, 8)]
    z2[m] = g2b[x, y, m]
    small = gto[x, y].astype(f32)
    for n, c in enumerate(gt_x):
        c.wait_recv()
        small = small + gtx[n].astype(f32)
    gs_ref[...] = small
    for c in g2_copies:
        c.wait_recv()
    g2_ref[...] = jnp.transpose(z2[...].astype(f32).reshape(128, 256))
    for c in sent:
        c.wait_send()


def run_kernel(*args):
    vm = pltpu.VMEM
    grad = [
        vm((4, 4, 8, 16, 256), bf16), vm((2, 3, 4, 4, 16, 256), bf16), vm((2, 3, 4, 16, 256), bf16),
    ]
    scratch = [
        vm((8, 128, 128), f32), vm((8, 64, 128), f32), vm((3, 64, 128), bf16),
        vm((3, 64, 128), bf16), vm((3, 64, 128), bf16), vm((3, 64, 128), bf16),
        vm((2, 16, 128), f32), vm((8, 16, 256), bf16),
        vm((4, 4, 8, 16, 256), bf16), vm((8, 4, 4, 16, 128), bf16), vm((4, 4, 8, 16, 256), bf16),
        vm((512, 128), bf16), vm((64, 512), bf16),
        vm((8, 512, 256), bf16), vm((8, 512, 256), f32), vm((256, 256), bf16),
        vm((512, 256), f32), vm((512, 256), f32),
        vm((8, 512, 256), bf16), vm((512, 256), bf16), vm((512, 256), bf16),
        vm((512, 256), bf16), vm((256, 512), bf16),
        *[vm((NROW, 64, ROWS), bf16)] * 3, vm((NROW, 3, 64, ROWS), bf16), vm((64, 512), bf16), vm((512, 128), bf16),
        vm((8, 512, 256), bf16), vm((4, 512, 256), bf16), vm((3, 512, 256), bf16),
        *grad, *grad, vm((8, 256, 256), f32), vm((8, 64, 256), f32),
        vm((4, 2, 4, 4, 16, 128), bf16), vm((4, 4, 4, 16, 128), bf16), vm((3, 4, 4, 16, 128), bf16),
        vm((4, 4, 16, 128), bf16), vm((15, 16, 128), bf16), vm((8, 16, 256), bf16),
        pltpu.SemaphoreType.DMA((NSEM,)), pltpu.SemaphoreType.DMA((NSEM,)),
    ]
    spec = pl.BlockSpec(memory_space=pltpu.VMEM)
    return pl.pallas_call(
        kernel,
        out_shape=(
            jax.ShapeDtypeStruct((256, 128), f32),
            jax.ShapeDtypeStruct((128, 256), f32),
            jax.ShapeDtypeStruct((16, 128), f32),
        ),
        in_specs=[spec] * 2 + [pl.BlockSpec(memory_space=pltpu.SMEM)] + [spec] * 4,
        out_specs=[spec] * 3,
        scratch_shapes=scratch,
        compiler_params=pltpu.CompilerParams(
            collective_id=0, has_side_effects=True, vmem_limit_bytes=60 * 1024 * 1024
        ),
        name="train_step",
    )(*args)


def update_kernel(
    g2, g3, gs, w_in, w_mid, w_top, w_out, m_in, m_mid, m_top, m_out,
    nw_in, nw_mid, nw_top, nw_out, nm_in, nm_mid, nm_top, nm_out,
):
    small = gs[...]
    grads = (small[:, 0:55], g2[...], g3[...], pltpu.roll(small, 64, 1)[:, 0:53])
    for grad, w, mo, nw, nm in zip(
        grads, (w_in, w_mid, w_top, w_out), (m_in, m_mid, m_top, m_out),
        (nw_in, nw_mid, nw_top, nw_out), (nm_in, nm_mid, nm_top, nm_out),
    ):
        value = momentum_decay * mo[...] + grad
        nm[...] = value
        nw[...] = w[...] - learn_rate * value


def on_device(
    samples, targets, counts,
    weight_in, weight_mid, weight_top, weight_out,
    moment_in, moment_mid, moment_top, moment_out,
):
    g_mid, g_top, g_small = run_kernel(
        jnp.transpose(samples, (1, 0, 2)), jnp.transpose(targets, (1, 0, 2)), counts,
        weight_in.T, weight_mid, weight_top, weight_out,
    )
    spec = pl.BlockSpec(memory_space=pltpu.VMEM)
    shapes = [(16, 55), (256, 128), (128, 256), (16, 53)] * 2
    out = pl.pallas_call(
        update_kernel,
        out_shape=[jax.ShapeDtypeStruct(s, f32) for s in shapes],
        in_specs=[spec] * 11,
        out_specs=[spec] * 8,
        name="update",
    )(
        g_mid, g_top, g_small, weight_in.T, weight_mid, weight_top, weight_out,
        moment_in.T, moment_mid, moment_top, moment_out,
    )
    return (out[0].T, *out[1:4], out[4].T, *out[5:])


def solution(mesh):
    weights = (P(None, ("mp", "dp")), P("mp", "dp"), P("dp", "mp"), P(("mp", "dp"), None))
    in_specs = (P("dp", None, None), P("dp", None, None), P("dp")) + weights + weights
    return jax.shard_map(
        on_device, mesh=mesh, in_specs=in_specs, out_specs=weights + weights, check_vma=False
    )
```

```python
import math

import jax
import jax.numpy as jnp
from jax import lax
from jax.experimental import pallas as pl
from jax.experimental.pallas import tpu as pltpu
from jax.sharding import PartitionSpec as P

momentum_decay = 0.9
learn_rate = 0.05
MESH = pl.DeviceIdType.MESH
f32, bf16 = jnp.float32, jnp.bfloat16
NSEM = 256
NROW = 2
ROWS = 512 // NROW


def gelu_act(value):
    return 0.5 * value * (1.0 + lax.erf(value * (1.0 / math.sqrt(2.0))))


def gelu_slope(value):
    return 0.5 * (1.0 + lax.erf(value * (1.0 / math.sqrt(2.0)))) + value * jnp.exp(
        -0.5 * value * value
    ) * (1.0 / math.sqrt(2.0 * math.pi))


def dot(left, right, a, b):
    return lax.dot_general(left, right, (((a,), (b,)), ((), ())), preferred_element_type=f32)


def adv(*tasks):
    for task in tasks:
        next(task, None)


def fin(*tasks):
    tasks = list(tasks)
    while tasks:
        tasks = [t for t in tasks if next(t, "end") != "end"]


def kernel(
    x_ref, y_ref, n_ref, win_ref, wmid_ref, wtop_ref, wout_ref,
    g2_ref, g3_ref, gs_ref,
    xf, yf, xs, ys, xr, yr, wide, w2s, cw, ct, w3b, xrow, xtb,
    h1, a1, d1, a2, a3, h2f, h3, d3, d2, d2t,
    psend, pp, psum, pr, et, erow,
    s2b, s2p, s2z,
    g3b, g3a, g3x, g2b, g2a, g2x, g2f, g1f, gtb, gtp, gtz, gto, gtx, z2,
    ssem, rsem,
):
    d, m = lax.axis_index("dp"), lax.axis_index("mp")
    x, y = lax.div(d, 4), lax.rem(d, 4)
    z, core = lax.div(m, 2), lax.rem(m, 2)

    def ring(v, k):
        return lax.rem(v + k, 4)

    def dp_dev(xx, yy):
        return (xx * 4 + yy, m)

    def mp_dev(mm):
        return (d, mm)

    partner = mp_dev(z * 2 + 1 - core)
    zdev = {k: mp_dev(ring(z, k) * 2 + core) for k in (1, 2, 3)}
    mdev = {k: lax.rem(m + k, 8) for k in range(1, 8)}
    plane = [(i, j) for i in range(4) for j in range(4) if i or j]
    plane.sort(key=lambda t: -((t[0] % 2) + (t[0] == 2) * 2 + (t[1] % 2) + (t[1] == 2) * 2))
    pair = dp_dev(ring(x, 2), y)

    count = [0]
    sent = []

    def send(src, dst, dev):
        k = count[0]
        count[0] += 1
        assert k < NSEM
        copy = pltpu.make_async_remote_copy(
            src_ref=src, dst_ref=dst, send_sem=ssem.at[k], recv_sem=rsem.at[k],
            device_id=dev, device_id_type=MESH,
        )
        copy.start()
        sent.append(copy)
        return copy

    barrier = pltpu.get_barrier_semaphore()
    peers = [dp_dev(ring(x, i), ring(y, j)) for i, j in plane]
    peers += [mp_dev(mdev[k]) for k in range(1, 8)]
    for dev in peers:
        pl.semaphore_signal(barrier, inc=1, device_id=dev, device_id_type=MESH)

    lanes = lax.broadcasted_iota(jnp.int32, (16, 128), 1)
    wide[...] = jnp.zeros_like(wide)
    wide[0, :, 0:55] = win_ref[...]
    wide[1, :, 0:53] = wout_ref[...]
    tile = wide[0] + pltpu.roll(wide[1], 64, 1)
    tile = jnp.where(lanes == 127, jnp.full((16, 128), n_ref[0], jnp.int32).astype(f32), tile)
    ct[m, x, y] = tile.astype(bf16)
    w2s[...] = jnp.transpose(wmid_ref[...]).astype(bf16).reshape(8, 16, 256)
    w3b[x, y] = wtop_ref[...].astype(bf16).reshape(8, 16, 256)
    cw[x, y, m] = w2s[m]
    xf[...] = jnp.zeros_like(xf)
    yf[...] = jnp.zeros_like(yf)
    xf[:, 0:55] = jnp.transpose(x_ref[...].astype(f32), (1, 0, 2))
    yf[:, 0:53] = jnp.transpose(y_ref[...].astype(f32), (1, 0, 2))
    for q in range(3):
        xs[q] = xf[4 + q, 0:64].astype(bf16)
        ys[q] = yf[4 + q].astype(bf16)
    pl.semaphore_wait(barrier, len(peers))

    def gather(buf, part):
        ms = slice(4 * part, 4 * part + 4)
        pos = (x, y) if part == 0 else (y, x)

        def at(a, b):
            return buf.at[a, b, ms] if part == 0 else buf.at[b, a, ms]

        def dev(a, b):
            return dp_dev(a, b) if part == 0 else dp_dev(b, a)

        own = at(pos[0], pos[1])
        first = {k: send(own, own, dev(ring(pos[0], k), pos[1])) for k in (2, 1, 3)}
        yield
        waits = [send(own, own, dev(pos[0], ring(pos[1], k))) for k in (2, 1, 3)]
        yield
        for k in (1, 3, 2):
            first[k].wait_recv()
            got = at(ring(pos[0], 4 - k), pos[1])
            waits += [send(got, got, dev(pos[0], ring(pos[1], j))) for j in (2, 1, 3)]
            yield
        for c in waits:
            c.wait_recv()

    def scatter(buf, part, abuf, xbuf, finish):
        lo = 4 * part
        ms = slice(lo, lo + 4)
        up, ap = (x, y) if part == 0 else (y, x)

        def at(u, a):
            return (u, a, ms) if part == 0 else (a, u, ms)

        def dev(u, a):
            return dp_dev(u, a) if part == 0 else dp_dev(a, u)

        first = {}
        for j in (2, 1, 3, 0):
            u = ring(up, j)
            for k in (2, 1, 3):
                first[j, k] = send(
                    buf.at[at(u, ring(ap, k))], abuf.at[part, k - 1, u], dev(up, ring(ap, k))
                )
        yield
        second = {}
        for j in (2, 1, 3, 0):
            u = ring(up, j)
            for k in (2, 1, 3):
                first[j, k].wait_recv()
            total = buf[at(u, ap)].astype(f32)
            for k in (1, 2, 3):
                total = total + abuf[part, k - 1, u].astype(f32)
            if j:
                buf[at(u, ap)] = total.astype(bf16)
                second[j] = send(buf.at[at(u, ap)], xbuf.at[part, j - 1], dev(u, ap))
                yield
        for j in (1, 3, 2):
            second[j].wait_recv()
            total = total + xbuf[part, j - 1].astype(f32)
        finish(lo, total)

    own_tile = ct.at[m, x, y]
    w2_copies = [send(w2s.at[mdev[k]], cw.at[x, y, m], mp_dev(mdev[k])) for k in range(1, 8)]
    tile_copies = [send(own_tile, own_tile, dp_dev(ring(x, i), ring(y, j))) for i, j in plane]
    x_copy = send(xs, xr, pair)
    t_cw = [gather(cw, 0), gather(cw, 1)]
    t_w3 = [gather(w3b, 0), gather(w3b, 1)]
    for c in w2_copies:
        c.wait_recv()
    adv(*t_cw, *t_cw)
    adv(*t_w3)
    for c in tile_copies:
        c.wait_recv()
    own_block = ct.at[m]
    block_copies = {k: send(own_block, own_block, zdev[k]) for k in (2, 1, 3)}
    partner_blocks = {0: send(own_block, own_block, partner)}

    lane = ct[m].reshape(256, 128).astype(f32)[:, 127:128]
    scale = 2.0 / (jnp.sum(lane, axis=0, keepdims=True) * (1.0 / 16.0) * 128.0)
    mine = ct[m, x, y].astype(f32)[0:1, 127:128]
    theirs = ct[m, ring(x, 2), y].astype(f32)[0:1, 127:128]

    def pick(ref, recv, q):
        value = ref[q, 0:64]
        for k in range(3):
            if q - k < 1:
                continue
            take = jnp.broadcast_to(mine, value.shape) == float(q - k)
            value = jnp.where(take, recv[k].astype(f32), value)
        return value

    x_copy.wait_recv()
    for q in range(4):
        value = pick(xf, xr, q)
        xtb[:, q * 128:(q + 1) * 128] = value.astype(bf16)
        tall = jnp.concatenate([value, jnp.zeros((64, 128), f32)], axis=0)
        xrow[q * 128:(q + 1) * 128] = jnp.transpose(tall).astype(bf16)

    def rows_of(r):
        return slice(r * ROWS, (r + 1) * ROWS)

    def chunks(body, lo=0, n=ROWS, step=32):
        lax.fori_loop(0, n // step, lambda i, c: (body(pl.ds(pl.multiple_of(lo + i * step, step), step)), c)[1], 0)

    def layer_one(k):
        a1[k] = dot(xrow[...], ct[k].reshape(256, 128), 1, 1)

        def act(rr):
            h1[k, rr] = gelu_act(a1[k, rr]).astype(bf16)

        chunks(act, 0, 512)

    def slope_one(lo, hi):
        def body(k, carry):
            def act(rr):
                a1[k, rr] = gelu_slope(a1[k, rr])

            chunks(act, 0, 512)
            return carry

        lax.fori_loop(lo, hi, body, 0)

    layer_one(m)
    adv(*t_cw)
    adv(*t_cw)
    partner_blocks[0].wait_recv()
    layer_one(z * 2 + 1 - core)
    adv(*t_cw)
    adv(*t_w3)
    for k in (1, 3, 2):
        block_copies[k].wait_recv()
        blk = ring(z, 4 - k) * 2 + core
        partner_blocks[k] = send(ct.at[blk], ct.at[blk], partner)
        layer_one(blk)
    y_copy = send(ys, yr, pair)
    for k in (1, 3, 2):
        partner_blocks[k].wait_recv()
        layer_one(ring(z, 4 - k) * 2 + 1 - core)
    fin(*t_cw)

    def layer_two(r):
        total = jnp.zeros((ROWS, 256), f32)
        for k in range(8):
            total = total + dot(h1[k, rows_of(r)], cw[:, :, k].reshape(256, 256), 1, 1)
        a2[rows_of(r)] = total

        def act(rr):
            h2f[m, rr] = gelu_act(a2[rr]).astype(bf16)

        chunks(act, r * ROWS)

    h2_z, h2_p = ([{} for _ in range(NROW)] for _ in range(2))

    def h2_send(r):
        own = h2f.at[m, rows_of(r)]
        for k in (2, 1, 3):
            h2_z[r][k] = send(own, own, zdev[k])
        h2_p[r][0] = send(own, own, partner)

    layer_two(0)
    h2_send(0)
    for _ in range(3):
        adv(*t_w3)
    layer_two(1)
    h2_send(1)
    slope_one(0, 8)
    fin(*t_w3)

    tm = ct[m].reshape(256, 128)

    def layer_three(r):
        rows = rows_of(r)

        def part(k):
            return dot(h2f[k, rows], w3b[:, :, k].reshape(256, 256), 1, 0)

        a3[rows] = part(m)
        h2_p[r][0].wait_recv()
        a3[rows] += part(z * 2 + 1 - core)
        for k in (1, 3, 2):
            h2_z[r][k].wait_recv()
            blk = ring(z, 4 - k) * 2 + core
            view = h2f.at[blk, rows]
            h2_p[r][k] = send(view, view, partner)
            a3[rows] += part(blk)
        for k in (1, 3, 2):
            h2_p[r][k].wait_recv()
            a3[rows] += part(ring(z, 4 - k) * 2 + 1 - core)

        def act(rr):
            v = a3[rr]
            h3[rr] = gelu_act(v).astype(bf16)

        chunks(act, r * ROWS)
        psend[r] = jnp.transpose(dot(h3[rows], tm, 1, 0))[64:128].astype(bf16)

    def slope_three(r):
        def act(rr):
            a3[rr] = gelu_slope(a3[rr])

        chunks(act, r * ROWS)

    def slope_two(r):
        def act(rr):
            a2[rr] = gelu_slope(a2[rr])

        chunks(act, r * ROWS)

    def p_task(r):
        c = send(psend.at[r], pp.at[r], partner)
        yield
        c.wait_recv()
        psum[r] = (psend[r].astype(f32) + pp[r].astype(f32)).astype(bf16)
        cs = [send(psum.at[r], pr.at[r, k - 1], zdev[k]) for k in (2, 1, 3)]
        yield
        for c in cs:
            c.wait_recv()

    t_p = [p_task(r) for r in range(NROW)]
    slope_two(0)
    slope_two(1)
    layer_three(0)
    adv(t_p[0])
    slope_three(0)
    adv(t_p[0])
    layer_three(1)
    adv(t_p[1])
    slope_three(1)
    adv(t_p[1])
    y_copy.wait_recv()
    fin(t_p[0])

    sub = lax.broadcasted_iota(jnp.int32, (64, 128), 0)

    def error(r):
        for h in range(4 // NROW):
            q = (4 // NROW) * r + h
            ls = slice(h * 128, (h + 1) * 128)
            want = pick(yf, yr, q)
            own_n = jnp.broadcast_to(mine, (64, 128))
            pair_n = jnp.broadcast_to(theirs, (64, 128))
            live = (own_n > float(q)) | (4.0 + float(q) - own_n < pair_n)
            predicted = psum[r, :, ls].astype(f32)
            for k in range(3):
                predicted = predicted + pr[r, k, :, ls].astype(f32)
            value = jnp.broadcast_to(scale, (64, 128)) * (predicted - want)
            value = jnp.where(live & (sub < 53), value, 0.0)
            et[:, q * 128:(q + 1) * 128] = value.astype(bf16)
            tall = jnp.concatenate([jnp.zeros((64, 128), f32), value], axis=0)
            erow[q * 128:(q + 1) * 128] = jnp.transpose(tall).astype(bf16)

    def delta_three(r):
        d3[rows_of(r)] = (dot(erow[rows_of(r)], tm, 1, 1) * a3[rows_of(r)]).astype(bf16)

    s2_d, s2_s = ([{} for _ in range(NROW)] for _ in range(2))

    def s2_part(r):
        dv = d3[rows_of(r)]
        for own in (False, True):
            for k in (2, 1, 3, 0):
                zz = ring(z, k)
                c = zz * 2 + (core if own else 1 - core)
                s2b[c, rows_of(r)] = dot(dv, w3b[:, :, c].reshape(256, 256), 1, 1).astype(bf16)
                if not own:
                    s2_d[r][k] = send(s2b.at[c, rows_of(r)], s2p.at[zz, rows_of(r)], partner)

    def s2_join(r):
        rr = rows_of(r)
        for k in (2, 1, 3):
            s2_d[r][k].wait_recv()
            zz = ring(z, k)
            c = zz * 2 + core
            s2b[c, rr] = (s2b[c, rr].astype(f32) + s2p[zz, rr].astype(f32)).astype(bf16)
            s2_s[r][k] = send(s2b.at[c, rr], s2z.at[k - 1, rr], zdev[k])

    def s2_end(r):
        rr = rows_of(r)
        s2_d[r][0].wait_recv()
        for k in (1, 3, 2):
            s2_s[r][k].wait_recv()
        total = s2b[m, rr].astype(f32) + s2p[z, rr].astype(f32)
        for k in range(3):
            total = total + s2z[k, rr].astype(f32)
        a2[rr] = total * a2[rr]
        d2[rr] = a2[rr].astype(bf16)
        d2t[:, rr] = jnp.transpose(a2[rr]).astype(bf16)

    error(0)
    delta_three(0)
    s2_part(0)
    s2_join(0)
    fin(t_p[1])
    error(1)
    delta_three(1)
    s2_part(1)
    s2_join(1)

    def grad_three(k, carry):
        g3b[:, :, k] = dot(h2f[k], d3[...], 0, 0).astype(bf16).reshape(4, 4, 16, 256)
        return carry

    def finish_three(lo, total):
        g3_ref[lo * 16:(lo + 4) * 16] = total.reshape(64, 256)

    t_g3 = [scatter(g3b, p, g3a, g3x, finish_three) for p in range(2)]
    lax.fori_loop(0, 4, grad_three, 0)
    adv(t_g3[0])
    lax.fori_loop(4, 8, grad_three, 0)
    adv(t_g3[1])
    g4 = dot(et[...], h3[...], 1, 0)

    def finish_two(lo, total):
        g2b[x, y, lo:lo + 4] = total.astype(bf16)

    t_g2 = [scatter(g2b, p, g2a, g2x, finish_two) for p in range(2)]

    upper, lower = slice(0, 256), slice(256, 512)

    def grad_two_a(k, carry):
        g2f[k] = dot(d2t[:, upper], h1[k, upper], 1, 0)
        return carry

    def grad_two_b(k, carry):
        total = g2f[k] + dot(d2t[:, lower], h1[k, lower], 1, 0)
        g2b[:, :, k] = total.astype(bf16).reshape(4, 4, 16, 256)
        return carry

    def grad_one(k, half):
        back = dot(d2[half], cw[:, :, k].reshape(256, 256), 1, 0)
        d1[...] = (back * a1[k, half]).astype(bf16)
        return dot(xtb[:, half], d1[...], 1, 0)

    def delta_one_a(k, carry):
        g1f[k] = grad_one(k, upper)
        return carry

    def delta_one_b(side):
        def body(i, carry):
            k = 2 * i + side
            low = g1f[k] + grad_one(k, lower)
            own = jnp.where(jnp.full((64, 256), k, jnp.int32) == m, g4, 0.0)
            tall = jnp.transpose(jnp.concatenate([low, own], axis=0))
            gtb[i, side] = tall.astype(bf16).reshape(4, 4, 16, 128)
            return carry

        lax.fori_loop(0, 4, body, 0)

    s2_end(0)
    lax.fori_loop(0, 8, grad_two_a, 0)
    lax.fori_loop(0, 8, delta_one_a, 0)
    s2_end(1)
    lax.fori_loop(0, 4, grad_two_b, 0)
    adv(t_g2[0])
    lax.fori_loop(4, 8, grad_two_b, 0)
    adv(t_g2[1])
    for _ in range(3):
        adv(*t_g3)
    delta_one_b(1 - core)
    gt_d = send(gtb.at[:, 1 - core], gtp, partner)
    delta_one_b(core)
    gt_d.wait_recv()
    gt_z = {}
    for k in (2, 1, 3):
        zz = ring(z, k)
        gtb[zz, core] = (gtb[zz, core].astype(f32) + gtp[zz].astype(f32)).astype(bf16)
        gt_z[k] = send(gtb.at[zz, core], gtz.at[k - 1], zdev[k])
    for _ in range(3):
        adv(*t_g2)
    total = gtb[z, core].astype(f32) + gtp[z].astype(f32)
    for k in (1, 3, 2):
        gt_z[k].wait_recv()
        total = total + gtz[k - 1].astype(f32)
    gto[...] = total.astype(bf16)
    gt_x = [
        send(gto.at[ring(x, i), ring(y, j)], gtx.at[n], dp_dev(ring(x, i), ring(y, j)))
        for n, (i, j) in enumerate(plane)
    ]
    fin(*t_g2)
    g2_copies = [send(g2b.at[x, y, mdev[k]], z2.at[m], mp_dev(mdev[k])) for k in range(1, 8)]
    fin(*t_g3)
    z2[m] = g2b[x, y, m]
    small = gto[x, y].astype(f32)
    for n, c in enumerate(gt_x):
        c.wait_recv()
        small = small + gtx[n].astype(f32)
    gs_ref[...] = small
    for c in g2_copies:
        c.wait_recv()
    g2_ref[...] = jnp.transpose(z2[...].astype(f32).reshape(128, 256))
    for c in sent:
        c.wait_send()


def run_kernel(*args):
    vm = pltpu.VMEM
    grad = [
        vm((4, 4, 8, 16, 256), bf16), vm((2, 3, 4, 4, 16, 256), bf16), vm((2, 3, 4, 16, 256), bf16),
    ]
    scratch = [
        vm((8, 128, 128), f32), vm((8, 64, 128), f32), vm((3, 64, 128), bf16),
        vm((3, 64, 128), bf16), vm((3, 64, 128), bf16), vm((3, 64, 128), bf16),
        vm((2, 16, 128), f32), vm((8, 16, 256), bf16),
        vm((4, 4, 8, 16, 256), bf16), vm((8, 4, 4, 16, 128), bf16), vm((4, 4, 8, 16, 256), bf16),
        vm((512, 128), bf16), vm((64, 512), bf16),
        vm((8, 512, 256), bf16), vm((8, 512, 256), f32), vm((256, 256), bf16),
        vm((512, 256), f32), vm((512, 256), f32),
        vm((8, 512, 256), bf16), vm((512, 256), bf16), vm((512, 256), bf16),
        vm((512, 256), bf16), vm((256, 512), bf16),
        *[vm((NROW, 64, ROWS), bf16)] * 3, vm((NROW, 3, 64, ROWS), bf16), vm((64, 512), bf16), vm((512, 128), bf16),
        vm((8, 512, 256), bf16), vm((4, 512, 256), bf16), vm((3, 512, 256), bf16),
        *grad, *grad, vm((8, 256, 256), f32), vm((8, 64, 256), f32),
        vm((4, 2, 4, 4, 16, 128), bf16), vm((4, 4, 4, 16, 128), bf16), vm((3, 4, 4, 16, 128), bf16),
        vm((4, 4, 16, 128), bf16), vm((15, 16, 128), bf16), vm((8, 16, 256), bf16),
        pltpu.SemaphoreType.DMA((NSEM,)), pltpu.SemaphoreType.DMA((NSEM,)),
    ]
    spec = pl.BlockSpec(memory_space=pltpu.VMEM)
    return pl.pallas_call(
        kernel,
        out_shape=(
            jax.ShapeDtypeStruct((256, 128), f32),
            jax.ShapeDtypeStruct((128, 256), f32),
            jax.ShapeDtypeStruct((16, 128), f32),
        ),
        in_specs=[spec] * 2 + [pl.BlockSpec(memory_space=pltpu.SMEM)] + [spec] * 4,
        out_specs=[spec] * 3,
        scratch_shapes=scratch,
        compiler_params=pltpu.CompilerParams(
            collective_id=0, has_side_effects=True, vmem_limit_bytes=60 * 1024 * 1024
        ),
        name="train_step",
    )(*args)


def update_kernel(
    g2, g3, gs, w_in, w_mid, w_top, w_out, m_in, m_mid, m_top, m_out,
    nw_in, nw_mid, nw_top, nw_out, nm_in, nm_mid, nm_top, nm_out,
):
    small = gs[...]
    grads = (small[:, 0:55], g2[...], g3[...], pltpu.roll(small, 64, 1)[:, 0:53])
    for grad, w, mo, nw, nm in zip(
        grads, (w_in, w_mid, w_top, w_out), (m_in, m_mid, m_top, m_out),
        (nw_in, nw_mid, nw_top, nw_out), (nm_in, nm_mid, nm_top, nm_out),
    ):
        value = momentum_decay * mo[...] + grad
        nm[...] = value
        nw[...] = w[...] - learn_rate * value


def on_device(
    samples, targets, counts,
    weight_in, weight_mid, weight_top, weight_out,
    moment_in, moment_mid, moment_top, moment_out,
):
    g_mid, g_top, g_small = run_kernel(
        jnp.transpose(samples, (1, 0, 2)), jnp.transpose(targets, (1, 0, 2)), counts,
        weight_in.T, weight_mid, weight_top, weight_out,
    )
    spec = pl.BlockSpec(memory_space=pltpu.VMEM)
    shapes = [(16, 55), (256, 128), (128, 256), (16, 53)] * 2
    out = pl.pallas_call(
        update_kernel,
        out_shape=[jax.ShapeDtypeStruct(s, f32) for s in shapes],
        in_specs=[spec] * 11,
        out_specs=[spec] * 8,
        name="update",
    )(
        g_mid, g_top, g_small, weight_in.T, weight_mid, weight_top, weight_out,
        moment_in.T, moment_mid, moment_top, moment_out,
    )
    return (out[0].T, *out[1:4], out[4].T, *out[5:])


def solution(mesh):
    weights = (P(None, ("mp", "dp")), P("mp", "dp"), P("dp", "mp"), P(("mp", "dp"), None))
    in_specs = (P("dp", None, None), P("dp", None, None), P("dp")) + weights + weights
    return jax.shard_map(
        on_device, mesh=mesh, in_specs=in_specs, out_specs=weights + weights, check_vma=False
    )
```

```python
import math

import jax
import jax.numpy as jnp
from jax import lax
from jax.experimental import pallas as pl
from jax.experimental.pallas import tpu as pltpu
from jax.sharding import PartitionSpec as P

momentum_decay = 0.9
learn_rate = 0.05
MESH = pl.DeviceIdType.MESH
f32, bf16 = jnp.float32, jnp.bfloat16
NSEM = 272
NROW = 2
ROWS = 512 // NROW


def gelu_act(value):
    return 0.5 * value * (1.0 + lax.erf(value * (1.0 / math.sqrt(2.0))))


def gelu_slope(value):
    return 0.5 * (1.0 + lax.erf(value * (1.0 / math.sqrt(2.0)))) + value * jnp.exp(
        -0.5 * value * value
    ) * (1.0 / math.sqrt(2.0 * math.pi))


def dot(left, right, a, b):
    return lax.dot_general(left, right, (((a,), (b,)), ((), ())), preferred_element_type=f32)


def adv(*tasks):
    for task in tasks:
        next(task, None)


def fin(*tasks):
    tasks = list(tasks)
    while tasks:
        tasks = [t for t in tasks if next(t, "end") != "end"]


def kernel(
    x_ref, y_ref, n_ref, win_ref, wmid_ref, wtop_ref, wout_ref,
    g2_ref, g3_ref, gs_ref,
    xf, yf, xs, ys, xr, yr, wide, w2s, cw, ct, w3b, xrow, xtb,
    h1, a1, d1, a2, a3, h2f, h3, d3, d2, d2t,
    psend, pp, psum, pr, et, erow,
    s2b, s2p, s2z,
    g3b, g3a, g3x, g2b, g2a, g2f, g1f, gtb, gtp, gtz, gto, gtx, z2,
    ssem, rsem, wsem, zsem,
):
    d, m = lax.axis_index("dp"), lax.axis_index("mp")
    x, y = lax.div(d, 4), lax.rem(d, 4)
    z, core = lax.div(m, 2), lax.rem(m, 2)

    def ring(v, k):
        return lax.rem(v + k, 4)

    def dp_dev(xx, yy):
        return (xx * 4 + yy, m)

    def mp_dev(mm):
        return (d, mm)

    partner = mp_dev(z * 2 + 1 - core)
    zdev = {k: mp_dev(ring(z, k) * 2 + core) for k in (1, 2, 3)}
    mdev = {k: lax.rem(m + k, 8) for k in range(1, 8)}
    plane = [(i, j) for i in range(4) for j in range(4) if i or j]
    plane.sort(key=lambda t: -((t[0] % 2) + (t[0] == 2) * 2 + (t[1] % 2) + (t[1] == 2) * 2))
    pair = dp_dev(ring(x, 2), y)

    count = [0]
    sent = []

    def send(src, dst, dev, sem=None, skip=None):
        k = count[0]
        count[0] += 1
        assert k < NSEM
        copy = pltpu.make_async_remote_copy(
            src_ref=src, dst_ref=dst, send_sem=ssem.at[k],
            recv_sem=rsem.at[k] if sem is None else sem,
            device_id=dev, device_id_type=MESH,
        )
        if skip is None:
            copy.start()
        else:
            pl.when(m != skip)(copy.start)
        sent.append((copy, skip))
        return copy

    def arrived(dst, sem, skip=None):
        copy = pltpu.make_async_remote_copy(
            src_ref=dst, dst_ref=dst, send_sem=ssem.at[0], recv_sem=sem,
            device_id=partner, device_id_type=MESH,
        )
        if skip is None:
            copy.wait_recv()
        else:
            pl.when(m != skip)(copy.wait_recv)

    barrier = pltpu.get_barrier_semaphore()
    peers = [dp_dev(ring(x, i), ring(y, j)) for i, j in plane]
    for i, j in [(0, 0)] + [t for t in plane if 0 in t]:
        peers += [(ring(x, i) * 4 + ring(y, j), mdev[k]) for k in range(1, 8)]
    for dev in peers:
        pl.semaphore_signal(barrier, inc=1, device_id=dev, device_id_type=MESH)

    lanes = lax.broadcasted_iota(jnp.int32, (16, 128), 1)
    wide[...] = jnp.zeros_like(wide)
    wide[0, :, 0:55] = win_ref[...]
    wide[1, :, 0:53] = wout_ref[...]
    tile = wide[0] + pltpu.roll(wide[1], 64, 1)
    tile = jnp.where(lanes == 127, jnp.full((16, 128), n_ref[0], jnp.int32).astype(f32), tile)
    ct[m, x, y] = tile.astype(bf16)
    w2s[...] = jnp.transpose(wmid_ref[...]).astype(bf16).reshape(8, 16, 256)
    w3b[x, y] = wtop_ref[...].astype(bf16).reshape(8, 16, 256)
    cw[x, y, m] = w2s[m]
    xf[...] = jnp.zeros_like(xf)
    yf[...] = jnp.zeros_like(yf)
    xf[:, 0:55] = jnp.transpose(x_ref[...].astype(f32), (1, 0, 2))
    yf[:, 0:53] = jnp.transpose(y_ref[...].astype(f32), (1, 0, 2))
    for q in range(3):
        xs[q] = xf[4 + q, 0:64].astype(bf16)
        ys[q] = yf[4 + q].astype(bf16)
    pl.semaphore_wait(barrier, len(peers))

    def gather(buf, part):
        ms = slice(4 * part, 4 * part + 4)
        pos = (x, y) if part == 0 else (y, x)

        def at(a, b):
            return buf.at[a, b, ms] if part == 0 else buf.at[b, a, ms]

        def dev(a, b):
            return dp_dev(a, b) if part == 0 else dp_dev(b, a)

        own = at(pos[0], pos[1])
        first = {k: send(own, own, dev(ring(pos[0], k), pos[1])) for k in (2, 1, 3)}
        yield
        waits = [send(own, own, dev(pos[0], ring(pos[1], k))) for k in (2, 1, 3)]
        yield
        for k in (1, 3, 2):
            first[k].wait_recv()
            got = at(ring(pos[0], 4 - k), pos[1])
            waits += [send(got, got, dev(pos[0], ring(pos[1], j))) for j in (2, 1, 3)]
            yield
        for c in waits:
            c.wait_recv()

    def gather_two(part):
        ms = slice(4 * part, 4 * part + 4)
        pos = (x, y) if part == 0 else (y, x)
        waits = []
        for j in (0, 1, 3, 2):
            a = ring(pos[0], 4 - j)
            src = (a, pos[1]) if part == 0 else (pos[1], a)
            for o in range(4 * part, 4 * part + 4):
                arrived(cw.at[src[0], src[1], o], wsem.at[4 * o + j], o if j == 0 else None)
            got = cw.at[src[0], src[1], ms]
            for k in (2, 1, 3):
                b = ring(pos[1], k)
                dev = dp_dev(pos[0], b) if part == 0 else dp_dev(b, pos[0])
                waits.append(send(got, got, dev))
            yield
        for c in waits:
            c.wait_recv()

    def scatter(buf, part, abuf, xbuf, finish, direct=False):
        lo = 4 * part
        ms = slice(lo, lo + 4)
        up, ap = (x, y) if part == 0 else (y, x)

        def at(u, a):
            return (u, a, ms) if part == 0 else (a, u, ms)

        def dev(u, a):
            return dp_dev(u, a) if part == 0 else dp_dev(a, u)

        first = {}
        for j in (2, 1, 3, 0):
            u = ring(up, j)
            for k in (2, 1, 3):
                first[j, k] = send(
                    buf.at[at(u, ring(ap, k))], abuf.at[part, k - 1, u], dev(up, ring(ap, k))
                )
        yield
        second = {}
        for j in (2, 1, 3, 0):
            u = ring(up, j)
            for k in (2, 1, 3):
                first[j, k].wait_recv()
            total = buf[at(u, ap)].astype(f32)
            for k in (1, 2, 3):
                total = total + abuf[part, k - 1, u].astype(f32)
            if j:
                buf[at(u, ap)] = total.astype(bf16)
                if direct:
                    for o in range(lo, lo + 4):
                        send(
                            buf.at[(u, ap, o) if part == 0 else (ap, u, o)], z2.at[m, j],
                            (dev(u, ap)[0], o), zsem.at[4 * m + j],
                        )
                    yield
                    continue
                second[j] = send(buf.at[at(u, ap)], xbuf.at[part, j - 1], dev(u, ap))
                yield
        for j in () if direct else (1, 3, 2):
            second[j].wait_recv()
            total = total + xbuf[part, j - 1].astype(f32)
        finish(lo, total)

    own_tile = ct.at[m, x, y]
    half = lax.div(m, 4)
    for j in (2, 1, 3, 0):
        there = ring(x, j * (1 - half)) * 4 + ring(y, j * half)
        for k in range(0 if j else 1, 8):
            c = lax.rem(m + k, 8)
            send(w2s.at[c], cw.at[x, y, m], (there, c), wsem.at[4 * m + j])
    tile_copies = [send(own_tile, own_tile, dp_dev(ring(x, i), ring(y, j))) for i, j in plane]
    x_copy = send(xs, xr, pair)
    t_cw = [gather_two(0), gather_two(1)]
    t_w3 = [gather(w3b, 0), gather(w3b, 1)]
    for c in tile_copies:
        c.wait_recv()
    own_block = ct.at[m]
    block_copies = {k: send(own_block, own_block, zdev[k]) for k in (2, 1, 3)}
    partner_blocks = {0: send(own_block, own_block, partner)}
    for _ in range(4):
        adv(*t_cw)
    adv(*t_w3, *t_w3)

    lane = ct[m].reshape(256, 128).astype(f32)[:, 127:128]
    scale = 2.0 / (jnp.sum(lane, axis=0, keepdims=True) * (1.0 / 16.0) * 128.0)
    mine = ct[m, x, y].astype(f32)[0:1, 127:128]
    theirs = ct[m, ring(x, 2), y].astype(f32)[0:1, 127:128]

    def pick(ref, recv, q):
        value = ref[q, 0:64]
        for k in range(3):
            if q - k < 1:
                continue
            take = jnp.broadcast_to(mine, value.shape) == float(q - k)
            value = jnp.where(take, recv[k].astype(f32), value)
        return value

    x_copy.wait_recv()
    for q in range(4):
        value = pick(xf, xr, q)
        xtb[:, q * 128:(q + 1) * 128] = value.astype(bf16)
        tall = jnp.concatenate([value, jnp.zeros((64, 128), f32)], axis=0)
        xrow[q * 128:(q + 1) * 128] = jnp.transpose(tall).astype(bf16)

    def rows_of(r):
        return slice(r * ROWS, (r + 1) * ROWS)

    def chunks(body, lo=0, n=ROWS, step=32):
        lax.fori_loop(0, n // step, lambda i, c: (body(pl.ds(pl.multiple_of(lo + i * step, step), step)), c)[1], 0)

    def layer_one(k):
        a1[k] = dot(xrow[...], ct[k].reshape(256, 128), 1, 1)

        def act(rr):
            h1[k, rr] = gelu_act(a1[k, rr]).astype(bf16)

        chunks(act, 0, 512)

    def slope_one(lo, hi):
        def body(k, carry):
            def act(rr):
                a1[k, rr] = gelu_slope(a1[k, rr])

            chunks(act, 0, 512)
            return carry

        lax.fori_loop(lo, hi, body, 0)

    layer_one(m)
    partner_blocks[0].wait_recv()
    layer_one(z * 2 + 1 - core)
    for k in (1, 3, 2):
        block_copies[k].wait_recv()
        blk = ring(z, 4 - k) * 2 + core
        partner_blocks[k] = send(ct.at[blk], ct.at[blk], partner)
        layer_one(blk)
    y_copy = send(ys, yr, pair)
    for k in (1, 3, 2):
        partner_blocks[k].wait_recv()
        layer_one(ring(z, 4 - k) * 2 + 1 - core)
    fin(*t_cw)

    def layer_two(r):
        total = jnp.zeros((ROWS, 256), f32)
        for k in range(8):
            total = total + dot(h1[k, rows_of(r)], cw[:, :, k].reshape(256, 256), 1, 1)
        a2[rows_of(r)] = total

        def act(rr):
            h2f[m, rr] = gelu_act(a2[rr]).astype(bf16)

        chunks(act, r * ROWS)

    h2_z, h2_p = ([{} for _ in range(NROW)] for _ in range(2))

    def h2_send(r):
        own = h2f.at[m, rows_of(r)]
        for k in (2, 1, 3):
            h2_z[r][k] = send(own, own, zdev[k])
        h2_p[r][0] = send(own, own, partner)

    layer_two(0)
    h2_send(0)
    for _ in range(3):
        adv(*t_w3)
    layer_two(1)
    h2_send(1)
    slope_one(0, 8)
    fin(*t_w3)

    tm = ct[m].reshape(256, 128)

    def layer_three(r):
        rows = rows_of(r)

        def part(k):
            return dot(h2f[k, rows], w3b[:, :, k].reshape(256, 256), 1, 0)

        a3[rows] = part(m)
        h2_p[r][0].wait_recv()
        a3[rows] += part(z * 2 + 1 - core)
        for k in (1, 3, 2):
            h2_z[r][k].wait_recv()
            blk = ring(z, 4 - k) * 2 + core
            view = h2f.at[blk, rows]
            h2_p[r][k] = send(view, view, partner)
            a3[rows] += part(blk)
        for k in (1, 3, 2):
            h2_p[r][k].wait_recv()
            a3[rows] += part(ring(z, 4 - k) * 2 + 1 - core)

        def act(rr):
            v = a3[rr]
            h3[rr] = gelu_act(v).astype(bf16)

        chunks(act, r * ROWS)
        psend[r] = jnp.transpose(dot(h3[rows], tm, 1, 0))[64:128].astype(bf16)

    def slope_three(r):
        def act(rr):
            a3[rr] = gelu_slope(a3[rr])

        chunks(act, r * ROWS)

    def slope_two(r):
        def act(rr):
            a2[rr] = gelu_slope(a2[rr])

        chunks(act, r * ROWS)

    def p_task(r):
        c = send(psend.at[r], pp.at[r], partner)
        yield
        c.wait_recv()
        psum[r] = (psend[r].astype(f32) + pp[r].astype(f32)).astype(bf16)
        cs = [send(psum.at[r], pr.at[r, k - 1], zdev[k]) for k in (2, 1, 3)]
        yield
        for c in cs:
            c.wait_recv()

    t_p = [p_task(r) for r in range(NROW)]
    slope_two(0)
    slope_two(1)
    layer_three(0)
    adv(t_p[0])
    slope_three(0)
    adv(t_p[0])
    layer_three(1)
    adv(t_p[1])
    slope_three(1)
    adv(t_p[1])
    y_copy.wait_recv()
    fin(t_p[0])

    sub = lax.broadcasted_iota(jnp.int32, (64, 128), 0)

    def error(r):
        for h in range(4 // NROW):
            q = (4 // NROW) * r + h
            ls = slice(h * 128, (h + 1) * 128)
            want = pick(yf, yr, q)
            own_n = jnp.broadcast_to(mine, (64, 128))
            pair_n = jnp.broadcast_to(theirs, (64, 128))
            live = (own_n > float(q)) | (4.0 + float(q) - own_n < pair_n)
            predicted = psum[r, :, ls].astype(f32)
            for k in range(3):
                predicted = predicted + pr[r, k, :, ls].astype(f32)
            value = jnp.broadcast_to(scale, (64, 128)) * (predicted - want)
            value = jnp.where(live & (sub < 53), value, 0.0)
            et[:, q * 128:(q + 1) * 128] = value.astype(bf16)
            tall = jnp.concatenate([jnp.zeros((64, 128), f32), value], axis=0)
            erow[q * 128:(q + 1) * 128] = jnp.transpose(tall).astype(bf16)

    def delta_three(r):
        d3[rows_of(r)] = (dot(erow[rows_of(r)], tm, 1, 1) * a3[rows_of(r)]).astype(bf16)

    s2_d, s2_s = ([{} for _ in range(NROW)] for _ in range(2))

    def s2_part(r):
        dv = d3[rows_of(r)]
        for own in (False, True):
            for k in (2, 1, 3, 0):
                zz = ring(z, k)
                c = zz * 2 + (core if own else 1 - core)
                s2b[c, rows_of(r)] = dot(dv, w3b[:, :, c].reshape(256, 256), 1, 1).astype(bf16)
                if not own:
                    s2_d[r][k] = send(s2b.at[c, rows_of(r)], s2p.at[zz, rows_of(r)], partner)

    def s2_join(r):
        rr = rows_of(r)
        for k in (2, 1, 3):
            s2_d[r][k].wait_recv()
            zz = ring(z, k)
            c = zz * 2 + core
            s2b[c, rr] = (s2b[c, rr].astype(f32) + s2p[zz, rr].astype(f32)).astype(bf16)
            s2_s[r][k] = send(s2b.at[c, rr], s2z.at[k - 1, rr], zdev[k])

    def s2_end(r):
        rr = rows_of(r)
        s2_d[r][0].wait_recv()
        for k in (1, 3, 2):
            s2_s[r][k].wait_recv()
        total = s2b[m, rr].astype(f32) + s2p[z, rr].astype(f32)
        for k in range(3):
            total = total + s2z[k, rr].astype(f32)
        a2[rr] = total * a2[rr]
        d2[rr] = a2[rr].astype(bf16)
        d2t[:, rr] = jnp.transpose(a2[rr]).astype(bf16)

    error(0)
    delta_three(0)
    s2_part(0)
    s2_join(0)
    fin(t_p[1])
    error(1)
    delta_three(1)
    s2_part(1)
    s2_join(1)

    def grad_three(k, carry):
        g3b[:, :, k] = dot(h2f[k], d3[...], 0, 0).astype(bf16).reshape(4, 4, 16, 256)
        return carry

    def finish_three(lo, total):
        g3_ref[lo * 16:(lo + 4) * 16] = total.reshape(64, 256)

    t_g3 = [scatter(g3b, p, g3a, g3x, finish_three) for p in range(2)]
    lax.fori_loop(0, 4, grad_three, 0)
    adv(t_g3[0])
    lax.fori_loop(4, 8, grad_three, 0)
    adv(t_g3[1])
    g4 = dot(et[...], h3[...], 1, 0)

    def finish_two(lo, total):
        g2b[x, y, lo:lo + 4] = total.astype(bf16)
        for o in range(lo, lo + 4):
            send(g2b.at[x, y, o], z2.at[m, 0], mp_dev(o), zsem.at[4 * m], o)

    t_g2 = [scatter(g2b, p, g2a, None, finish_two, True) for p in range(2)]

    upper, lower = slice(0, 256), slice(256, 512)

    def grad_two_a(k, carry):
        g2f[k] = dot(d2t[:, upper], h1[k, upper], 1, 0)
        return carry

    def grad_two_b(k, carry):
        total = g2f[k] + dot(d2t[:, lower], h1[k, lower], 1, 0)
        g2b[:, :, k] = total.astype(bf16).reshape(4, 4, 16, 256)
        return carry

    def grad_one(k, half):
        back = dot(d2[half], cw[:, :, k].reshape(256, 256), 1, 0)
        d1[...] = (back * a1[k, half]).astype(bf16)
        return dot(xtb[:, half], d1[...], 1, 0)

    def delta_one_a(k, carry):
        g1f[k] = grad_one(k, upper)
        return carry

    def delta_one_b(side):
        def body(i, carry):
            k = 2 * i + side
            low = g1f[k] + grad_one(k, lower)
            own = jnp.where(jnp.full((64, 256), k, jnp.int32) == m, g4, 0.0)
            tall = jnp.transpose(jnp.concatenate([low, own], axis=0))
            gtb[i, side] = tall.astype(bf16).reshape(4, 4, 16, 128)
            return carry

        lax.fori_loop(0, 4, body, 0)

    s2_end(0)
    lax.fori_loop(0, 8, grad_two_a, 0)
    lax.fori_loop(0, 8, delta_one_a, 0)
    s2_end(1)
    lax.fori_loop(0, 4, grad_two_b, 0)
    adv(t_g2[0])
    lax.fori_loop(4, 8, grad_two_b, 0)
    adv(t_g2[1])
    for _ in range(3):
        adv(*t_g3)
    delta_one_b(1 - core)
    gt_d = send(gtb.at[:, 1 - core], gtp, partner)
    delta_one_b(core)
    gt_d.wait_recv()
    gt_z = {}
    for k in (2, 1, 3):
        zz = ring(z, k)
        gtb[zz, core] = (gtb[zz, core].astype(f32) + gtp[zz].astype(f32)).astype(bf16)
        gt_z[k] = send(gtb.at[zz, core], gtz.at[k - 1], zdev[k])
    for _ in range(3):
        adv(*t_g2)
    total = gtb[z, core].astype(f32) + gtp[z].astype(f32)
    for k in (1, 3, 2):
        gt_z[k].wait_recv()
        total = total + gtz[k - 1].astype(f32)
    gto[...] = total.astype(bf16)
    gt_x = [
        send(gto.at[ring(x, i), ring(y, j)], gtx.at[n], dp_dev(ring(x, i), ring(y, j)))
        for n, (i, j) in enumerate(plane)
    ]
    fin(*t_g2)
    fin(*t_g3)
    z2[m, 0] = g2b[x, y, m]
    small = gto[x, y].astype(f32)
    for n, c in enumerate(gt_x):
        c.wait_recv()
        small = small + gtx[n].astype(f32)
    gs_ref[...] = small
    for o in range(8):
        for j in range(4):
            arrived(z2.at[o, j], zsem.at[4 * o + j], None if j else o)
    g2_ref[...] = jnp.transpose(jnp.sum(z2[...].astype(f32), axis=1).reshape(128, 256))
    for c, skip in sent:
        if skip is None:
            c.wait_send()
        else:
            pl.when(m != skip)(c.wait_send)


def run_kernel(*args):
    vm = pltpu.VMEM
    grad = [
        vm((4, 4, 8, 16, 256), bf16), vm((2, 3, 4, 4, 16, 256), bf16), vm((2, 3, 4, 16, 256), bf16),
    ]
    scratch = [
        vm((8, 128, 128), f32), vm((8, 64, 128), f32), vm((3, 64, 128), bf16),
        vm((3, 64, 128), bf16), vm((3, 64, 128), bf16), vm((3, 64, 128), bf16),
        vm((2, 16, 128), f32), vm((8, 16, 256), bf16),
        vm((4, 4, 8, 16, 256), bf16), vm((8, 4, 4, 16, 128), bf16), vm((4, 4, 8, 16, 256), bf16),
        vm((512, 128), bf16), vm((64, 512), bf16),
        vm((8, 512, 256), bf16), vm((8, 512, 256), f32), vm((256, 256), bf16),
        vm((512, 256), f32), vm((512, 256), f32),
        vm((8, 512, 256), bf16), vm((512, 256), bf16), vm((512, 256), bf16),
        vm((512, 256), bf16), vm((256, 512), bf16),
        *[vm((NROW, 64, ROWS), bf16)] * 3, vm((NROW, 3, 64, ROWS), bf16), vm((64, 512), bf16), vm((512, 128), bf16),
        vm((8, 512, 256), bf16), vm((4, 512, 256), bf16), vm((3, 512, 256), bf16),
        *grad, *grad[:2], vm((8, 256, 256), f32), vm((8, 64, 256), f32),
        vm((4, 2, 4, 4, 16, 128), bf16), vm((4, 4, 4, 16, 128), bf16), vm((3, 4, 4, 16, 128), bf16),
        vm((4, 4, 16, 128), bf16), vm((15, 16, 128), bf16), vm((8, 4, 16, 256), bf16),
        pltpu.SemaphoreType.DMA((NSEM,)), pltpu.SemaphoreType.DMA((NSEM,)),
        pltpu.SemaphoreType.DMA((32,)), pltpu.SemaphoreType.DMA((32,)),
    ]
    spec = pl.BlockSpec(memory_space=pltpu.VMEM)
    return pl.pallas_call(
        kernel,
        out_shape=(
            jax.ShapeDtypeStruct((256, 128), f32),
            jax.ShapeDtypeStruct((128, 256), f32),
            jax.ShapeDtypeStruct((16, 128), f32),
        ),
        in_specs=[spec] * 2 + [pl.BlockSpec(memory_space=pltpu.SMEM)] + [spec] * 4,
        out_specs=[spec] * 3,
        scratch_shapes=scratch,
        compiler_params=pltpu.CompilerParams(
            collective_id=0, has_side_effects=True, vmem_limit_bytes=60 * 1024 * 1024
        ),
        name="train_step",
    )(*args)


def update_kernel(
    g2, g3, gs, w_in, w_mid, w_top, w_out, m_in, m_mid, m_top, m_out,
    nw_in, nw_mid, nw_top, nw_out, nm_in, nm_mid, nm_top, nm_out,
):
    small = gs[...]
    grads = (small[:, 0:55], g2[...], g3[...], pltpu.roll(small, 64, 1)[:, 0:53])
    for grad, w, mo, nw, nm in zip(
        grads, (w_in, w_mid, w_top, w_out), (m_in, m_mid, m_top, m_out),
        (nw_in, nw_mid, nw_top, nw_out), (nm_in, nm_mid, nm_top, nm_out),
    ):
        value = momentum_decay * mo[...] + grad
        nm[...] = value
        nw[...] = w[...] - learn_rate * value


def on_device(
    samples, targets, counts,
    weight_in, weight_mid, weight_top, weight_out,
    moment_in, moment_mid, moment_top, moment_out,
):
    g_mid, g_top, g_small = run_kernel(
        jnp.transpose(samples, (1, 0, 2)), jnp.transpose(targets, (1, 0, 2)), counts,
        weight_in.T, weight_mid, weight_top, weight_out,
    )
    spec = pl.BlockSpec(memory_space=pltpu.VMEM)
    shapes = [(16, 55), (256, 128), (128, 256), (16, 53)] * 2
    out = pl.pallas_call(
        update_kernel,
        out_shape=[jax.ShapeDtypeStruct(s, f32) for s in shapes],
        in_specs=[spec] * 11,
        out_specs=[spec] * 8,
        name="update",
    )(
        g_mid, g_top, g_small, weight_in.T, weight_mid, weight_top, weight_out,
        moment_in.T, moment_mid, moment_top, moment_out,
    )
    return (out[0].T, *out[1:4], out[4].T, *out[5:])


def solution(mesh):
    weights = (P(None, ("mp", "dp")), P("mp", "dp"), P("dp", "mp"), P(("mp", "dp"), None))
    in_specs = (P("dp", None, None), P("dp", None, None), P("dp")) + weights + weights
    return jax.shard_map(
        on_device, mesh=mesh, in_specs=in_specs, out_specs=weights + weights, check_vma=False
    )
```

```python
import math

import jax
import jax.numpy as jnp
from jax import lax
from jax.experimental import pallas as pl
from jax.experimental.pallas import tpu as pltpu
from jax.sharding import PartitionSpec as P

momentum_decay = 0.9
learn_rate = 0.05
MESH = pl.DeviceIdType.MESH
f32, bf16 = jnp.float32, jnp.bfloat16
NSEM = 272
NROW = 2
ROWS = 512 // NROW


def gelu_act(value):
    return 0.5 * value * (1.0 + lax.erf(value * (1.0 / math.sqrt(2.0))))


def gelu_slope(value):
    return 0.5 * (1.0 + lax.erf(value * (1.0 / math.sqrt(2.0)))) + value * jnp.exp(
        -0.5 * value * value
    ) * (1.0 / math.sqrt(2.0 * math.pi))


def dot(left, right, a, b):
    return lax.dot_general(left, right, (((a,), (b,)), ((), ())), preferred_element_type=f32)


def adv(*tasks):
    for task in tasks:
        next(task, None)


def fin(*tasks):
    tasks = list(tasks)
    while tasks:
        tasks = [t for t in tasks if next(t, "end") != "end"]


def kernel(
    x_ref, y_ref, n_ref, win_ref, wmid_ref, wtop_ref, wout_ref,
    g2_ref, g3_ref, gs_ref,
    xf, yf, xs, ys, xr, yr, wide, w2s, cw, ct, w3b, xrow, xtb,
    h1, a1, d1, a2, a3, h2f, h3, d3, d2, d2t,
    psend, pp, psum, pr, et, erow,
    s2b, s2p, s2z,
    g3b, g3a, g3x, g2b, g2a, g2f, g1f, gtb, gtp, gtz, gto, gtx, z2,
    ssem, rsem, wsem, zsem,
):
    d, m = lax.axis_index("dp"), lax.axis_index("mp")
    x, y = lax.div(d, 4), lax.rem(d, 4)
    z, core = lax.div(m, 2), lax.rem(m, 2)

    def ring(v, k):
        return lax.rem(v + k, 4)

    def dp_dev(xx, yy):
        return (xx * 4 + yy, m)

    def mp_dev(mm):
        return (d, mm)

    partner = mp_dev(z * 2 + 1 - core)
    zdev = {k: mp_dev(ring(z, k) * 2 + core) for k in (1, 2, 3)}
    mdev = {k: lax.rem(m + k, 8) for k in range(1, 8)}
    plane = [(i, j) for i in range(4) for j in range(4) if i or j]
    plane.sort(key=lambda t: -((t[0] % 2) + (t[0] == 2) * 2 + (t[1] % 2) + (t[1] == 2) * 2))
    pair = dp_dev(ring(x, 2), y)

    count = [0]
    sent = []

    def send(src, dst, dev, sem=None, skip=None):
        k = count[0]
        count[0] += 1
        assert k < NSEM
        copy = pltpu.make_async_remote_copy(
            src_ref=src, dst_ref=dst, send_sem=ssem.at[k],
            recv_sem=rsem.at[k] if sem is None else sem,
            device_id=dev, device_id_type=MESH,
        )
        if skip is None:
            copy.start()
        else:
            pl.when(m != skip)(copy.start)
        sent.append((copy, skip))
        return copy

    def arrived(dst, sem, skip=None):
        copy = pltpu.make_async_remote_copy(
            src_ref=dst, dst_ref=dst, send_sem=ssem.at[0], recv_sem=sem,
            device_id=partner, device_id_type=MESH,
        )
        if skip is None:
            copy.wait_recv()
        else:
            pl.when(m != skip)(copy.wait_recv)

    barrier = pltpu.get_barrier_semaphore()
    peers = [dp_dev(ring(x, i), ring(y, j)) for i, j in plane]
    for i, j in [(0, 0)] + [t for t in plane if 0 in t]:
        peers += [(ring(x, i) * 4 + ring(y, j), mdev[k]) for k in range(1, 8)]
    for dev in peers:
        pl.semaphore_signal(barrier, inc=1, device_id=dev, device_id_type=MESH)

    lanes = lax.broadcasted_iota(jnp.int32, (16, 128), 1)
    wide[...] = jnp.zeros_like(wide)
    wide[0, :, 0:55] = win_ref[...]
    wide[1, :, 0:53] = wout_ref[...]
    tile = wide[0] + pltpu.roll(wide[1], 64, 1)
    tile = jnp.where(lanes == 127, jnp.full((16, 128), n_ref[0], jnp.int32).astype(f32), tile)
    ct[m, x, y] = tile.astype(bf16)
    w2s[...] = jnp.transpose(wmid_ref[...]).astype(bf16).reshape(8, 16, 256)
    w3b[x, y] = wtop_ref[...].astype(bf16).reshape(8, 16, 256)
    cw[x, y, m] = w2s[m]
    xf[...] = jnp.zeros_like(xf)
    yf[...] = jnp.zeros_like(yf)
    xf[:, 0:55] = jnp.transpose(x_ref[...].astype(f32), (1, 0, 2))
    yf[:, 0:53] = jnp.transpose(y_ref[...].astype(f32), (1, 0, 2))
    for q in range(3):
        xs[q] = xf[4 + q, 0:64].astype(bf16)
        ys[q] = yf[4 + q].astype(bf16)
    pl.semaphore_wait(barrier, len(peers))

    def gather(buf, part):
        ms = slice(4 * part, 4 * part + 4)
        pos = (x, y) if part == 0 else (y, x)

        def at(a, b):
            return buf.at[a, b, ms] if part == 0 else buf.at[b, a, ms]

        def dev(a, b):
            return dp_dev(a, b) if part == 0 else dp_dev(b, a)

        own = at(pos[0], pos[1])
        first = {k: send(own, own, dev(ring(pos[0], k), pos[1])) for k in (2, 1, 3)}
        yield
        waits = [send(own, own, dev(pos[0], ring(pos[1], k))) for k in (2, 1, 3)]
        yield
        for k in (1, 3, 2):
            first[k].wait_recv()
            got = at(ring(pos[0], 4 - k), pos[1])
            waits += [send(got, got, dev(pos[0], ring(pos[1], j))) for j in (2, 1, 3)]
            yield
        for c in waits:
            c.wait_recv()

    def gather_two(part):
        ms = slice(4 * part, 4 * part + 4)
        pos = (x, y) if part == 0 else (y, x)
        waits = []
        for j in (0, 1, 3, 2):
            a = ring(pos[0], 4 - j)
            src = (a, pos[1]) if part == 0 else (pos[1], a)
            for o in range(4 * part, 4 * part + 4):
                arrived(cw.at[src[0], src[1], o], wsem.at[4 * o + j], o if j == 0 else None)
            got = cw.at[src[0], src[1], ms]
            for k in (2, 1, 3):
                b = ring(pos[1], k)
                dev = dp_dev(pos[0], b) if part == 0 else dp_dev(b, pos[0])
                waits.append(send(got, got, dev))
            yield
        for c in waits:
            c.wait_recv()

    def scatter(buf, part, abuf, xbuf, finish, direct=False):
        lo = 4 * part
        ms = slice(lo, lo + 4)
        up, ap = (x, y) if part == 0 else (y, x)

        def at(u, a):
            return (u, a, ms) if part == 0 else (a, u, ms)

        def dev(u, a):
            return dp_dev(u, a) if part == 0 else dp_dev(a, u)

        first = {}
        for j in (2, 1, 3, 0):
            u = ring(up, j)
            for k in (2, 1, 3):
                first[j, k] = send(
                    buf.at[at(u, ring(ap, k))], abuf.at[part, k - 1, u], dev(up, ring(ap, k))
                )
        yield
        second = {}
        for j in (2, 1, 3, 0):
            u = ring(up, j)
            for k in (2, 1, 3):
                first[j, k].wait_recv()
            total = buf[at(u, ap)].astype(f32)
            for k in (1, 2, 3):
                total = total + abuf[part, k - 1, u].astype(f32)
            if j:
                buf[at(u, ap)] = total.astype(bf16)
                if direct:
                    for o in range(lo, lo + 4):
                        send(
                            buf.at[(u, ap, o) if part == 0 else (ap, u, o)], z2.at[m, j],
                            (dev(u, ap)[0], o), zsem.at[4 * m + j],
                        )
                    yield
                    continue
                second[j] = send(buf.at[at(u, ap)], xbuf.at[part, j - 1], dev(u, ap))
                yield
        for j in () if direct else (1, 3, 2):
            second[j].wait_recv()
            total = total + xbuf[part, j - 1].astype(f32)
        finish(lo, total)

    own_tile = ct.at[m, x, y]
    tile_copies = [send(own_tile, own_tile, dp_dev(ring(x, i), ring(y, j))) for i, j in plane]
    half = lax.div(m, 4)
    for j in (2, 1, 3, 0):
        there = ring(x, j * (1 - half)) * 4 + ring(y, j * half)
        for k in range(0 if j else 1, 8):
            c = lax.rem(m + k, 8)
            send(w2s.at[c], cw.at[x, y, m], (there, c), wsem.at[4 * m + j])
    x_copy = send(xs, xr, pair)
    t_cw = [gather_two(0), gather_two(1)]
    t_w3 = [gather(w3b, 0), gather(w3b, 1)]
    for c in tile_copies:
        c.wait_recv()
    own_block = ct.at[m]
    block_copies = {k: send(own_block, own_block, zdev[k]) for k in (2, 1, 3)}
    partner_blocks = {0: send(own_block, own_block, partner)}
    for _ in range(4):
        adv(*t_cw)

    lane = ct[m].reshape(256, 128).astype(f32)[:, 127:128]
    scale = 2.0 / (jnp.sum(lane, axis=0, keepdims=True) * (1.0 / 16.0) * 128.0)
    mine = ct[m, x, y].astype(f32)[0:1, 127:128]
    theirs = ct[m, ring(x, 2), y].astype(f32)[0:1, 127:128]

    def pick(ref, recv, q):
        value = ref[q, 0:64]
        for k in range(3):
            if q - k < 1:
                continue
            take = jnp.broadcast_to(mine, value.shape) == float(q - k)
            value = jnp.where(take, recv[k].astype(f32), value)
        return value

    x_copy.wait_recv()
    for q in range(4):
        value = pick(xf, xr, q)
        xtb[:, q * 128:(q + 1) * 128] = value.astype(bf16)
        tall = jnp.concatenate([value, jnp.zeros((64, 128), f32)], axis=0)
        xrow[q * 128:(q + 1) * 128] = jnp.transpose(tall).astype(bf16)

    def rows_of(r):
        return slice(r * ROWS, (r + 1) * ROWS)

    def chunks(body, lo=0, n=ROWS, step=32):
        lax.fori_loop(0, n // step, lambda i, c: (body(pl.ds(pl.multiple_of(lo + i * step, step), step)), c)[1], 0)

    def layer_one(k):
        a1[k] = dot(xrow[...], ct[k].reshape(256, 128), 1, 1)

        def act(rr):
            h1[k, rr] = gelu_act(a1[k, rr]).astype(bf16)

        chunks(act, 0, 512)

    def slope_one(lo, hi):
        def body(k, carry):
            def act(rr):
                a1[k, rr] = gelu_slope(a1[k, rr])

            chunks(act, 0, 512)
            return carry

        lax.fori_loop(lo, hi, body, 0)

    layer_one(m)
    partner_blocks[0].wait_recv()
    layer_one(z * 2 + 1 - core)
    for k in (1, 3, 2):
        block_copies[k].wait_recv()
        blk = ring(z, 4 - k) * 2 + core
        partner_blocks[k] = send(ct.at[blk], ct.at[blk], partner)
        layer_one(blk)
    adv(*t_w3, *t_w3)
    y_copy = send(ys, yr, pair)
    for k in (1, 3, 2):
        partner_blocks[k].wait_recv()
        layer_one(ring(z, 4 - k) * 2 + 1 - core)
    fin(*t_cw)

    def layer_two(r):
        total = jnp.zeros((ROWS, 256), f32)
        for k in range(8):
            total = total + dot(h1[k, rows_of(r)], cw[:, :, k].reshape(256, 256), 1, 1)
        a2[rows_of(r)] = total

        def act(rr):
            h2f[m, rr] = gelu_act(a2[rr]).astype(bf16)

        chunks(act, r * ROWS)

    h2_z, h2_p = ([{} for _ in range(NROW)] for _ in range(2))

    def h2_send(r):
        own = h2f.at[m, rows_of(r)]
        for k in (2, 1, 3):
            h2_z[r][k] = send(own, own, zdev[k])
        h2_p[r][0] = send(own, own, partner)

    layer_two(0)
    h2_send(0)
    for _ in range(3):
        adv(*t_w3)
    layer_two(1)
    h2_send(1)
    slope_one(0, 8)
    fin(*t_w3)

    tm = ct[m].reshape(256, 128)

    def layer_three(r):
        rows = rows_of(r)

        def part(k):
            return dot(h2f[k, rows], w3b[:, :, k].reshape(256, 256), 1, 0)

        a3[rows] = part(m)
        h2_p[r][0].wait_recv()
        a3[rows] += part(z * 2 + 1 - core)
        for k in (1, 3, 2):
            h2_z[r][k].wait_recv()
            blk = ring(z, 4 - k) * 2 + core
            view = h2f.at[blk, rows]
            h2_p[r][k] = send(view, view, partner)
            a3[rows] += part(blk)
        for k in (1, 3, 2):
            h2_p[r][k].wait_recv()
            a3[rows] += part(ring(z, 4 - k) * 2 + 1 - core)

        def act(rr):
            v = a3[rr]
            h3[rr] = gelu_act(v).astype(bf16)

        chunks(act, r * ROWS)
        psend[r] = jnp.transpose(dot(h3[rows], tm, 1, 0))[64:128].astype(bf16)

    def slope_three(r):
        def act(rr):
            a3[rr] = gelu_slope(a3[rr])

        chunks(act, r * ROWS)

    def slope_two(r):
        def act(rr):
            a2[rr] = gelu_slope(a2[rr])

        chunks(act, r * ROWS)

    def p_task(r):
        c = send(psend.at[r], pp.at[r], partner)
        yield
        c.wait_recv()
        psum[r] = (psend[r].astype(f32) + pp[r].astype(f32)).astype(bf16)
        cs = [send(psum.at[r], pr.at[r, k - 1], zdev[k]) for k in (2, 1, 3)]
        yield
        for c in cs:
            c.wait_recv()

    t_p = [p_task(r) for r in range(NROW)]
    slope_two(0)
    slope_two(1)
    layer_three(0)
    adv(t_p[0])
    slope_three(0)
    adv(t_p[0])
    layer_three(1)
    adv(t_p[1])
    slope_three(1)
    adv(t_p[1])
    y_copy.wait_recv()
    fin(t_p[0])

    sub = lax.broadcasted_iota(jnp.int32, (64, 128), 0)

    def error(r):
        for h in range(4 // NROW):
            q = (4 // NROW) * r + h
            ls = slice(h * 128, (h + 1) * 128)
            want = pick(yf, yr, q)
            own_n = jnp.broadcast_to(mine, (64, 128))
            pair_n = jnp.broadcast_to(theirs, (64, 128))
            live = (own_n > float(q)) | (4.0 + float(q) - own_n < pair_n)
            predicted = psum[r, :, ls].astype(f32)
            for k in range(3):
                predicted = predicted + pr[r, k, :, ls].astype(f32)
            value = jnp.broadcast_to(scale, (64, 128)) * (predicted - want)
            value = jnp.where(live & (sub < 53), value, 0.0)
            et[:, q * 128:(q + 1) * 128] = value.astype(bf16)
            tall = jnp.concatenate([jnp.zeros((64, 128), f32), value], axis=0)
            erow[q * 128:(q + 1) * 128] = jnp.transpose(tall).astype(bf16)

    def delta_three(r):
        d3[rows_of(r)] = (dot(erow[rows_of(r)], tm, 1, 1) * a3[rows_of(r)]).astype(bf16)

    s2_d, s2_s = ([{} for _ in range(NROW)] for _ in range(2))

    def s2_part(r):
        dv = d3[rows_of(r)]
        for own in (False, True):
            for k in (2, 1, 3, 0):
                zz = ring(z, k)
                c = zz * 2 + (core if own else 1 - core)
                s2b[c, rows_of(r)] = dot(dv, w3b[:, :, c].reshape(256, 256), 1, 1).astype(bf16)
                if not own:
                    s2_d[r][k] = send(s2b.at[c, rows_of(r)], s2p.at[zz, rows_of(r)], partner)

    def s2_join(r):
        rr = rows_of(r)
        for k in (2, 1, 3):
            s2_d[r][k].wait_recv()
            zz = ring(z, k)
            c = zz * 2 + core
            s2b[c, rr] = (s2b[c, rr].astype(f32) + s2p[zz, rr].astype(f32)).astype(bf16)
            s2_s[r][k] = send(s2b.at[c, rr], s2z.at[k - 1, rr], zdev[k])

    def s2_end(r):
        rr = rows_of(r)
        s2_d[r][0].wait_recv()
        for k in (1, 3, 2):
            s2_s[r][k].wait_recv()
        total = s2b[m, rr].astype(f32) + s2p[z, rr].astype(f32)
        for k in range(3):
            total = total + s2z[k, rr].astype(f32)
        a2[rr] = total * a2[rr]
        d2[rr] = a2[rr].astype(bf16)
        d2t[:, rr] = jnp.transpose(a2[rr]).astype(bf16)

    error(0)
    delta_three(0)
    s2_part(0)
    s2_join(0)
    fin(t_p[1])
    error(1)
    delta_three(1)
    s2_part(1)
    s2_join(1)

    def grad_three(k, carry):
        g3b[:, :, k] = dot(h2f[k], d3[...], 0, 0).astype(bf16).reshape(4, 4, 16, 256)
        return carry

    def finish_three(lo, total):
        g3_ref[lo * 16:(lo + 4) * 16] = total.reshape(64, 256)

    t_g3 = [scatter(g3b, p, g3a, g3x, finish_three) for p in range(2)]
    lax.fori_loop(0, 4, grad_three, 0)
    adv(t_g3[0])
    lax.fori_loop(4, 8, grad_three, 0)
    adv(t_g3[1])
    g4 = dot(et[...], h3[...], 1, 0)

    def finish_two(lo, total):
        g2b[x, y, lo:lo + 4] = total.astype(bf16)
        for o in range(lo, lo + 4):
            send(g2b.at[x, y, o], z2.at[m, 0], mp_dev(o), zsem.at[4 * m], o)

    t_g2 = [scatter(g2b, p, g2a, None, finish_two, True) for p in range(2)]

    upper, lower = slice(0, 256), slice(256, 512)

    def grad_two_a(k, carry):
        g2f[k] = dot(d2t[:, upper], h1[k, upper], 1, 0)
        return carry

    def grad_two_b(k, carry):
        total = g2f[k] + dot(d2t[:, lower], h1[k, lower], 1, 0)
        g2b[:, :, k] = total.astype(bf16).reshape(4, 4, 16, 256)
        return carry

    def grad_one(k, half):
        back = dot(d2[half], cw[:, :, k].reshape(256, 256), 1, 0)
        d1[...] = (back * a1[k, half]).astype(bf16)
        return dot(xtb[:, half], d1[...], 1, 0)

    def delta_one_a(k, carry):
        g1f[k] = grad_one(k, upper)
        return carry

    def delta_one_b(zz, side):
        k = 2 * zz + side
        low = g1f[k] + grad_one(k, lower)
        own = jnp.where(jnp.full((64, 256), k, jnp.int32) == m, g4, 0.0)
        tall = jnp.transpose(jnp.concatenate([low, own], axis=0))
        gtb[zz, side] = tall.astype(bf16).reshape(4, 4, 16, 128)

    s2_end(0)
    lax.fori_loop(0, 8, grad_two_a, 0)
    lax.fori_loop(0, 8, delta_one_a, 0)
    s2_end(1)
    lax.fori_loop(0, 4, grad_two_b, 0)
    adv(t_g2[0])
    lax.fori_loop(4, 8, grad_two_b, 0)
    adv(t_g2[1])
    for _ in range(3):
        adv(*t_g3)
    gt_d, gt_z = {}, {}

    def gt_join(k):
        zz = ring(z, k)
        gt_d[k].wait_recv()
        gtb[zz, core] = (gtb[zz, core].astype(f32) + gtp[zz].astype(f32)).astype(bf16)
        gt_z[k] = send(gtb.at[zz, core], gtz.at[k - 1], zdev[k])

    last = None
    for k in (2, 1, 3, 0):
        zz = ring(z, k)
        delta_one_b(zz, 1 - core)
        gt_d[k] = send(gtb.at[zz, 1 - core], gtp.at[zz], partner)
        if last:
            gt_join(last)
        delta_one_b(zz, core)
        last = k
    gt_d[0].wait_recv()
    total = gtb[z, core].astype(f32) + gtp[z].astype(f32)
    for _ in range(3):
        adv(*t_g2)
    fin(*t_g2)
    for k in (1, 3, 2):
        gt_z[k].wait_recv()
        total = total + gtz[k - 1].astype(f32)
    gto[...] = total.astype(bf16)
    gt_x = [
        send(gto.at[ring(x, i), ring(y, j)], gtx.at[n], dp_dev(ring(x, i), ring(y, j)))
        for n, (i, j) in enumerate(plane)
    ]
    fin(*t_g3)
    z2[m, 0] = g2b[x, y, m]
    small = gto[x, y].astype(f32)
    for n, c in enumerate(gt_x):
        c.wait_recv()
        small = small + gtx[n].astype(f32)
    gs_ref[...] = small
    for o in range(8):
        for j in range(4):
            arrived(z2.at[o, j], zsem.at[4 * o + j], None if j else o)
    g2_ref[...] = jnp.transpose(jnp.sum(z2[...].astype(f32), axis=1).reshape(128, 256))
    for c, skip in sent:
        if skip is None:
            c.wait_send()
        else:
            pl.when(m != skip)(c.wait_send)


def run_kernel(*args):
    vm = pltpu.VMEM
    grad = [
        vm((4, 4, 8, 16, 256), bf16), vm((2, 3, 4, 4, 16, 256), bf16), vm((2, 3, 4, 16, 256), bf16),
    ]
    scratch = [
        vm((8, 128, 128), f32), vm((8, 64, 128), f32), vm((3, 64, 128), bf16),
        vm((3, 64, 128), bf16), vm((3, 64, 128), bf16), vm((3, 64, 128), bf16),
        vm((2, 16, 128), f32), vm((8, 16, 256), bf16),
        vm((4, 4, 8, 16, 256), bf16), vm((8, 4, 4, 16, 128), bf16), vm((4, 4, 8, 16, 256), bf16),
        vm((512, 128), bf16), vm((64, 512), bf16),
        vm((8, 512, 256), bf16), vm((8, 512, 256), f32), vm((256, 256), bf16),
        vm((512, 256), f32), vm((512, 256), f32),
        vm((8, 512, 256), bf16), vm((512, 256), bf16), vm((512, 256), bf16),
        vm((512, 256), bf16), vm((256, 512), bf16),
        *[vm((NROW, 64, ROWS), bf16)] * 3, vm((NROW, 3, 64, ROWS), bf16), vm((64, 512), bf16), vm((512, 128), bf16),
        vm((8, 512, 256), bf16), vm((4, 512, 256), bf16), vm((3, 512, 256), bf16),
        *grad, *grad[:2], vm((8, 256, 256), f32), vm((8, 64, 256), f32),
        vm((4, 2, 4, 4, 16, 128), bf16), vm((4, 4, 4, 16, 128), bf16), vm((3, 4, 4, 16, 128), bf16),
        vm((4, 4, 16, 128), bf16), vm((15, 16, 128), bf16), vm((8, 4, 16, 256), bf16),
        pltpu.SemaphoreType.DMA((NSEM,)), pltpu.SemaphoreType.DMA((NSEM,)),
        pltpu.SemaphoreType.DMA((32,)), pltpu.SemaphoreType.DMA((32,)),
    ]
    spec = pl.BlockSpec(memory_space=pltpu.VMEM)
    return pl.pallas_call(
        kernel,
        out_shape=(
            jax.ShapeDtypeStruct((256, 128), f32),
            jax.ShapeDtypeStruct((128, 256), f32),
            jax.ShapeDtypeStruct((16, 128), f32),
        ),
        in_specs=[spec] * 2 + [pl.BlockSpec(memory_space=pltpu.SMEM)] + [spec] * 4,
        out_specs=[spec] * 3,
        scratch_shapes=scratch,
        compiler_params=pltpu.CompilerParams(
            collective_id=0, has_side_effects=True, vmem_limit_bytes=60 * 1024 * 1024
        ),
        name="train_step",
    )(*args)


def update_kernel(
    g2, g3, gs, w_in, w_mid, w_top, w_out, m_in, m_mid, m_top, m_out,
    nw_in, nw_mid, nw_top, nw_out, nm_in, nm_mid, nm_top, nm_out,
):
    small = gs[...]
    grads = (small[:, 0:55], g2[...], g3[...], pltpu.roll(small, 64, 1)[:, 0:53])
    for grad, w, mo, nw, nm in zip(
        grads, (w_in, w_mid, w_top, w_out), (m_in, m_mid, m_top, m_out),
        (nw_in, nw_mid, nw_top, nw_out), (nm_in, nm_mid, nm_top, nm_out),
    ):
        value = momentum_decay * mo[...] + grad
        nm[...] = value
        nw[...] = w[...] - learn_rate * value


def on_device(
    samples, targets, counts,
    weight_in, weight_mid, weight_top, weight_out,
    moment_in, moment_mid, moment_top, moment_out,
):
    g_mid, g_top, g_small = run_kernel(
        jnp.transpose(samples, (1, 0, 2)), jnp.transpose(targets, (1, 0, 2)), counts,
        weight_in.T, weight_mid, weight_top, weight_out,
    )
    spec = pl.BlockSpec(memory_space=pltpu.VMEM)
    shapes = [(16, 55), (256, 128), (128, 256), (16, 53)] * 2
    out = pl.pallas_call(
        update_kernel,
        out_shape=[jax.ShapeDtypeStruct(s, f32) for s in shapes],
        in_specs=[spec] * 11,
        out_specs=[spec] * 8,
        name="update",
    )(
        g_mid, g_top, g_small, weight_in.T, weight_mid, weight_top, weight_out,
        moment_in.T, moment_mid, moment_top, moment_out,
    )
    return (out[0].T, *out[1:4], out[4].T, *out[5:])


def solution(mesh):
    weights = (P(None, ("mp", "dp")), P("mp", "dp"), P("dp", "mp"), P(("mp", "dp"), None))
    in_specs = (P("dp", None, None), P("dp", None, None), P("dp")) + weights + weights
    return jax.shard_map(
        on_device, mesh=mesh, in_specs=in_specs, out_specs=weights + weights, check_vma=False
    )
```

```python
import math

import jax
import jax.numpy as jnp
from jax import lax
from jax.experimental import pallas as pl
from jax.experimental.pallas import tpu as pltpu
from jax.sharding import PartitionSpec as P

momentum_decay = 0.9
learn_rate = 0.05
MESH = pl.DeviceIdType.MESH
f32, bf16 = jnp.float32, jnp.bfloat16
NSEM = 272
NROW = 2
ROWS = 512 // NROW


def gelu_act(value):
    return 0.5 * value * (1.0 + lax.erf(value * (1.0 / math.sqrt(2.0))))


def gelu_slope(value):
    return 0.5 * (1.0 + lax.erf(value * (1.0 / math.sqrt(2.0)))) + value * jnp.exp(
        -0.5 * value * value
    ) * (1.0 / math.sqrt(2.0 * math.pi))


def dot(left, right, a, b):
    return lax.dot_general(left, right, (((a,), (b,)), ((), ())), preferred_element_type=f32)


def adv(*tasks):
    for task in tasks:
        next(task, None)


def fin(*tasks):
    tasks = list(tasks)
    while tasks:
        tasks = [t for t in tasks if next(t, "end") != "end"]


def kernel(
    x_ref, y_ref, n_ref, win_ref, wmid_ref, wtop_ref, wout_ref,
    g2_ref, g3_ref, gs_ref,
    xf, yf, xs, ys, xr, yr, wide, w2s, cw, ct, w3b, xrow, xtb,
    h1, a1, d1, a2, a3, h2f, h3, d3, d2, d2t,
    psend, pp, psum, pr, et, erow,
    s2b, s2p, s2z,
    g3b, g3a, g3x, g2b, g2a, g2f, g1f, gtb, gtp, gtz, gto, gtx, z2,
    ssem, rsem, wsem, zsem,
):
    d, m = lax.axis_index("dp"), lax.axis_index("mp")
    x, y = lax.div(d, 4), lax.rem(d, 4)
    z, core = lax.div(m, 2), lax.rem(m, 2)

    def ring(v, k):
        return lax.rem(v + k, 4)

    def dp_dev(xx, yy):
        return (xx * 4 + yy, m)

    def mp_dev(mm):
        return (d, mm)

    partner = mp_dev(z * 2 + 1 - core)
    zdev = {k: mp_dev(ring(z, k) * 2 + core) for k in (1, 2, 3)}
    mdev = {k: lax.rem(m + k, 8) for k in range(1, 8)}
    plane = [(i, j) for i in range(4) for j in range(4) if i or j]
    plane.sort(key=lambda t: -((t[0] % 2) + (t[0] == 2) * 2 + (t[1] % 2) + (t[1] == 2) * 2))
    pair = dp_dev(ring(x, 2), y)

    count = [0]
    sent = []

    def send(src, dst, dev, sem=None, skip=None):
        k = count[0]
        count[0] += 1
        assert k < NSEM
        copy = pltpu.make_async_remote_copy(
            src_ref=src, dst_ref=dst, send_sem=ssem.at[k],
            recv_sem=rsem.at[k] if sem is None else sem,
            device_id=dev, device_id_type=MESH,
        )
        if skip is None:
            copy.start()
        else:
            pl.when(m != skip)(copy.start)
        sent.append((copy, skip))
        return copy

    def arrived(dst, sem, skip=None):
        copy = pltpu.make_async_remote_copy(
            src_ref=dst, dst_ref=dst, send_sem=ssem.at[0], recv_sem=sem,
            device_id=partner, device_id_type=MESH,
        )
        if skip is None:
            copy.wait_recv()
        else:
            pl.when(m != skip)(copy.wait_recv)

    barrier = pltpu.get_barrier_semaphore()
    peers = [dp_dev(ring(x, i), ring(y, j)) for i, j in plane]
    for i, j in [(0, 0)] + [t for t in plane if 0 in t]:
        peers += [(ring(x, i) * 4 + ring(y, j), mdev[k]) for k in range(1, 8)]
    for dev in peers:
        pl.semaphore_signal(barrier, inc=1, device_id=dev, device_id_type=MESH)

    lanes = lax.broadcasted_iota(jnp.int32, (16, 128), 1)
    wide[...] = jnp.zeros_like(wide)
    wide[0, :, 0:55] = win_ref[...]
    wide[1, :, 0:53] = wout_ref[...]
    tile = wide[0] + pltpu.roll(wide[1], 64, 1)
    tile = jnp.where(lanes == 127, jnp.full((16, 128), n_ref[0], jnp.int32).astype(f32), tile)
    ct[m, x, y] = tile.astype(bf16)
    w2s[...] = jnp.transpose(wmid_ref[...]).astype(bf16).reshape(8, 16, 256)
    w3b[x, y] = wtop_ref[...].astype(bf16).reshape(8, 16, 256)
    cw[x, y, m] = w2s[m]
    xf[...] = jnp.zeros_like(xf)
    yf[...] = jnp.zeros_like(yf)
    xf[:, 0:55] = jnp.transpose(x_ref[...].astype(f32), (1, 0, 2))
    yf[:, 0:53] = jnp.transpose(y_ref[...].astype(f32), (1, 0, 2))
    for q in range(3):
        xs[q] = xf[4 + q, 0:64].astype(bf16)
        ys[q] = yf[4 + q].astype(bf16)
    pl.semaphore_wait(barrier, len(peers))

    def gather(buf, part):
        ms = slice(4 * part, 4 * part + 4)
        pos = (x, y) if part == 0 else (y, x)

        def at(a, b):
            return buf.at[a, b, ms] if part == 0 else buf.at[b, a, ms]

        def dev(a, b):
            return dp_dev(a, b) if part == 0 else dp_dev(b, a)

        own = at(pos[0], pos[1])
        first = {k: send(own, own, dev(ring(pos[0], k), pos[1])) for k in (2, 1, 3)}
        yield
        waits = [send(own, own, dev(pos[0], ring(pos[1], k))) for k in (2, 1, 3)]
        yield
        for k in (1, 3, 2):
            first[k].wait_recv()
            got = at(ring(pos[0], 4 - k), pos[1])
            waits += [send(got, got, dev(pos[0], ring(pos[1], j))) for j in (2, 1, 3)]
            yield
        for c in waits:
            c.wait_recv()

    def gather_two(part):
        ms = slice(4 * part, 4 * part + 4)
        pos = (x, y) if part == 0 else (y, x)
        waits = []
        for j in (0, 1, 3, 2):
            a = ring(pos[0], 4 - j)
            src = (a, pos[1]) if part == 0 else (pos[1], a)
            for o in range(4 * part, 4 * part + 4):
                arrived(cw.at[src[0], src[1], o], wsem.at[4 * o + j], o if j == 0 else None)
            got = cw.at[src[0], src[1], ms]
            for k in (2, 1, 3):
                b = ring(pos[1], k)
                dev = dp_dev(pos[0], b) if part == 0 else dp_dev(b, pos[0])
                waits.append(send(got, got, dev))
            yield
        for c in waits:
            c.wait_recv()

    def scatter(buf, part, abuf, xbuf, finish, direct=False):
        lo = 4 * part
        ms = slice(lo, lo + 4)
        up, ap = (x, y) if part == 0 else (y, x)

        def at(u, a):
            return (u, a, ms) if part == 0 else (a, u, ms)

        def dev(u, a):
            return dp_dev(u, a) if part == 0 else dp_dev(a, u)

        first = {}
        for j in (2, 1, 3, 0):
            u = ring(up, j)
            for k in (2, 1, 3):
                first[j, k] = send(
                    buf.at[at(u, ring(ap, k))], abuf.at[part, k - 1, u], dev(up, ring(ap, k))
                )
        yield
        second = {}
        for j in (2, 1, 3, 0):
            u = ring(up, j)
            for k in (2, 1, 3):
                first[j, k].wait_recv()
            total = buf[at(u, ap)].astype(f32)
            for k in (1, 2, 3):
                total = total + abuf[part, k - 1, u].astype(f32)
            if j:
                buf[at(u, ap)] = total.astype(bf16)
                if direct:
                    for o in range(lo, lo + 4):
                        send(
                            buf.at[(u, ap, o) if part == 0 else (ap, u, o)], z2.at[m, j],
                            (dev(u, ap)[0], o), zsem.at[4 * m + j],
                        )
                    yield
                    continue
                second[j] = send(buf.at[at(u, ap)], xbuf.at[part, j - 1], dev(u, ap))
                yield
        for j in () if direct else (1, 3, 2):
            second[j].wait_recv()
            total = total + xbuf[part, j - 1].astype(f32)
        finish(lo, total)

    own_tile = ct.at[m, x, y]
    tile_copies = [send(own_tile, own_tile, dp_dev(ring(x, i), ring(y, j))) for i, j in plane]
    half = lax.div(m, 4)
    for j in (2, 1, 3, 0):
        there = ring(x, j * (1 - half)) * 4 + ring(y, j * half)
        for k in range(0 if j else 1, 8):
            c = lax.rem(m + k, 8)
            send(w2s.at[c], cw.at[x, y, m], (there, c), wsem.at[4 * m + j])
    x_copy = send(xs, xr, pair)
    t_cw = [gather_two(0), gather_two(1)]
    t_w3 = [gather(w3b, 0), gather(w3b, 1)]
    for c in tile_copies:
        c.wait_recv()
    own_block = ct.at[m]
    block_copies = {k: send(own_block, own_block, zdev[k]) for k in (2, 1, 3)}
    partner_blocks = {0: send(own_block, own_block, partner)}
    for _ in range(4):
        adv(*t_cw)
    adv(*t_w3)

    lane = ct[m].reshape(256, 128).astype(f32)[:, 127:128]
    scale = 2.0 / (jnp.sum(lane, axis=0, keepdims=True) * (1.0 / 16.0) * 128.0)
    mine = ct[m, x, y].astype(f32)[0:1, 127:128]
    theirs = ct[m, ring(x, 2), y].astype(f32)[0:1, 127:128]

    def pick(ref, recv, q):
        value = ref[q, 0:64]
        for k in range(3):
            if q - k < 1:
                continue
            take = jnp.broadcast_to(mine, value.shape) == float(q - k)
            value = jnp.where(take, recv[k].astype(f32), value)
        return value

    x_copy.wait_recv()
    for q in range(4):
        value = pick(xf, xr, q)
        xtb[:, q * 128:(q + 1) * 128] = value.astype(bf16)
        tall = jnp.concatenate([value, jnp.zeros((64, 128), f32)], axis=0)
        xrow[q * 128:(q + 1) * 128] = jnp.transpose(tall).astype(bf16)

    def rows_of(r):
        return slice(r * ROWS, (r + 1) * ROWS)

    def chunks(body, lo=0, n=ROWS, step=32):
        lax.fori_loop(0, n // step, lambda i, c: (body(pl.ds(pl.multiple_of(lo + i * step, step), step)), c)[1], 0)

    def layer_one(k):
        a1[k] = dot(xrow[...], ct[k].reshape(256, 128), 1, 1)

        def act(rr):
            h1[k, rr] = gelu_act(a1[k, rr]).astype(bf16)

        chunks(act, 0, 512)

    def slope_one(lo, hi):
        def body(k, carry):
            def act(rr):
                a1[k, rr] = gelu_slope(a1[k, rr])

            chunks(act, 0, 512)
            return carry

        lax.fori_loop(lo, hi, body, 0)

    layer_one(m)
    partner_blocks[0].wait_recv()
    layer_one(z * 2 + 1 - core)
    for k in (1, 3, 2):
        block_copies[k].wait_recv()
        blk = ring(z, 4 - k) * 2 + core
        partner_blocks[k] = send(ct.at[blk], ct.at[blk], partner)
        layer_one(blk)
    adv(*t_w3)
    y_copy = send(ys, yr, pair)
    for k in (1, 3, 2):
        partner_blocks[k].wait_recv()
        layer_one(ring(z, 4 - k) * 2 + 1 - core)
    fin(*t_cw)

    def layer_two(r):
        total = jnp.zeros((ROWS, 256), f32)
        for k in range(8):
            total = total + dot(h1[k, rows_of(r)], cw[:, :, k].reshape(256, 256), 1, 1)
        a2[rows_of(r)] = total

        def act(rr):
            h2f[m, rr] = gelu_act(a2[rr]).astype(bf16)

        chunks(act, r * ROWS)

    h2_z, h2_p = ([{} for _ in range(NROW)] for _ in range(2))

    def h2_send(r):
        own = h2f.at[m, rows_of(r)]
        for k in (2, 1, 3):
            h2_z[r][k] = send(own, own, zdev[k])
        h2_p[r][0] = send(own, own, partner)

    layer_two(0)
    h2_send(0)
    for _ in range(3):
        adv(*t_w3)
    layer_two(1)
    h2_send(1)
    slope_one(0, 8)

    tm = ct[m].reshape(256, 128)

    def h2_forward(r):
        for k in (1, 3, 2):
            h2_z[r][k].wait_recv()
            view = h2f.at[ring(z, 4 - k) * 2 + core, rows_of(r)]
            h2_p[r][k] = send(view, view, partner)

    def layer_three(r):
        rows = rows_of(r)

        def part(k):
            return dot(h2f[k, rows], w3b[:, :, k].reshape(256, 256), 1, 0)

        a3[rows] = part(m)
        h2_p[r][0].wait_recv()
        a3[rows] += part(z * 2 + 1 - core)
        for k in (1, 3, 2):
            a3[rows] += part(ring(z, 4 - k) * 2 + core)
        for k in (1, 3, 2):
            h2_p[r][k].wait_recv()
            a3[rows] += part(ring(z, 4 - k) * 2 + 1 - core)

        def act(rr):
            v = a3[rr]
            h3[rr] = gelu_act(v).astype(bf16)

        chunks(act, r * ROWS)
        psend[r] = jnp.transpose(dot(h3[rows], tm, 1, 0))[64:128].astype(bf16)

    def slope_three(r):
        def act(rr):
            a3[rr] = gelu_slope(a3[rr])

        chunks(act, r * ROWS)

    def slope_two(r):
        def act(rr):
            a2[rr] = gelu_slope(a2[rr])

        chunks(act, r * ROWS)

    def p_task(r):
        c = send(psend.at[r], pp.at[r], partner)
        yield
        c.wait_recv()
        psum[r] = (psend[r].astype(f32) + pp[r].astype(f32)).astype(bf16)
        cs = [send(psum.at[r], pr.at[r, k - 1], zdev[k]) for k in (2, 1, 3)]
        yield
        for c in cs:
            c.wait_recv()

    t_p = [p_task(r) for r in range(NROW)]
    slope_two(0)
    slope_two(1)
    h2_forward(0)
    fin(*t_w3)
    layer_three(0)
    adv(t_p[0])
    slope_three(0)
    adv(t_p[0])
    h2_forward(1)
    layer_three(1)
    adv(t_p[1])
    slope_three(1)
    adv(t_p[1])
    y_copy.wait_recv()
    fin(t_p[0])

    sub = lax.broadcasted_iota(jnp.int32, (64, 128), 0)

    def error(r):
        for h in range(4 // NROW):
            q = (4 // NROW) * r + h
            ls = slice(h * 128, (h + 1) * 128)
            want = pick(yf, yr, q)
            own_n = jnp.broadcast_to(mine, (64, 128))
            pair_n = jnp.broadcast_to(theirs, (64, 128))
            live = (own_n > float(q)) | (4.0 + float(q) - own_n < pair_n)
            predicted = psum[r, :, ls].astype(f32)
            for k in range(3):
                predicted = predicted + pr[r, k, :, ls].astype(f32)
            value = jnp.broadcast_to(scale, (64, 128)) * (predicted - want)
            value = jnp.where(live & (sub < 53), value, 0.0)
            et[:, q * 128:(q + 1) * 128] = value.astype(bf16)
            tall = jnp.concatenate([jnp.zeros((64, 128), f32), value], axis=0)
            erow[q * 128:(q + 1) * 128] = jnp.transpose(tall).astype(bf16)

    def delta_three(r):
        d3[rows_of(r)] = (dot(erow[rows_of(r)], tm, 1, 1) * a3[rows_of(r)]).astype(bf16)

    s2_d, s2_s = ([{} for _ in range(NROW)] for _ in range(2))

    def s2_part(r):
        dv = d3[rows_of(r)]
        for own in (False, True):
            for k in (2, 1, 3, 0):
                zz = ring(z, k)
                c = zz * 2 + (core if own else 1 - core)
                s2b[c, rows_of(r)] = dot(dv, w3b[:, :, c].reshape(256, 256), 1, 1).astype(bf16)
                if not own:
                    s2_d[r][k] = send(s2b.at[c, rows_of(r)], s2p.at[zz, rows_of(r)], partner)

    def s2_join(r):
        rr = rows_of(r)
        for k in (2, 1, 3):
            s2_d[r][k].wait_recv()
            zz = ring(z, k)
            c = zz * 2 + core
            s2b[c, rr] = (s2b[c, rr].astype(f32) + s2p[zz, rr].astype(f32)).astype(bf16)
            s2_s[r][k] = send(s2b.at[c, rr], s2z.at[k - 1, rr], zdev[k])

    def s2_end(r):
        rr = rows_of(r)
        s2_d[r][0].wait_recv()
        for k in (1, 3, 2):
            s2_s[r][k].wait_recv()
        total = s2b[m, rr].astype(f32) + s2p[z, rr].astype(f32)
        for k in range(3):
            total = total + s2z[k, rr].astype(f32)
        a2[rr] = total * a2[rr]
        d2[rr] = a2[rr].astype(bf16)
        d2t[:, rr] = jnp.transpose(a2[rr]).astype(bf16)

    error(0)
    delta_three(0)
    s2_part(0)
    s2_join(0)
    fin(t_p[1])
    error(1)
    delta_three(1)
    s2_part(1)
    s2_join(1)

    def grad_three(k, carry):
        g3b[:, :, k] = dot(h2f[k], d3[...], 0, 0).astype(bf16).reshape(4, 4, 16, 256)
        return carry

    def finish_three(lo, total):
        g3_ref[lo * 16:(lo + 4) * 16] = total.reshape(64, 256)

    t_g3 = [scatter(g3b, p, g3a, g3x, finish_three) for p in range(2)]
    lax.fori_loop(0, 4, grad_three, 0)
    adv(t_g3[0])
    lax.fori_loop(4, 8, grad_three, 0)
    adv(t_g3[1])
    g4 = dot(et[...], h3[...], 1, 0)

    def finish_two(lo, total):
        g2b[x, y, lo:lo + 4] = total.astype(bf16)
        for o in range(lo, lo + 4):
            send(g2b.at[x, y, o], z2.at[m, 0], mp_dev(o), zsem.at[4 * m], o)

    t_g2 = [scatter(g2b, p, g2a, None, finish_two, True) for p in range(2)]

    upper, lower = slice(0, 256), slice(256, 512)

    def grad_two_a(k, carry):
        g2f[k] = dot(d2t[:, upper], h1[k, upper], 1, 0)
        return carry

    def grad_two_b(k, carry):
        total = g2f[k] + dot(d2t[:, lower], h1[k, lower], 1, 0)
        g2b[:, :, k] = total.astype(bf16).reshape(4, 4, 16, 256)
        return carry

    def grad_one(k, half):
        back = dot(d2[half], cw[:, :, k].reshape(256, 256), 1, 0)
        d1[...] = (back * a1[k, half]).astype(bf16)
        return dot(xtb[:, half], d1[...], 1, 0)

    def delta_one_a(k, carry):
        g1f[k] = grad_one(k, upper)
        return carry

    def delta_one_b(zz, side):
        k = 2 * zz + side
        low = g1f[k] + grad_one(k, lower)
        own = jnp.where(jnp.full((64, 256), k, jnp.int32) == m, g4, 0.0)
        tall = jnp.transpose(jnp.concatenate([low, own], axis=0))
        gtb[zz, side] = tall.astype(bf16).reshape(4, 4, 16, 128)

    s2_end(0)
    lax.fori_loop(0, 8, grad_two_a, 0)
    lax.fori_loop(0, 8, delta_one_a, 0)
    s2_end(1)
    lax.fori_loop(0, 4, grad_two_b, 0)
    adv(t_g2[0])
    lax.fori_loop(4, 8, grad_two_b, 0)
    adv(t_g2[1])
    for _ in range(3):
        adv(*t_g3)
    gt_d, gt_z = {}, {}

    def gt_join(k):
        zz = ring(z, k)
        gt_d[k].wait_recv()
        gtb[zz, core] = (gtb[zz, core].astype(f32) + gtp[zz].astype(f32)).astype(bf16)
        gt_z[k] = send(gtb.at[zz, core], gtz.at[k - 1], zdev[k])

    last = None
    for k in (2, 1, 3, 0):
        zz = ring(z, k)
        delta_one_b(zz, 1 - core)
        gt_d[k] = send(gtb.at[zz, 1 - core], gtp.at[zz], partner)
        if last:
            gt_join(last)
        delta_one_b(zz, core)
        last = k
    gt_d[0].wait_recv()
    total = gtb[z, core].astype(f32) + gtp[z].astype(f32)
    adv(*t_g2)
    adv(*t_g2)
    for k in (1, 3, 2):
        gt_z[k].wait_recv()
        total = total + gtz[k - 1].astype(f32)
    gto[...] = total.astype(bf16)
    gt_x = [
        send(gto.at[ring(x, i), ring(y, j)], gtx.at[n], dp_dev(ring(x, i), ring(y, j)))
        for n, (i, j) in enumerate(plane)
    ]
    adv(*t_g2)
    fin(*t_g2)
    fin(*t_g3)
    z2[m, 0] = g2b[x, y, m]
    small = gto[x, y].astype(f32)
    for n, c in enumerate(gt_x):
        c.wait_recv()
        small = small + gtx[n].astype(f32)
    gs_ref[...] = small
    for o in range(8):
        for j in range(4):
            arrived(z2.at[o, j], zsem.at[4 * o + j], None if j else o)
    g2_ref[...] = jnp.transpose(jnp.sum(z2[...].astype(f32), axis=1).reshape(128, 256))
    for c, skip in sent:
        if skip is None:
            c.wait_send()
        else:
            pl.when(m != skip)(c.wait_send)


def run_kernel(*args):
    vm = pltpu.VMEM
    grad = [
        vm((4, 4, 8, 16, 256), bf16), vm((2, 3, 4, 4, 16, 256), bf16), vm((2, 3, 4, 16, 256), bf16),
    ]
    scratch = [
        vm((8, 128, 128), f32), vm((8, 64, 128), f32), vm((3, 64, 128), bf16),
        vm((3, 64, 128), bf16), vm((3, 64, 128), bf16), vm((3, 64, 128), bf16),
        vm((2, 16, 128), f32), vm((8, 16, 256), bf16),
        vm((4, 4, 8, 16, 256), bf16), vm((8, 4, 4, 16, 128), bf16), vm((4, 4, 8, 16, 256), bf16),
        vm((512, 128), bf16), vm((64, 512), bf16),
        vm((8, 512, 256), bf16), vm((8, 512, 256), f32), vm((256, 256), bf16),
        vm((512, 256), f32), vm((512, 256), f32),
        vm((8, 512, 256), bf16), vm((512, 256), bf16), vm((512, 256), bf16),
        vm((512, 256), bf16), vm((256, 512), bf16),
        *[vm((NROW, 64, ROWS), bf16)] * 3, vm((NROW, 3, 64, ROWS), bf16), vm((64, 512), bf16), vm((512, 128), bf16),
        vm((8, 512, 256), bf16), vm((4, 512, 256), bf16), vm((3, 512, 256), bf16),
        *grad, *grad[:2], vm((8, 256, 256), f32), vm((8, 64, 256), f32),
        vm((4, 2, 4, 4, 16, 128), bf16), vm((4, 4, 4, 16, 128), bf16), vm((3, 4, 4, 16, 128), bf16),
        vm((4, 4, 16, 128), bf16), vm((15, 16, 128), bf16), vm((8, 4, 16, 256), bf16),
        pltpu.SemaphoreType.DMA((NSEM,)), pltpu.SemaphoreType.DMA((NSEM,)),
        pltpu.SemaphoreType.DMA((32,)), pltpu.SemaphoreType.DMA((32,)),
    ]
    spec = pl.BlockSpec(memory_space=pltpu.VMEM)
    return pl.pallas_call(
        kernel,
        out_shape=(
            jax.ShapeDtypeStruct((256, 128), f32),
            jax.ShapeDtypeStruct((128, 256), f32),
            jax.ShapeDtypeStruct((16, 128), f32),
        ),
        in_specs=[spec] * 2 + [pl.BlockSpec(memory_space=pltpu.SMEM)] + [spec] * 4,
        out_specs=[spec] * 3,
        scratch_shapes=scratch,
        compiler_params=pltpu.CompilerParams(
            collective_id=0, has_side_effects=True, vmem_limit_bytes=60 * 1024 * 1024
        ),
        name="train_step",
    )(*args)


def update_kernel(
    g2, g3, gs, w_in, w_mid, w_top, w_out, m_in, m_mid, m_top, m_out,
    nw_in, nw_mid, nw_top, nw_out, nm_in, nm_mid, nm_top, nm_out,
):
    small = gs[...]
    grads = (small[:, 0:55], g2[...], g3[...], pltpu.roll(small, 64, 1)[:, 0:53])
    for grad, w, mo, nw, nm in zip(
        grads, (w_in, w_mid, w_top, w_out), (m_in, m_mid, m_top, m_out),
        (nw_in, nw_mid, nw_top, nw_out), (nm_in, nm_mid, nm_top, nm_out),
    ):
        value = momentum_decay * mo[...] + grad
        nm[...] = value
        nw[...] = w[...] - learn_rate * value


def on_device(
    samples, targets, counts,
    weight_in, weight_mid, weight_top, weight_out,
    moment_in, moment_mid, moment_top, moment_out,
):
    g_mid, g_top, g_small = run_kernel(
        jnp.transpose(samples, (1, 0, 2)), jnp.transpose(targets, (1, 0, 2)), counts,
        weight_in.T, weight_mid, weight_top, weight_out,
    )
    spec = pl.BlockSpec(memory_space=pltpu.VMEM)
    shapes = [(16, 55), (256, 128), (128, 256), (16, 53)] * 2
    out = pl.pallas_call(
        update_kernel,
        out_shape=[jax.ShapeDtypeStruct(s, f32) for s in shapes],
        in_specs=[spec] * 11,
        out_specs=[spec] * 8,
        name="update",
    )(
        g_mid, g_top, g_small, weight_in.T, weight_mid, weight_top, weight_out,
        moment_in.T, moment_mid, moment_top, moment_out,
    )
    return (out[0].T, *out[1:4], out[4].T, *out[5:])


def solution(mesh):
    weights = (P(None, ("mp", "dp")), P("mp", "dp"), P("dp", "mp"), P(("mp", "dp"), None))
    in_specs = (P("dp", None, None), P("dp", None, None), P("dp")) + weights + weights
    return jax.shard_map(
        on_device, mesh=mesh, in_specs=in_specs, out_specs=weights + weights, check_vma=False
    )
```

```python
import math

import jax
import jax.numpy as jnp
from jax import lax
from jax.experimental import pallas as pl
from jax.experimental.pallas import tpu as pltpu
from jax.sharding import PartitionSpec as P

momentum_decay = 0.9
learn_rate = 0.05
MESH = pl.DeviceIdType.MESH
f32, bf16 = jnp.float32, jnp.bfloat16
NSEM = 272
NROW = 2
ROWS = 512 // NROW


def gelu_act(value):
    return 0.5 * value * (1.0 + lax.erf(value * (1.0 / math.sqrt(2.0))))


def gelu_slope(value):
    return 0.5 * (1.0 + lax.erf(value * (1.0 / math.sqrt(2.0)))) + value * jnp.exp(
        -0.5 * value * value
    ) * (1.0 / math.sqrt(2.0 * math.pi))


def dot(left, right, a, b):
    return lax.dot_general(left, right, (((a,), (b,)), ((), ())), preferred_element_type=f32)


def adv(*tasks):
    for task in tasks:
        next(task, None)


def fin(*tasks):
    tasks = list(tasks)
    while tasks:
        tasks = [t for t in tasks if next(t, "end") != "end"]


def kernel(
    x_ref, y_ref, n_ref, win_ref, wmid_ref, wtop_ref, wout_ref,
    g2_ref, g3_ref, gs_ref,
    xf, yf, xs, ys, xr, yr, wide, w2s, cw, ct, w3b, xrow, xtb,
    h1, a1, a2, a3, h2f, h3, d3, d2, d2t,
    psend, pp, psum, pr, et, erow,
    s2b, s2p, s2z,
    g3b, g3a, g3x, g2b, g2a, g2f, g1f, gtb, gtp, gtz, gto, gtx, z2,
    ssem, rsem, wsem, zsem,
):
    d, m = lax.axis_index("dp"), lax.axis_index("mp")
    x, y = lax.div(d, 4), lax.rem(d, 4)
    z, core = lax.div(m, 2), lax.rem(m, 2)

    def ring(v, k):
        return lax.rem(v + k, 4)

    def dp_dev(xx, yy):
        return (xx * 4 + yy, m)

    def mp_dev(mm):
        return (d, mm)

    partner = mp_dev(z * 2 + 1 - core)
    zdev = {k: mp_dev(ring(z, k) * 2 + core) for k in (1, 2, 3)}
    mdev = {k: lax.rem(m + k, 8) for k in range(1, 8)}
    plane = [(i, j) for i in range(4) for j in range(4) if i or j]
    plane.sort(key=lambda t: -((t[0] % 2) + (t[0] == 2) * 2 + (t[1] % 2) + (t[1] == 2) * 2))
    pair = dp_dev(ring(x, 2), y)

    count = [0]
    sent = []

    def send(src, dst, dev, sem=None, skip=None):
        k = count[0]
        count[0] += 1
        assert k < NSEM
        copy = pltpu.make_async_remote_copy(
            src_ref=src, dst_ref=dst, send_sem=ssem.at[k],
            recv_sem=rsem.at[k] if sem is None else sem,
            device_id=dev, device_id_type=MESH,
        )
        if skip is None:
            copy.start()
        else:
            pl.when(m != skip)(copy.start)
        sent.append((copy, skip))
        return copy

    def arrived(dst, sem, skip=None):
        copy = pltpu.make_async_remote_copy(
            src_ref=dst, dst_ref=dst, send_sem=ssem.at[0], recv_sem=sem,
            device_id=partner, device_id_type=MESH,
        )
        if skip is None:
            copy.wait_recv()
        else:
            pl.when(m != skip)(copy.wait_recv)

    barrier = pltpu.get_barrier_semaphore()
    peers = [dp_dev(ring(x, i), ring(y, j)) for i, j in plane]
    for i, j in [(0, 0)] + [t for t in plane if 0 in t]:
        peers += [(ring(x, i) * 4 + ring(y, j), mdev[k]) for k in range(1, 8)]
    for dev in peers:
        pl.semaphore_signal(barrier, inc=1, device_id=dev, device_id_type=MESH)

    lanes = lax.broadcasted_iota(jnp.int32, (16, 128), 1)
    wide[...] = jnp.zeros_like(wide)
    wide[0, :, 0:55] = win_ref[...]
    wide[1, :, 0:53] = wout_ref[...]
    tile = wide[0] + pltpu.roll(wide[1], 64, 1)
    tile = jnp.where(lanes == 127, jnp.full((16, 128), n_ref[0], jnp.int32).astype(f32), tile)
    ct[m, x, y] = tile.astype(bf16)
    w2s[...] = jnp.transpose(wmid_ref[...]).astype(bf16).reshape(8, 16, 256)
    w3b[x, y] = wtop_ref[...].astype(bf16).reshape(8, 16, 256)
    cw[x, y, m] = w2s[m]
    xf[...] = jnp.zeros_like(xf)
    yf[...] = jnp.zeros_like(yf)
    xf[:, 0:55] = jnp.transpose(x_ref[...].astype(f32), (1, 0, 2))
    yf[:, 0:53] = jnp.transpose(y_ref[...].astype(f32), (1, 0, 2))
    for q in range(3):
        xs[q] = xf[4 + q, 0:64].astype(bf16)
        ys[q] = yf[4 + q].astype(bf16)
    pl.semaphore_wait(barrier, len(peers))

    def gather(buf, part):
        ms = slice(4 * part, 4 * part + 4)
        pos = (x, y) if part == 0 else (y, x)

        def at(a, b):
            return buf.at[a, b, ms] if part == 0 else buf.at[b, a, ms]

        def dev(a, b):
            return dp_dev(a, b) if part == 0 else dp_dev(b, a)

        own = at(pos[0], pos[1])
        first = {k: send(own, own, dev(ring(pos[0], k), pos[1])) for k in (2, 1, 3)}
        yield
        waits = [send(own, own, dev(pos[0], ring(pos[1], k))) for k in (2, 1, 3)]
        yield
        for k in (1, 3, 2):
            first[k].wait_recv()
            got = at(ring(pos[0], 4 - k), pos[1])
            waits += [send(got, got, dev(pos[0], ring(pos[1], j))) for j in (2, 1, 3)]
            yield
        for c in waits:
            c.wait_recv()

    def gather_two(part):
        ms = slice(4 * part, 4 * part + 4)
        pos = (x, y) if part == 0 else (y, x)
        waits = []
        for j in (0, 1, 3, 2):
            a = ring(pos[0], 4 - j)
            src = (a, pos[1]) if part == 0 else (pos[1], a)
            for o in range(4 * part, 4 * part + 4):
                arrived(cw.at[src[0], src[1], o], wsem.at[4 * o + j], o if j == 0 else None)
            got = cw.at[src[0], src[1], ms]
            for k in (2, 1, 3):
                b = ring(pos[1], k)
                dev = dp_dev(pos[0], b) if part == 0 else dp_dev(b, pos[0])
                waits.append(send(got, got, dev))
            yield
        for c in waits:
            c.wait_recv()

    def scatter(buf, part, abuf, xbuf, finish, direct=False):
        lo = 4 * part
        ms = slice(lo, lo + 4)
        up, ap = (x, y) if part == 0 else (y, x)

        def at(u, a):
            return (u, a, ms) if part == 0 else (a, u, ms)

        def dev(u, a):
            return dp_dev(u, a) if part == 0 else dp_dev(a, u)

        first = {}
        for j in (2, 1, 3, 0):
            u = ring(up, j)
            for k in (2, 1, 3):
                first[j, k] = send(
                    buf.at[at(u, ring(ap, k))], abuf.at[part, k - 1, u], dev(up, ring(ap, k))
                )
        yield
        second = {}
        for j in (2, 1, 3, 0):
            u = ring(up, j)
            for k in (2, 1, 3):
                first[j, k].wait_recv()
            total = buf[at(u, ap)].astype(f32)
            for k in (1, 2, 3):
                total = total + abuf[part, k - 1, u].astype(f32)
            if j:
                buf[at(u, ap)] = total.astype(bf16)
                if direct:
                    for o in range(lo, lo + 4):
                        send(
                            buf.at[(u, ap, o) if part == 0 else (ap, u, o)], z2.at[m, j],
                            (dev(u, ap)[0], o), zsem.at[4 * m + j],
                        )
                    yield
                    continue
                second[j] = send(buf.at[at(u, ap)], xbuf.at[part, j - 1], dev(u, ap))
                yield
        for j in () if direct else (1, 3, 2):
            second[j].wait_recv()
            total = total + xbuf[part, j - 1].astype(f32)
        finish(lo, total)

    own_tile = ct.at[m, x, y]
    tile_copies = [send(own_tile, own_tile, dp_dev(ring(x, i), ring(y, j))) for i, j in plane]
    half = lax.div(m, 4)
    for j in (2, 1, 3, 0):
        there = ring(x, j * (1 - half)) * 4 + ring(y, j * half)
        for k in range(0 if j else 1, 8):
            c = lax.rem(m + k, 8)
            send(w2s.at[c], cw.at[x, y, m], (there, c), wsem.at[4 * m + j])
    x_copy = send(xs, xr, pair)
    t_cw = [gather_two(0), gather_two(1)]
    t_w3 = [gather(w3b, 0), gather(w3b, 1)]
    for c in tile_copies:
        c.wait_recv()
    own_block = ct.at[m]
    block_copies = {k: send(own_block, own_block, zdev[k]) for k in (2, 1, 3)}
    partner_blocks = {0: send(own_block, own_block, partner)}
    for _ in range(4):
        adv(*t_cw)
    adv(*t_w3)

    lane = ct[m].reshape(256, 128).astype(f32)[:, 127:128]
    scale = 2.0 / (jnp.sum(lane, axis=0, keepdims=True) * (1.0 / 16.0) * 128.0)
    mine = ct[m, x, y].astype(f32)[0:1, 127:128]
    theirs = ct[m, ring(x, 2), y].astype(f32)[0:1, 127:128]

    def pick(ref, recv, q):
        value = ref[q, 0:64]
        for k in range(3):
            if q - k < 1:
                continue
            take = jnp.broadcast_to(mine, value.shape) == float(q - k)
            value = jnp.where(take, recv[k].astype(f32), value)
        return value

    x_copy.wait_recv()
    for q in range(4):
        value = pick(xf, xr, q)
        xtb[:, q * 128:(q + 1) * 128] = value.astype(bf16)
        tall = jnp.concatenate([value, jnp.zeros((64, 128), f32)], axis=0)
        xrow[q * 128:(q + 1) * 128] = jnp.transpose(tall).astype(bf16)

    def rows_of(r):
        return slice(r * ROWS, (r + 1) * ROWS)

    def chunks(body, lo=0, n=ROWS, step=32):
        lax.fori_loop(0, n // step, lambda i, c: (body(pl.ds(pl.multiple_of(lo + i * step, step), step)), c)[1], 0)

    def layer_one(k):
        a1[k] = dot(xrow[...], ct[k].reshape(256, 128), 1, 1)

        def act(rr):
            h1[k, rr] = gelu_act(a1[k, rr]).astype(bf16)

        chunks(act, 0, 512)

    def slope_one(lo, hi):
        def body(k, carry):
            def act(rr):
                a1[k, rr] = gelu_slope(a1[k, rr])

            chunks(act, 0, 512)
            return carry

        lax.fori_loop(lo, hi, body, 0)

    layer_one(m)
    partner_blocks[0].wait_recv()
    layer_one(z * 2 + 1 - core)
    for k in (1, 3, 2):
        block_copies[k].wait_recv()
        blk = ring(z, 4 - k) * 2 + core
        partner_blocks[k] = send(ct.at[blk], ct.at[blk], partner)
        layer_one(blk)
    adv(*t_w3)
    y_copy = send(ys, yr, pair)
    for k in (1, 3, 2):
        partner_blocks[k].wait_recv()
        layer_one(ring(z, 4 - k) * 2 + 1 - core)
    fin(*t_cw)

    def layer_two(r):
        total = jnp.zeros((ROWS, 256), f32)
        for k in range(8):
            total = total + dot(h1[k, rows_of(r)], cw[:, :, k].reshape(256, 256), 1, 1)
        a2[rows_of(r)] = total

        def act(rr):
            h2f[m, rr] = gelu_act(a2[rr]).astype(bf16)

        chunks(act, r * ROWS)

    h2_z, h2_p = ([{} for _ in range(NROW)] for _ in range(2))

    def h2_send(r):
        own = h2f.at[m, rows_of(r)]
        for k in (1, 3):
            h2_z[r][k] = send(own, own, zdev[k])
        h2_p[r][0] = send(own, own, partner)

    layer_two(0)
    h2_send(0)
    for _ in range(3):
        adv(*t_w3)
    layer_two(1)
    h2_send(1)
    slope_one(0, 8)

    tm = ct[m].reshape(256, 128)

    h2_far = [[], []]

    def h2_relay(r):
        rows = rows_of(r)
        for k in (1, 3):
            blk = ring(z, 4 - k) * 2 + core
            h2_z[r][k].wait_recv()
            lo = r * ROWS + (0 if k == 1 else ROWS // 2)
            view = h2f.at[blk, slice(lo, lo + ROWS // 2)]
            h2_far[r].append(send(view, view, zdev[k]))
            view = h2f.at[blk, rows]
            h2_p[r][k] = send(view, view, partner)

    def h2_forward(r):
        for c in h2_far[r]:
            c.wait_recv()
        view = h2f.at[ring(z, 2) * 2 + core, rows_of(r)]
        h2_p[r][2] = send(view, view, partner)

    def layer_three(r):
        rows = rows_of(r)

        def part(k):
            return dot(h2f[k, rows], w3b[:, :, k].reshape(256, 256), 1, 0)

        a3[rows] = part(m)
        h2_p[r][0].wait_recv()
        a3[rows] += part(z * 2 + 1 - core)
        for k in (1, 3, 2):
            a3[rows] += part(ring(z, 4 - k) * 2 + core)
        for k in (1, 3, 2):
            h2_p[r][k].wait_recv()
            a3[rows] += part(ring(z, 4 - k) * 2 + 1 - core)

        def act(rr):
            v = a3[rr]
            h3[rr] = gelu_act(v).astype(bf16)

        chunks(act, r * ROWS)
        psend[r] = jnp.transpose(dot(h3[rows], tm, 1, 0))[64:128].astype(bf16)

    def slope_three(r):
        def act(rr):
            a3[rr] = gelu_slope(a3[rr])

        chunks(act, r * ROWS)

    def slope_two(r):
        def act(rr):
            a2[rr] = gelu_slope(a2[rr])

        chunks(act, r * ROWS)

    def p_task(r):
        c = send(psend.at[r], pp.at[r], partner)
        yield
        c.wait_recv()
        psum[r] = (psend[r].astype(f32) + pp[r].astype(f32)).astype(bf16)
        cs = [send(psum.at[r], pr.at[r, k - 1], zdev[k]) for k in (2, 1, 3)]
        yield
        for c in cs:
            c.wait_recv()

    t_p = [p_task(r) for r in range(NROW)]
    slope_two(0)
    slope_two(1)
    h2_relay(0)
    h2_relay(1)
    h2_forward(0)
    fin(*t_w3)
    layer_three(0)
    adv(t_p[0])
    slope_three(0)
    adv(t_p[0])
    h2_forward(1)
    layer_three(1)
    adv(t_p[1])
    slope_three(1)
    adv(t_p[1])
    y_copy.wait_recv()
    fin(t_p[0])

    sub = lax.broadcasted_iota(jnp.int32, (64, 128), 0)

    def error(r):
        for h in range(4 // NROW):
            q = (4 // NROW) * r + h
            ls = slice(h * 128, (h + 1) * 128)
            want = pick(yf, yr, q)
            own_n = jnp.broadcast_to(mine, (64, 128))
            pair_n = jnp.broadcast_to(theirs, (64, 128))
            live = (own_n > float(q)) | (4.0 + float(q) - own_n < pair_n)
            predicted = psum[r, :, ls].astype(f32)
            for k in range(3):
                predicted = predicted + pr[r, k, :, ls].astype(f32)
            value = jnp.broadcast_to(scale, (64, 128)) * (predicted - want)
            value = jnp.where(live & (sub < 53), value, 0.0)
            et[:, q * 128:(q + 1) * 128] = value.astype(bf16)
            tall = jnp.concatenate([jnp.zeros((64, 128), f32), value], axis=0)
            erow[q * 128:(q + 1) * 128] = jnp.transpose(tall).astype(bf16)

    def delta_three(r):
        d3[rows_of(r)] = (dot(erow[rows_of(r)], tm, 1, 1) * a3[rows_of(r)]).astype(bf16)

    s2_d, s2_s = ([{} for _ in range(NROW)] for _ in range(2))

    def s2_part(r):
        dv = d3[rows_of(r)]
        for own in (False, True):
            for k in (2, 1, 3, 0):
                zz = ring(z, k)
                c = zz * 2 + (core if own else 1 - core)
                s2b[c, rows_of(r)] = dot(dv, w3b[:, :, c].reshape(256, 256), 1, 1).astype(bf16)
                if not own:
                    s2_d[r][k] = send(s2b.at[c, rows_of(r)], s2p.at[zz, rows_of(r)], partner)

    s2_a = [{}, {}]

    def s2_half(r, k):
        lo = r * ROWS + (0 if k == 1 else ROWS // 2)
        return slice(lo, lo + ROWS // 2)

    def s2_join(r):
        rr = rows_of(r)
        for k in (2, 1, 3):
            s2_d[r][k].wait_recv()
            zz = ring(z, k)
            c = zz * 2 + core
            s2b[c, rr] = (s2b[c, rr].astype(f32) + s2p[zz, rr].astype(f32)).astype(bf16)
            if k == 2:
                for j in (1, 3):
                    hh = s2_half(r, j)
                    s2_a[r][j] = send(s2b.at[c, hh], s2z.at[2, hh], zdev[j])

    def s2_relay(r):
        for k in (1, 3):
            s2_a[r][k].wait_recv()
            c, hh = ring(z, k) * 2 + core, s2_half(r, k)
            s2b[c, hh] = (s2b[c, hh].astype(f32) + s2z[2, hh].astype(f32)).astype(bf16)
            s2_s[r][k] = send(s2b.at[c, rows_of(r)], s2z.at[k // 2, rows_of(r)], zdev[k])

    def s2_end(r):
        rr = rows_of(r)
        s2_d[r][0].wait_recv()
        total = s2b[m, rr].astype(f32) + s2p[z, rr].astype(f32)
        for k in (1, 3):
            s2_s[r][k].wait_recv()
            total = total + s2z[k // 2, rr].astype(f32)
        a2[rr] = total * a2[rr]
        d2[rr] = a2[rr].astype(bf16)
        d2t[:, rr] = jnp.transpose(a2[rr]).astype(bf16)

    error(0)
    delta_three(0)
    s2_part(0)
    s2_join(0)
    fin(t_p[1])
    error(1)
    delta_three(1)
    s2_part(1)
    s2_join(1)

    def grad_three(k, carry):
        g3b[:, :, k] = dot(h2f[k], d3[...], 0, 0).astype(bf16).reshape(4, 4, 16, 256)
        return carry

    def finish_three(lo, total):
        g3_ref[lo * 16:(lo + 4) * 16] = total.reshape(64, 256)

    t_g3 = [scatter(g3b, p, g3a, g3x, finish_three) for p in range(2)]
    lax.fori_loop(0, 4, grad_three, 0)
    s2_relay(0)
    adv(t_g3[0])
    lax.fori_loop(4, 8, grad_three, 0)
    adv(t_g3[1])
    g4 = dot(et[...], h3[...], 1, 0)
    s2_relay(1)

    def finish_two(lo, total):
        g2b[x, y, lo:lo + 4] = total.astype(bf16)
        for o in range(lo, lo + 4):
            send(g2b.at[x, y, o], z2.at[m, 0], mp_dev(o), zsem.at[4 * m], o)

    t_g2 = [scatter(g2b, p, g2a, None, finish_two, True) for p in range(2)]

    upper, lower = slice(0, 256), slice(256, 512)

    def grad_two_a(i, carry):
        g2f[2 * i], g2f[2 * i + 1] = [
            dot(d2t[:, upper], h1[k, upper], 1, 0) for k in (2 * i, 2 * i + 1)
        ]
        return carry

    def grad_two_b(i, carry):
        pair = (2 * i, 2 * i + 1)
        both = [dot(d2t[:, lower], h1[k, lower], 1, 0) for k in pair]
        both = [(g2f[k] + b).astype(bf16) for b, k in zip(both, pair)]
        for b, k in zip(both, pair):
            g2b[:, :, k] = b.reshape(4, 4, 16, 256)
        return carry

    def grad_one(pair, half):
        back = [dot(d2[half], cw[:, :, k].reshape(256, 256), 1, 0) for k in pair]
        back = [(b * a1[k, half]).astype(bf16) for b, k in zip(back, pair)]
        return [dot(xtb[:, half], b, 1, 0) for b in back]

    def delta_one_a(i, carry):
        g1f[2 * i], g1f[2 * i + 1] = grad_one((2 * i, 2 * i + 1), upper)
        return carry

    def delta_one_b(zz):
        pair = (2 * zz, 2 * zz + 1)
        for side, (k, low) in enumerate(zip(pair, grad_one(pair, lower))):
            own = jnp.where(jnp.full((64, 256), k, jnp.int32) == m, g4, 0.0)
            tall = jnp.transpose(jnp.concatenate([g1f[k] + low, own], axis=0))
            gtb[zz, side] = tall.astype(bf16).reshape(4, 4, 16, 128)

    s2_end(0)
    lax.fori_loop(0, 4, grad_two_a, 0)
    lax.fori_loop(0, 2, delta_one_a, 0)
    s2_end(1)
    lax.fori_loop(0, 2, grad_two_b, 0)
    adv(t_g2[0])
    lax.fori_loop(2, 4, grad_two_b, 0)
    adv(t_g2[1])
    for _ in range(3):
        adv(*t_g3)
    lax.fori_loop(2, 4, delta_one_a, 0)
    gt_d, gt_z = {}, {}

    def gt_join(k):
        zz = ring(z, k)
        gt_d[k].wait_recv()
        gtb[zz, core] = (gtb[zz, core].astype(f32) + gtp[zz].astype(f32)).astype(bf16)
        gt_z[k] = send(gtb.at[zz, core], gtz.at[k - 1], zdev[k])

    for n, k in enumerate((2, 1, 3, 0)):
        zz = ring(z, k)
        delta_one_b(zz)
        gt_d[k] = send(gtb.at[zz, 1 - core], gtp.at[zz], partner)
        if n >= 2:
            gt_join((2, 1)[n - 2])
    gt_join(3)
    gt_d[0].wait_recv()
    total = gtb[z, core].astype(f32) + gtp[z].astype(f32)
    for _ in range(2):
        adv(*t_g2)
    for k in (1, 3, 2):
        gt_z[k].wait_recv()
        total = total + gtz[k - 1].astype(f32)
    gto[...] = total.astype(bf16)
    gt_x = [
        send(gto.at[ring(x, i), ring(y, j)], gtx.at[n], dp_dev(ring(x, i), ring(y, j)))
        for n, (i, j) in enumerate(plane)
    ]
    adv(*t_g2)
    fin(*t_g2)
    fin(*t_g3)
    z2[m, 0] = g2b[x, y, m]
    small = gto[x, y].astype(f32)
    for n, c in enumerate(gt_x):
        c.wait_recv()
        small = small + gtx[n].astype(f32)
    gs_ref[...] = small
    for o in range(8):
        for j in range(4):
            arrived(z2.at[o, j], zsem.at[4 * o + j], None if j else o)
    g2_ref[...] = jnp.transpose(jnp.sum(z2[...].astype(f32), axis=1).reshape(128, 256))
    for c, skip in sent:
        if skip is None:
            c.wait_send()
        else:
            pl.when(m != skip)(c.wait_send)


def run_kernel(*args):
    vm = pltpu.VMEM
    grad = [
        vm((4, 4, 8, 16, 256), bf16), vm((2, 3, 4, 4, 16, 256), bf16), vm((2, 3, 4, 16, 256), bf16),
    ]
    scratch = [
        vm((8, 128, 128), f32), vm((8, 64, 128), f32), vm((3, 64, 128), bf16),
        vm((3, 64, 128), bf16), vm((3, 64, 128), bf16), vm((3, 64, 128), bf16),
        vm((2, 16, 128), f32), vm((8, 16, 256), bf16),
        vm((4, 4, 8, 16, 256), bf16), vm((8, 4, 4, 16, 128), bf16), vm((4, 4, 8, 16, 256), bf16),
        vm((512, 128), bf16), vm((64, 512), bf16),
        vm((8, 512, 256), bf16), vm((8, 512, 256), f32),
        vm((512, 256), f32), vm((512, 256), f32),
        vm((8, 512, 256), bf16), vm((512, 256), bf16), vm((512, 256), bf16),
        vm((512, 256), bf16), vm((256, 512), bf16),
        *[vm((NROW, 64, ROWS), bf16)] * 3, vm((NROW, 3, 64, ROWS), bf16), vm((64, 512), bf16), vm((512, 128), bf16),
        vm((8, 512, 256), bf16), vm((4, 512, 256), bf16), vm((3, 512, 256), bf16),
        *grad, *grad[:2], vm((8, 256, 256), f32), vm((8, 64, 256), f32),
        vm((4, 2, 4, 4, 16, 128), bf16), vm((4, 4, 4, 16, 128), bf16), vm((3, 4, 4, 16, 128), bf16),
        vm((4, 4, 16, 128), bf16), vm((15, 16, 128), bf16), vm((8, 4, 16, 256), bf16),
        pltpu.SemaphoreType.DMA((NSEM,)), pltpu.SemaphoreType.DMA((NSEM,)),
        pltpu.SemaphoreType.DMA((32,)), pltpu.SemaphoreType.DMA((32,)),
    ]
    spec = pl.BlockSpec(memory_space=pltpu.VMEM)
    return pl.pallas_call(
        kernel,
        out_shape=(
            jax.ShapeDtypeStruct((256, 128), f32),
            jax.ShapeDtypeStruct((128, 256), f32),
            jax.ShapeDtypeStruct((16, 128), f32),
        ),
        in_specs=[spec] * 2 + [pl.BlockSpec(memory_space=pltpu.SMEM)] + [spec] * 4,
        out_specs=[spec] * 3,
        scratch_shapes=scratch,
        compiler_params=pltpu.CompilerParams(
            collective_id=0, has_side_effects=True, vmem_limit_bytes=60 * 1024 * 1024
        ),
        name="train_step",
    )(*args)


def update_kernel(
    g2, g3, gs, w_in, w_mid, w_top, w_out, m_in, m_mid, m_top, m_out,
    nw_in, nw_mid, nw_top, nw_out, nm_in, nm_mid, nm_top, nm_out,
):
    small = gs[...]
    grads = (small[:, 0:55], g2[...], g3[...], pltpu.roll(small, 64, 1)[:, 0:53])
    for grad, w, mo, nw, nm in zip(
        grads, (w_in, w_mid, w_top, w_out), (m_in, m_mid, m_top, m_out),
        (nw_in, nw_mid, nw_top, nw_out), (nm_in, nm_mid, nm_top, nm_out),
    ):
        value = momentum_decay * mo[...] + grad
        nm[...] = value
        nw[...] = w[...] - learn_rate * value


def on_device(
    samples, targets, counts,
    weight_in, weight_mid, weight_top, weight_out,
    moment_in, moment_mid, moment_top, moment_out,
):
    g_mid, g_top, g_small = run_kernel(
        jnp.transpose(samples, (1, 0, 2)), jnp.transpose(targets, (1, 0, 2)), counts,
        weight_in.T, weight_mid, weight_top, weight_out,
    )
    spec = pl.BlockSpec(memory_space=pltpu.VMEM)
    shapes = [(16, 55), (256, 128), (128, 256), (16, 53)] * 2
    out = pl.pallas_call(
        update_kernel,
        out_shape=[jax.ShapeDtypeStruct(s, f32) for s in shapes],
        in_specs=[spec] * 11,
        out_specs=[spec] * 8,
        name="update",
    )(
        g_mid, g_top, g_small, weight_in.T, weight_mid, weight_top, weight_out,
        moment_in.T, moment_mid, moment_top, moment_out,
    )
    return (out[0].T, *out[1:4], out[4].T, *out[5:])


def solution(mesh):
    weights = (P(None, ("mp", "dp")), P("mp", "dp"), P("dp", "mp"), P(("mp", "dp"), None))
    in_specs = (P("dp", None, None), P("dp", None, None), P("dp")) + weights + weights
    return jax.shard_map(
        on_device, mesh=mesh, in_specs=in_specs, out_specs=weights + weights, check_vma=False
    )
```

```python
import math

import jax
import jax.numpy as jnp
from jax import lax
from jax.experimental import pallas as pl
from jax.experimental.pallas import tpu as pltpu
from jax.sharding import PartitionSpec as P

momentum_decay = 0.9
learn_rate = 0.05
MESH = pl.DeviceIdType.MESH
f32, bf16 = jnp.float32, jnp.bfloat16
NSEM = 272
NROW = 2
ROWS = 512 // NROW


def gelu_act(value):
    return 0.5 * value * (1.0 + lax.erf(value * (1.0 / math.sqrt(2.0))))


def gelu_slope(value):
    return 0.5 * (1.0 + lax.erf(value * (1.0 / math.sqrt(2.0)))) + value * jnp.exp(
        -0.5 * value * value
    ) * (1.0 / math.sqrt(2.0 * math.pi))


def dot(left, right, a, b):
    return lax.dot_general(left, right, (((a,), (b,)), ((), ())), preferred_element_type=f32)


def adv(*tasks):
    for task in tasks:
        next(task, None)


def fin(*tasks):
    tasks = list(tasks)
    while tasks:
        tasks = [t for t in tasks if next(t, "end") != "end"]


def kernel(
    x_ref, y_ref, n_ref, win_ref, wmid_ref, wtop_ref, wout_ref,
    g2_ref, g3_ref, gs_ref,
    xf, yf, xs, ys, xr, yr, wide, w2s, cw, ct, w3b, xrow, xtb,
    h1, a1, a2, a3, h2f, h3, d3, d2, d2t,
    psend, pp, psum, pr, et, erow,
    s2b, s2p, s2z,
    g3b, g3a, g3x, g2b, g2a, g2f, g1f, gtb, gtp, gtz, gto, gtx, z2,
    ssem, rsem, wsem, zsem,
):
    d, m = lax.axis_index("dp"), lax.axis_index("mp")
    x, y = lax.div(d, 4), lax.rem(d, 4)
    z, core = lax.div(m, 2), lax.rem(m, 2)

    def ring(v, k):
        return lax.rem(v + k, 4)

    def dp_dev(xx, yy):
        return (xx * 4 + yy, m)

    def mp_dev(mm):
        return (d, mm)

    partner = mp_dev(z * 2 + 1 - core)
    zdev = {k: mp_dev(ring(z, k) * 2 + core) for k in (1, 2, 3)}
    mdev = {k: lax.rem(m + k, 8) for k in range(1, 8)}
    plane = [(i, j) for i in range(4) for j in range(4) if i or j]
    plane.sort(key=lambda t: -((t[0] % 2) + (t[0] == 2) * 2 + (t[1] % 2) + (t[1] == 2) * 2))
    pair = dp_dev(ring(x, 2), y)

    count = [0]
    sent = []

    def send(src, dst, dev, sem=None, skip=None):
        k = count[0]
        count[0] += 1
        assert k < NSEM
        copy = pltpu.make_async_remote_copy(
            src_ref=src, dst_ref=dst, send_sem=ssem.at[k],
            recv_sem=rsem.at[k] if sem is None else sem,
            device_id=dev, device_id_type=MESH,
        )
        if skip is None:
            copy.start()
        else:
            pl.when(m != skip)(copy.start)
        sent.append((copy, skip))
        return copy

    def arrived(dst, sem, skip=None):
        copy = pltpu.make_async_remote_copy(
            src_ref=dst, dst_ref=dst, send_sem=ssem.at[0], recv_sem=sem,
            device_id=partner, device_id_type=MESH,
        )
        if skip is None:
            copy.wait_recv()
        else:
            pl.when(m != skip)(copy.wait_recv)

    barrier = pltpu.get_barrier_semaphore()
    peers = [dp_dev(ring(x, i), ring(y, j)) for i, j in plane]
    for i, j in [(0, 0)] + [t for t in plane if 0 in t]:
        peers += [(ring(x, i) * 4 + ring(y, j), mdev[k]) for k in range(1, 8)]
    for dev in peers:
        pl.semaphore_signal(barrier, inc=1, device_id=dev, device_id_type=MESH)

    lanes = lax.broadcasted_iota(jnp.int32, (16, 128), 1)
    wide[...] = jnp.zeros_like(wide)
    wide[0, :, 0:55] = win_ref[...]
    wide[1, :, 0:53] = wout_ref[...]
    tile = wide[0] + pltpu.roll(wide[1], 64, 1)
    tile = jnp.where(lanes == 127, jnp.full((16, 128), n_ref[0], jnp.int32).astype(f32), tile)
    ct[m, x, y] = tile.astype(bf16)
    w2s[...] = jnp.transpose(wmid_ref[...]).astype(bf16).reshape(8, 16, 256)
    w3b[x, y] = wtop_ref[...].astype(bf16).reshape(8, 16, 256)
    cw[x, y, m] = w2s[m]
    xf[...] = jnp.zeros_like(xf)
    yf[...] = jnp.zeros_like(yf)
    xf[:, 0:55] = jnp.transpose(x_ref[...].astype(f32), (1, 0, 2))
    yf[:, 0:53] = jnp.transpose(y_ref[...].astype(f32), (1, 0, 2))
    for q in range(3):
        xs[q] = xf[4 + q, 0:64].astype(bf16)
        ys[q] = yf[4 + q].astype(bf16)
    pl.semaphore_wait(barrier, len(peers))

    def gather(buf, part):
        ms = slice(4 * part, 4 * part + 4)
        pos = (x, y) if part == 0 else (y, x)

        def at(a, b):
            return buf.at[a, b, ms] if part == 0 else buf.at[b, a, ms]

        def dev(a, b):
            return dp_dev(a, b) if part == 0 else dp_dev(b, a)

        own = at(pos[0], pos[1])
        first = {k: send(own, own, dev(ring(pos[0], k), pos[1])) for k in (2, 1, 3)}
        yield
        waits = [send(own, own, dev(pos[0], ring(pos[1], k))) for k in (2, 1, 3)]
        yield
        for k in (1, 3, 2):
            first[k].wait_recv()
            got = at(ring(pos[0], 4 - k), pos[1])
            waits += [send(got, got, dev(pos[0], ring(pos[1], j))) for j in (2, 1, 3)]
            yield
        for c in waits:
            c.wait_recv()

    def gather_two(part):
        ms = slice(4 * part, 4 * part + 4)
        pos = (x, y) if part == 0 else (y, x)
        waits = []
        for j in (0, 1, 3, 2):
            a = ring(pos[0], 4 - j)
            src = (a, pos[1]) if part == 0 else (pos[1], a)
            for o in range(4 * part, 4 * part + 4):
                arrived(cw.at[src[0], src[1], o], wsem.at[4 * o + j], o if j == 0 else None)
            got = cw.at[src[0], src[1], ms]
            for k in (2, 1, 3):
                b = ring(pos[1], k)
                dev = dp_dev(pos[0], b) if part == 0 else dp_dev(b, pos[0])
                waits.append(send(got, got, dev))
            yield
        for c in waits:
            c.wait_recv()

    def scatter(buf, part, abuf, xbuf, finish, direct=False):
        lo = 4 * part
        ms = slice(lo, lo + 4)
        up, ap = (x, y) if part == 0 else (y, x)

        def at(u, a):
            return (u, a, ms) if part == 0 else (a, u, ms)

        def dev(u, a):
            return dp_dev(u, a) if part == 0 else dp_dev(a, u)

        first = {}
        for j in (2, 1, 3, 0):
            u = ring(up, j)
            for k in (2, 1, 3):
                first[j, k] = send(
                    buf.at[at(u, ring(ap, k))], abuf.at[part, k - 1, u], dev(up, ring(ap, k))
                )
        yield
        second = {}
        for j in (2, 1, 3, 0):
            u = ring(up, j)
            for k in (2, 1, 3):
                first[j, k].wait_recv()
            total = buf[at(u, ap)].astype(f32)
            for k in (1, 2, 3):
                total = total + abuf[part, k - 1, u].astype(f32)
            if j:
                buf[at(u, ap)] = total.astype(bf16)
                if direct:
                    for o in range(lo, lo + 4):
                        send(
                            buf.at[(u, ap, o) if part == 0 else (ap, u, o)], z2.at[m, j],
                            (dev(u, ap)[0], o), zsem.at[4 * m + j],
                        )
                    yield
                    continue
                second[j] = send(buf.at[at(u, ap)], xbuf.at[part, j - 1], dev(u, ap))
                yield
        for j in () if direct else (1, 3, 2):
            second[j].wait_recv()
            total = total + xbuf[part, j - 1].astype(f32)
        finish(lo, total)

    own_tile = ct.at[m, x, y]
    tile_copies = [send(own_tile, own_tile, dp_dev(ring(x, i), ring(y, j))) for i, j in plane]
    half = lax.div(m, 4)
    for j in (2, 1, 3, 0):
        there = ring(x, j * (1 - half)) * 4 + ring(y, j * half)
        for k in range(0 if j else 1, 8):
            c = lax.rem(m + k, 8)
            send(w2s.at[c], cw.at[x, y, m], (there, c), wsem.at[4 * m + j])
    x_copy = send(xs, xr, pair)
    t_cw = [gather_two(0), gather_two(1)]
    t_w3 = [gather(w3b, 0), gather(w3b, 1)]
    for c in tile_copies:
        c.wait_recv()
    own_block = ct.at[m]
    block_copies = {k: send(own_block, own_block, zdev[k]) for k in (2, 1, 3)}
    partner_blocks = {0: send(own_block, own_block, partner)}
    for _ in range(4):
        adv(*t_cw)
    adv(*t_w3)

    lane = ct[m].reshape(256, 128).astype(f32)[:, 127:128]
    scale = 2.0 / (jnp.sum(lane, axis=0, keepdims=True) * (1.0 / 16.0) * 128.0)
    mine = ct[m, x, y].astype(f32)[0:1, 127:128]
    theirs = ct[m, ring(x, 2), y].astype(f32)[0:1, 127:128]

    def pick(ref, recv, q):
        value = ref[q, 0:64]
        for k in range(3):
            if q - k < 1:
                continue
            take = jnp.broadcast_to(mine, value.shape) == float(q - k)
            value = jnp.where(take, recv[k].astype(f32), value)
        return value

    x_copy.wait_recv()
    for q in range(4):
        value = pick(xf, xr, q)
        xtb[:, q * 128:(q + 1) * 128] = value.astype(bf16)
        tall = jnp.concatenate([value, jnp.zeros((64, 128), f32)], axis=0)
        xrow[q * 128:(q + 1) * 128] = jnp.transpose(tall).astype(bf16)

    def rows_of(r):
        return slice(r * ROWS, (r + 1) * ROWS)

    def chunks(body, lo=0, n=ROWS, step=32):
        lax.fori_loop(0, n // step, lambda i, c: (body(pl.ds(pl.multiple_of(lo + i * step, step), step)), c)[1], 0)

    def layer_one(k):
        a1[k] = dot(xrow[...], ct[k].reshape(256, 128), 1, 1)

        def act(rr):
            h1[k, rr] = gelu_act(a1[k, rr]).astype(bf16)

        chunks(act, 0, 512)

    def slope_one(lo, hi):
        def body(k, carry):
            def act(rr):
                a1[k, rr] = gelu_slope(a1[k, rr])

            chunks(act, 0, 512)
            return carry

        lax.fori_loop(lo, hi, body, 0)

    layer_one(m)
    partner_blocks[0].wait_recv()
    layer_one(z * 2 + 1 - core)
    for k in (1, 3, 2):
        block_copies[k].wait_recv()
        blk = ring(z, 4 - k) * 2 + core
        partner_blocks[k] = send(ct.at[blk], ct.at[blk], partner)
        layer_one(blk)
    adv(*t_w3)
    y_copy = send(ys, yr, pair)
    for k in (1, 3, 2):
        partner_blocks[k].wait_recv()
        layer_one(ring(z, 4 - k) * 2 + 1 - core)
    fin(*t_cw)

    def layer_two(r):
        total = jnp.zeros((ROWS, 256), f32)
        for k in range(8):
            total = total + dot(h1[k, rows_of(r)], cw[:, :, k].reshape(256, 256), 1, 1)
        a2[rows_of(r)] = total

        def act(rr):
            h2f[m, rr] = gelu_act(a2[rr]).astype(bf16)

        chunks(act, r * ROWS)

    h2_z, h2_p = ([{} for _ in range(NROW)] for _ in range(2))

    def h2_send(r):
        own = h2f.at[m, rows_of(r)]
        for k in (1, 3):
            h2_z[r][k] = send(own, own, zdev[k])
        h2_p[r][0] = send(own, own, partner)

    layer_two(0)
    h2_send(0)
    for _ in range(3):
        adv(*t_w3)
    layer_two(1)
    h2_send(1)
    slope_one(0, 8)

    tm = ct[m].reshape(256, 128)

    h2_far = [[], []]

    def h2_relay(r):
        rows = rows_of(r)
        for k in (1, 3):
            blk = ring(z, 4 - k) * 2 + core
            h2_z[r][k].wait_recv()
            lo = r * ROWS + (0 if k == 1 else ROWS // 2)
            view = h2f.at[blk, slice(lo, lo + ROWS // 2)]
            h2_far[r].append(send(view, view, zdev[k]))
            view = h2f.at[blk, rows]
            h2_p[r][k] = send(view, view, partner)

    def h2_forward(r):
        for c in h2_far[r]:
            c.wait_recv()
        view = h2f.at[ring(z, 2) * 2 + core, rows_of(r)]
        h2_p[r][2] = send(view, view, partner)

    def layer_three(r):
        rows = rows_of(r)

        def part(k):
            return dot(h2f[k, rows], w3b[:, :, k].reshape(256, 256), 1, 0)

        h2_p[r][0].wait_recv()
        total = part(m) + part(z * 2 + 1 - core)
        for k in (1, 3, 2):
            total = total + part(ring(z, 4 - k) * 2 + core)
        a3[rows] = total
        for k in (1, 3, 2):
            h2_p[r][k].wait_recv()
        total = a3[rows]
        for k in (1, 3, 2):
            total = total + part(ring(z, 4 - k) * 2 + 1 - core)
        a3[rows] = total

        def act(rr):
            v = a3[rr]
            h3[rr] = gelu_act(v).astype(bf16)

        chunks(act, r * ROWS)
        psend[r] = jnp.transpose(dot(h3[rows], tm, 1, 0))[64:128].astype(bf16)

    def slope_three(r):
        def act(rr):
            a3[rr] = gelu_slope(a3[rr])

        chunks(act, r * ROWS)

    def slope_two(r):
        def act(rr):
            a2[rr] = gelu_slope(a2[rr])

        chunks(act, r * ROWS)

    def p_task(r):
        c = send(psend.at[r], pp.at[r], partner)
        yield
        c.wait_recv()
        psum[r] = (psend[r].astype(f32) + pp[r].astype(f32)).astype(bf16)
        cs = [send(psum.at[r], pr.at[r, k - 1], zdev[k]) for k in (2, 1, 3)]
        yield
        for c in cs:
            c.wait_recv()

    t_p = [p_task(r) for r in range(NROW)]
    slope_two(0)
    slope_two(1)
    h2_relay(0)
    h2_relay(1)
    h2_forward(0)
    fin(*t_w3)
    layer_three(0)
    adv(t_p[0])
    slope_three(0)
    adv(t_p[0])
    h2_forward(1)
    layer_three(1)
    adv(t_p[1])
    slope_three(1)
    adv(t_p[1])
    y_copy.wait_recv()
    fin(t_p[0])

    sub = lax.broadcasted_iota(jnp.int32, (64, 128), 0)

    def error(r):
        for h in range(4 // NROW):
            q = (4 // NROW) * r + h
            ls = slice(h * 128, (h + 1) * 128)
            want = pick(yf, yr, q)
            own_n = jnp.broadcast_to(mine, (64, 128))
            pair_n = jnp.broadcast_to(theirs, (64, 128))
            live = (own_n > float(q)) | (4.0 + float(q) - own_n < pair_n)
            predicted = psum[r, :, ls].astype(f32)
            for k in range(3):
                predicted = predicted + pr[r, k, :, ls].astype(f32)
            value = jnp.broadcast_to(scale, (64, 128)) * (predicted - want)
            value = jnp.where(live & (sub < 53), value, 0.0)
            et[:, q * 128:(q + 1) * 128] = value.astype(bf16)
            tall = jnp.concatenate([jnp.zeros((64, 128), f32), value], axis=0)
            erow[q * 128:(q + 1) * 128] = jnp.transpose(tall).astype(bf16)

    def delta_three(r):
        d3[rows_of(r)] = (dot(erow[rows_of(r)], tm, 1, 1) * a3[rows_of(r)]).astype(bf16)

    s2_d, s2_s = ([{} for _ in range(NROW)] for _ in range(2))

    def s2_part(r):
        dv = d3[rows_of(r)]
        for own, pair in ((False, (2, 1)), (False, (3, 0)), (True, (2, 1)), (True, (3, 0))):
            zs = [ring(z, k) for k in pair]
            cs = [zz * 2 + (core if own else 1 - core) for zz in zs]
            both = [dot(dv, w3b[:, :, c].reshape(256, 256), 1, 1).astype(bf16) for c in cs]
            for c, b in zip(cs, both):
                s2b[c, rows_of(r)] = b
            for k, zz, c in zip(pair, zs, cs):
                if not own:
                    s2_d[r][k] = send(s2b.at[c, rows_of(r)], s2p.at[zz, rows_of(r)], partner)

    s2_a = [{}, {}]

    def s2_half(r, k):
        lo = r * ROWS + (0 if k == 1 else ROWS // 2)
        return slice(lo, lo + ROWS // 2)

    def s2_join(r):
        rr = rows_of(r)
        for k in (2, 1, 3):
            s2_d[r][k].wait_recv()
            zz = ring(z, k)
            c = zz * 2 + core
            s2b[c, rr] = (s2b[c, rr].astype(f32) + s2p[zz, rr].astype(f32)).astype(bf16)
            if k == 2:
                for j in (1, 3):
                    hh = s2_half(r, j)
                    s2_a[r][j] = send(s2b.at[c, hh], s2z.at[2, hh], zdev[j])

    def s2_relay(r):
        for k in (1, 3):
            s2_a[r][k].wait_recv()
            c, hh = ring(z, k) * 2 + core, s2_half(r, k)
            s2b[c, hh] = (s2b[c, hh].astype(f32) + s2z[2, hh].astype(f32)).astype(bf16)
            s2_s[r][k] = send(s2b.at[c, rows_of(r)], s2z.at[k // 2, rows_of(r)], zdev[k])

    def s2_end(r):
        rr = rows_of(r)
        s2_d[r][0].wait_recv()
        total = s2b[m, rr].astype(f32) + s2p[z, rr].astype(f32)
        for k in (1, 3):
            s2_s[r][k].wait_recv()
            total = total + s2z[k // 2, rr].astype(f32)
        a2[rr] = total * a2[rr]
        d2[rr] = a2[rr].astype(bf16)
        d2t[:, rr] = jnp.transpose(a2[rr]).astype(bf16)

    error(0)
    delta_three(0)
    s2_part(0)
    s2_join(0)
    fin(t_p[1])
    error(1)
    delta_three(1)
    s2_part(1)
    s2_join(1)

    def grad_three(k, carry):
        g3b[:, :, k] = dot(h2f[k], d3[...], 0, 0).astype(bf16).reshape(4, 4, 16, 256)
        return carry

    def finish_three(lo, total):
        g3_ref[lo * 16:(lo + 4) * 16] = total.reshape(64, 256)

    t_g3 = [scatter(g3b, p, g3a, g3x, finish_three) for p in range(2)]
    lax.fori_loop(0, 4, grad_three, 0)
    s2_relay(0)
    adv(t_g3[0])
    lax.fori_loop(4, 8, grad_three, 0)
    adv(t_g3[1])
    g4 = dot(et[...], h3[...], 1, 0)
    s2_relay(1)

    def finish_two(lo, total):
        g2b[x, y, lo:lo + 4] = total.astype(bf16)
        for o in range(lo, lo + 4):
            send(g2b.at[x, y, o], z2.at[m, 0], mp_dev(o), zsem.at[4 * m], o)

    t_g2 = [scatter(g2b, p, g2a, None, finish_two, True) for p in range(2)]

    upper, lower = slice(0, 256), slice(256, 512)

    def grad_two_a(i, carry):
        g2f[2 * i], g2f[2 * i + 1] = [
            dot(d2t[:, upper], h1[k, upper], 1, 0) for k in (2 * i, 2 * i + 1)
        ]
        return carry

    def grad_two_b(i, carry):
        pair = (2 * i, 2 * i + 1)
        both = [dot(d2t[:, lower], h1[k, lower], 1, 0) for k in pair]
        both = [(g2f[k] + b).astype(bf16) for b, k in zip(both, pair)]
        for b, k in zip(both, pair):
            g2b[:, :, k] = b.reshape(4, 4, 16, 256)
        return carry

    def grad_one(pair, half):
        back = [dot(d2[half], cw[:, :, k].reshape(256, 256), 1, 0) for k in pair]
        back = [(b * a1[k, half]).astype(bf16) for b, k in zip(back, pair)]
        return [dot(xtb[:, half], b, 1, 0) for b in back]

    def delta_one_a(i, carry):
        g1f[2 * i], g1f[2 * i + 1] = grad_one((2 * i, 2 * i + 1), upper)
        return carry

    def delta_one_b(zz):
        pair = (2 * zz, 2 * zz + 1)
        for side, (k, low) in enumerate(zip(pair, grad_one(pair, lower))):
            own = jnp.where(jnp.full((64, 256), k, jnp.int32) == m, g4, 0.0)
            tall = jnp.transpose(jnp.concatenate([g1f[k] + low, own], axis=0))
            gtb[zz, side] = tall.astype(bf16).reshape(4, 4, 16, 128)

    s2_end(0)
    lax.fori_loop(0, 4, grad_two_a, 0)
    lax.fori_loop(0, 2, delta_one_a, 0)
    s2_end(1)
    lax.fori_loop(0, 2, grad_two_b, 0)
    adv(t_g2[0])
    lax.fori_loop(2, 4, grad_two_b, 0)
    adv(t_g2[1])
    for _ in range(3):
        adv(*t_g3)
    lax.fori_loop(2, 4, delta_one_a, 0)
    gt_d, gt_z = {}, {}

    def gt_join(k):
        zz = ring(z, k)
        gt_d[k].wait_recv()
        gtb[zz, core] = (gtb[zz, core].astype(f32) + gtp[zz].astype(f32)).astype(bf16)
        gt_z[k] = send(gtb.at[zz, core], gtz.at[k - 1], zdev[k])

    for n, k in enumerate((2, 1, 3, 0)):
        zz = ring(z, k)
        delta_one_b(zz)
        gt_d[k] = send(gtb.at[zz, 1 - core], gtp.at[zz], partner)
        if n >= 2:
            gt_join((2, 1)[n - 2])
    gt_join(3)
    gt_d[0].wait_recv()
    total = gtb[z, core].astype(f32) + gtp[z].astype(f32)
    for _ in range(2):
        adv(*t_g2)
    for k in (1, 3, 2):
        gt_z[k].wait_recv()
        total = total + gtz[k - 1].astype(f32)
    gto[...] = total.astype(bf16)
    gt_x = [
        send(gto.at[ring(x, i), ring(y, j)], gtx.at[n], dp_dev(ring(x, i), ring(y, j)))
        for n, (i, j) in enumerate(plane)
    ]
    adv(*t_g2)
    fin(*t_g2)
    fin(*t_g3)
    z2[m, 0] = g2b[x, y, m]
    small = gto[x, y].astype(f32)
    for n, c in enumerate(gt_x):
        c.wait_recv()
        small = small + gtx[n].astype(f32)
    gs_ref[...] = small
    for o in range(8):
        for j in range(4):
            arrived(z2.at[o, j], zsem.at[4 * o + j], None if j else o)
    g2_ref[...] = jnp.transpose(jnp.sum(z2[...].astype(f32), axis=1).reshape(128, 256))
    for c, skip in sent:
        if skip is None:
            c.wait_send()
        else:
            pl.when(m != skip)(c.wait_send)


def run_kernel(*args):
    vm = pltpu.VMEM
    grad = [
        vm((4, 4, 8, 16, 256), bf16), vm((2, 3, 4, 4, 16, 256), bf16), vm((2, 3, 4, 16, 256), bf16),
    ]
    scratch = [
        vm((8, 128, 128), f32), vm((8, 64, 128), f32), vm((3, 64, 128), bf16),
        vm((3, 64, 128), bf16), vm((3, 64, 128), bf16), vm((3, 64, 128), bf16),
        vm((2, 16, 128), f32), vm((8, 16, 256), bf16),
        vm((4, 4, 8, 16, 256), bf16), vm((8, 4, 4, 16, 128), bf16), vm((4, 4, 8, 16, 256), bf16),
        vm((512, 128), bf16), vm((64, 512), bf16),
        vm((8, 512, 256), bf16), vm((8, 512, 256), f32),
        vm((512, 256), f32), vm((512, 256), f32),
        vm((8, 512, 256), bf16), vm((512, 256), bf16), vm((512, 256), bf16),
        vm((512, 256), bf16), vm((256, 512), bf16),
        *[vm((NROW, 64, ROWS), bf16)] * 3, vm((NROW, 3, 64, ROWS), bf16), vm((64, 512), bf16), vm((512, 128), bf16),
        vm((8, 512, 256), bf16), vm((4, 512, 256), bf16), vm((3, 512, 256), bf16),
        *grad, *grad[:2], vm((8, 256, 256), f32), vm((8, 64, 256), f32),
        vm((4, 2, 4, 4, 16, 128), bf16), vm((4, 4, 4, 16, 128), bf16), vm((3, 4, 4, 16, 128), bf16),
        vm((4, 4, 16, 128), bf16), vm((15, 16, 128), bf16), vm((8, 4, 16, 256), bf16),
        pltpu.SemaphoreType.DMA((NSEM,)), pltpu.SemaphoreType.DMA((NSEM,)),
        pltpu.SemaphoreType.DMA((32,)), pltpu.SemaphoreType.DMA((32,)),
    ]
    spec = pl.BlockSpec(memory_space=pltpu.VMEM)
    return pl.pallas_call(
        kernel,
        out_shape=(
            jax.ShapeDtypeStruct((256, 128), f32),
            jax.ShapeDtypeStruct((128, 256), f32),
            jax.ShapeDtypeStruct((16, 128), f32),
        ),
        in_specs=[spec] * 2 + [pl.BlockSpec(memory_space=pltpu.SMEM)] + [spec] * 4,
        out_specs=[spec] * 3,
        scratch_shapes=scratch,
        compiler_params=pltpu.CompilerParams(
            collective_id=0, has_side_effects=True, vmem_limit_bytes=60 * 1024 * 1024
        ),
        name="train_step",
    )(*args)


def update_kernel(
    g2, g3, gs, w_in, w_mid, w_top, w_out, m_in, m_mid, m_top, m_out,
    nw_in, nw_mid, nw_top, nw_out, nm_in, nm_mid, nm_top, nm_out,
):
    small = gs[...]
    grads = (small[:, 0:55], g2[...], g3[...], pltpu.roll(small, 64, 1)[:, 0:53])
    for grad, w, mo, nw, nm in zip(
        grads, (w_in, w_mid, w_top, w_out), (m_in, m_mid, m_top, m_out),
        (nw_in, nw_mid, nw_top, nw_out), (nm_in, nm_mid, nm_top, nm_out),
    ):
        value = momentum_decay * mo[...] + grad
        nm[...] = value
        nw[...] = w[...] - learn_rate * value


def on_device(
    samples, targets, counts,
    weight_in, weight_mid, weight_top, weight_out,
    moment_in, moment_mid, moment_top, moment_out,
):
    g_mid, g_top, g_small = run_kernel(
        jnp.transpose(samples, (1, 0, 2)), jnp.transpose(targets, (1, 0, 2)), counts,
        weight_in.T, weight_mid, weight_top, weight_out,
    )
    spec = pl.BlockSpec(memory_space=pltpu.VMEM)
    shapes = [(16, 55), (256, 128), (128, 256), (16, 53)] * 2
    out = pl.pallas_call(
        update_kernel,
        out_shape=[jax.ShapeDtypeStruct(s, f32) for s in shapes],
        in_specs=[spec] * 11,
        out_specs=[spec] * 8,
        name="update",
    )(
        g_mid, g_top, g_small, weight_in.T, weight_mid, weight_top, weight_out,
        moment_in.T, moment_mid, moment_top, moment_out,
    )
    return (out[0].T, *out[1:4], out[4].T, *out[5:])


def solution(mesh):
    weights = (P(None, ("mp", "dp")), P("mp", "dp"), P("dp", "mp"), P(("mp", "dp"), None))
    in_specs = (P("dp", None, None), P("dp", None, None), P("dp")) + weights + weights
    return jax.shard_map(
        on_device, mesh=mesh, in_specs=in_specs, out_specs=weights + weights, check_vma=False
    )
```

```python
import math

import jax
import jax.numpy as jnp
from jax import lax
from jax.experimental import pallas as pl
from jax.experimental.pallas import tpu as pltpu
from jax.sharding import PartitionSpec as P

momentum_decay = 0.9
learn_rate = 0.05
MESH = pl.DeviceIdType.MESH
f32, bf16 = jnp.float32, jnp.bfloat16
NSEM = 272
NROW = 2
ROWS = 512 // NROW


def gelu_act(value):
    return 0.5 * value * (1.0 + lax.erf(value * (1.0 / math.sqrt(2.0))))


def gelu_slope(value):
    return 0.5 * (1.0 + lax.erf(value * (1.0 / math.sqrt(2.0)))) + value * jnp.exp(
        -0.5 * value * value
    ) * (1.0 / math.sqrt(2.0 * math.pi))


def dot(left, right, a, b):
    return lax.dot_general(left, right, (((a,), (b,)), ((), ())), preferred_element_type=f32)


def adv(*tasks):
    for task in tasks:
        next(task, None)


def fin(*tasks):
    tasks = list(tasks)
    while tasks:
        tasks = [t for t in tasks if next(t, "end") != "end"]


def kernel(
    x_ref, y_ref, n_ref, win_ref, wmid_ref, wtop_ref, wout_ref,
    g2_ref, g3_ref, gs_ref,
    xf, yf, xs, ys, xr, yr, wide, w2s, cw, ct, w3b, xrow, xtb,
    h1, a1, a2, a3, h2f, h3, d3, d2, d2t,
    psend, pp, psum, pr, et, erow,
    s2b, s2p, s2z,
    g3b, g3a, g3x, g2b, g2a, g2f, g1f, gtb, gtp, gtz, gto, gtx, z2,
    ssem, rsem, wsem, zsem,
):
    d, m = lax.axis_index("dp"), lax.axis_index("mp")
    x, y = lax.div(d, 4), lax.rem(d, 4)
    z, core = lax.div(m, 2), lax.rem(m, 2)

    def ring(v, k):
        return lax.rem(v + k, 4)

    def dp_dev(xx, yy):
        return (xx * 4 + yy, m)

    def mp_dev(mm):
        return (d, mm)

    partner = mp_dev(z * 2 + 1 - core)
    zdev = {k: mp_dev(ring(z, k) * 2 + core) for k in (1, 2, 3)}
    mdev = {k: lax.rem(m + k, 8) for k in range(1, 8)}
    plane = [(i, j) for i in range(4) for j in range(4) if i or j]
    plane.sort(key=lambda t: -((t[0] % 2) + (t[0] == 2) * 2 + (t[1] % 2) + (t[1] == 2) * 2))
    pair = dp_dev(ring(x, 2), y)

    count = [0]
    sent = []

    def send(src, dst, dev, sem=None, skip=None):
        k = count[0]
        count[0] += 1
        assert k < NSEM
        copy = pltpu.make_async_remote_copy(
            src_ref=src, dst_ref=dst, send_sem=ssem.at[k],
            recv_sem=rsem.at[k] if sem is None else sem,
            device_id=dev, device_id_type=MESH,
        )
        if skip is None:
            copy.start()
        else:
            pl.when(m != skip)(copy.start)
        sent.append((copy, skip))
        return copy

    def arrived(dst, sem, skip=None):
        copy = pltpu.make_async_remote_copy(
            src_ref=dst, dst_ref=dst, send_sem=ssem.at[0], recv_sem=sem,
            device_id=partner, device_id_type=MESH,
        )
        if skip is None:
            copy.wait_recv()
        else:
            pl.when(m != skip)(copy.wait_recv)

    barrier = pltpu.get_barrier_semaphore()
    peers = [dp_dev(ring(x, i), ring(y, j)) for i, j in plane]
    for i, j in [(0, 0)] + [t for t in plane if 0 in t]:
        peers += [(ring(x, i) * 4 + ring(y, j), mdev[k]) for k in range(1, 8)]
    for dev in peers:
        pl.semaphore_signal(barrier, inc=1, device_id=dev, device_id_type=MESH)

    lanes = lax.broadcasted_iota(jnp.int32, (16, 128), 1)
    wide[...] = jnp.zeros_like(wide)
    wide[0, :, 0:55] = win_ref[...]
    wide[1, :, 0:53] = wout_ref[...]
    tile = wide[0] + pltpu.roll(wide[1], 64, 1)
    tile = jnp.where(lanes == 127, jnp.full((16, 128), n_ref[0], jnp.int32).astype(f32), tile)
    ct[m, x, y] = tile.astype(bf16)
    w2s[...] = jnp.transpose(wmid_ref[...]).astype(bf16).reshape(8, 16, 256)
    w3b[x, y] = wtop_ref[...].astype(bf16).reshape(8, 16, 256)
    cw[x, y, m] = w2s[m]
    xf[...] = jnp.zeros_like(xf)
    yf[...] = jnp.zeros_like(yf)
    xf[:, 0:55] = jnp.transpose(x_ref[...].astype(f32), (1, 0, 2))
    yf[:, 0:53] = jnp.transpose(y_ref[...].astype(f32), (1, 0, 2))
    for q in range(3):
        xs[q] = xf[4 + q, 0:64].astype(bf16)
        ys[q] = yf[4 + q].astype(bf16)
    pl.semaphore_wait(barrier, len(peers))

    def gather(buf, part):
        ms = slice(4 * part, 4 * part + 4)
        pos = (x, y) if part == 0 else (y, x)

        def at(a, b):
            return buf.at[a, b, ms] if part == 0 else buf.at[b, a, ms]

        def dev(a, b):
            return dp_dev(a, b) if part == 0 else dp_dev(b, a)

        own = at(pos[0], pos[1])
        first = {k: send(own, own, dev(ring(pos[0], k), pos[1])) for k in (2, 1, 3)}
        yield
        waits = [send(own, own, dev(pos[0], ring(pos[1], k))) for k in (2, 1, 3)]
        yield
        for k in (1, 3, 2):
            first[k].wait_recv()
            got = at(ring(pos[0], 4 - k), pos[1])
            waits += [send(got, got, dev(pos[0], ring(pos[1], j))) for j in (2, 1, 3)]
            yield
        for c in waits:
            c.wait_recv()

    def gather_two(part):
        ms = slice(4 * part, 4 * part + 4)
        pos = (x, y) if part == 0 else (y, x)
        waits = []
        for j in (0, 1, 3, 2):
            a = ring(pos[0], 4 - j)
            src = (a, pos[1]) if part == 0 else (pos[1], a)
            for o in range(4 * part, 4 * part + 4):
                arrived(cw.at[src[0], src[1], o], wsem.at[4 * o + j], o if j == 0 else None)
            got = cw.at[src[0], src[1], ms]
            for k in (2, 1, 3):
                b = ring(pos[1], k)
                dev = dp_dev(pos[0], b) if part == 0 else dp_dev(b, pos[0])
                waits.append(send(got, got, dev))
            yield
        for c in waits:
            c.wait_recv()

    def scatter(buf, part, abuf, xbuf, finish, direct=False):
        lo = 4 * part
        ms = slice(lo, lo + 4)
        up, ap = (x, y) if part == 0 else (y, x)

        def at(u, a):
            return (u, a, ms) if part == 0 else (a, u, ms)

        def dev(u, a):
            return dp_dev(u, a) if part == 0 else dp_dev(a, u)

        first = {}
        for j in (2, 1, 3, 0):
            u = ring(up, j)
            for k in (2, 1, 3):
                first[j, k] = send(
                    buf.at[at(u, ring(ap, k))], abuf.at[part, k - 1, u], dev(up, ring(ap, k))
                )
        yield
        second = {}
        for j in (2, 1, 3, 0):
            u = ring(up, j)
            for k in (2, 1, 3):
                first[j, k].wait_recv()
            total = buf[at(u, ap)].astype(f32)
            for k in (1, 2, 3):
                total = total + abuf[part, k - 1, u].astype(f32)
            if j:
                buf[at(u, ap)] = total.astype(bf16)
                if direct:
                    for o in range(lo, lo + 4):
                        send(
                            buf.at[(u, ap, o) if part == 0 else (ap, u, o)], z2.at[m, j],
                            (dev(u, ap)[0], o), zsem.at[4 * m + j],
                        )
                    yield
                    continue
                second[j] = send(buf.at[at(u, ap)], xbuf.at[part, j - 1], dev(u, ap))
                yield
        for j in () if direct else (1, 3, 2):
            second[j].wait_recv()
            total = total + xbuf[part, j - 1].astype(f32)
        finish(lo, total)

    own_tile = ct.at[m, x, y]
    tile_copies = [send(own_tile, own_tile, dp_dev(ring(x, i), ring(y, j))) for i, j in plane]
    half = lax.div(m, 4)
    for j in (2, 1, 3, 0):
        there = ring(x, j * (1 - half)) * 4 + ring(y, j * half)
        for k in range(0 if j else 1, 8):
            c = lax.rem(m + k, 8)
            send(w2s.at[c], cw.at[x, y, m], (there, c), wsem.at[4 * m + j])
    x_copy = send(xs, xr, pair)
    t_cw = [gather_two(0), gather_two(1)]
    t_w3 = [gather(w3b, 0), gather(w3b, 1)]
    for c in tile_copies:
        c.wait_recv()
    own_block = ct.at[m]
    block_copies = {k: send(own_block, own_block, zdev[k]) for k in (2, 1, 3)}
    partner_blocks = {0: send(own_block, own_block, partner)}
    for _ in range(4):
        adv(*t_cw)
    adv(*t_w3)

    lane = ct[m].reshape(256, 128).astype(f32)[:, 127:128]
    scale = 2.0 / (jnp.sum(lane, axis=0, keepdims=True) * (1.0 / 16.0) * 128.0)
    mine = ct[m, x, y].astype(f32)[0:1, 127:128]
    theirs = ct[m, ring(x, 2), y].astype(f32)[0:1, 127:128]

    def pick(ref, recv, q):
        value = ref[q, 0:64]
        for k in range(3):
            if q - k < 1:
                continue
            take = jnp.broadcast_to(mine, value.shape) == float(q - k)
            value = jnp.where(take, recv[k].astype(f32), value)
        return value

    x_copy.wait_recv()
    for q in range(4):
        value = pick(xf, xr, q)
        xtb[:, q * 128:(q + 1) * 128] = value.astype(bf16)
        tall = jnp.concatenate([value, jnp.zeros((64, 128), f32)], axis=0)
        xrow[q * 128:(q + 1) * 128] = jnp.transpose(tall).astype(bf16)

    def rows_of(r):
        return slice(r * ROWS, (r + 1) * ROWS)

    def chunks(body, lo=0, n=ROWS, step=32):
        lax.fori_loop(0, n // step, lambda i, c: (body(pl.ds(pl.multiple_of(lo + i * step, step), step)), c)[1], 0)

    def layer_one(k):
        a1[k] = dot(xrow[...], ct[k].reshape(256, 128), 1, 1)

        def act(rr):
            h1[k, rr] = gelu_act(a1[k, rr]).astype(bf16)

        chunks(act, 0, 512)

    def slope_one(lo, hi):
        def body(k, carry):
            def act(rr):
                a1[k, rr] = gelu_slope(a1[k, rr])

            chunks(act, 0, 512)
            return carry

        lax.fori_loop(lo, hi, body, 0)

    layer_one(m)
    partner_blocks[0].wait_recv()
    layer_one(z * 2 + 1 - core)
    for k in (1, 3, 2):
        block_copies[k].wait_recv()
        blk = ring(z, 4 - k) * 2 + core
        partner_blocks[k] = send(ct.at[blk], ct.at[blk], partner)
        layer_one(blk)
    adv(*t_w3)
    y_copy = send(ys, yr, pair)
    for k in (1, 3, 2):
        partner_blocks[k].wait_recv()
        layer_one(ring(z, 4 - k) * 2 + 1 - core)
    fin(*t_cw)

    def layer_two(r):
        total = jnp.zeros((ROWS, 256), f32)
        for k in range(8):
            total = total + dot(h1[k, rows_of(r)], cw[:, :, k].reshape(256, 256), 1, 1)
        a2[rows_of(r)] = total

        def act(rr):
            h2f[m, rr] = gelu_act(a2[rr]).astype(bf16)

        chunks(act, r * ROWS)

    h2_z, h2_p = ([{} for _ in range(NROW)] for _ in range(2))

    def h2_send(r):
        own = h2f.at[m, rows_of(r)]
        for k in (1, 3):
            h2_z[r][k] = send(own, own, zdev[k])
        h2_p[r][0] = send(own, own, partner)

    layer_two(0)
    h2_send(0)
    for _ in range(3):
        adv(*t_w3)
    layer_two(1)
    h2_send(1)
    slope_one(0, 8)

    tm = ct[m].reshape(256, 128)

    h2_far = [[], []]

    def h2_relay(r):
        rows = rows_of(r)
        for k in (1, 3):
            blk = ring(z, 4 - k) * 2 + core
            h2_z[r][k].wait_recv()
            lo = r * ROWS + (0 if k == 1 else ROWS // 2)
            view = h2f.at[blk, slice(lo, lo + ROWS // 2)]
            h2_far[r].append(send(view, view, zdev[k]))
            view = h2f.at[blk, rows]
            h2_p[r][k] = send(view, view, partner)

    def h2_forward(r):
        for c in h2_far[r]:
            c.wait_recv()
        view = h2f.at[ring(z, 2) * 2 + core, rows_of(r)]
        h2_p[r][2] = send(view, view, partner)

    def layer_three(r):
        rows = rows_of(r)

        def part(k):
            return dot(h2f[k, rows], w3b[:, :, k].reshape(256, 256), 1, 0)

        h2_p[r][0].wait_recv()
        total = part(m) + part(z * 2 + 1 - core)
        for k in (1, 3, 2):
            total = total + part(ring(z, 4 - k) * 2 + core)
        a3[rows] = total
        for k in (1, 3, 2):
            h2_p[r][k].wait_recv()
        total = a3[rows]
        for k in (1, 3, 2):
            total = total + part(ring(z, 4 - k) * 2 + 1 - core)
        a3[rows] = total

        def act(rr):
            v = a3[rr]
            h3[rr] = gelu_act(v).astype(bf16)

        chunks(act, r * ROWS)
        psend[r] = jnp.transpose(dot(h3[rows], tm, 1, 0))[64:128].astype(bf16)

    def slope_three(r):
        def act(rr):
            a3[rr] = gelu_slope(a3[rr])

        chunks(act, r * ROWS)

    def slope_two(r):
        def act(rr):
            a2[rr] = gelu_slope(a2[rr])

        chunks(act, r * ROWS)

    def p_task(r):
        c = send(psend.at[r], pp.at[r], partner)
        yield
        c.wait_recv()
        psum[r] = (psend[r].astype(f32) + pp[r].astype(f32)).astype(bf16)
        cs = [send(psum.at[r], pr.at[r, k - 1], zdev[k]) for k in (2, 1, 3)]
        yield
        for c in cs:
            c.wait_recv()

    t_p = [p_task(r) for r in range(NROW)]
    slope_two(0)
    slope_two(1)
    h2_relay(0)
    h2_relay(1)
    h2_forward(0)
    fin(*t_w3)
    layer_three(0)
    adv(t_p[0])
    slope_three(0)
    h2_forward(1)
    adv(t_p[0])
    layer_three(1)
    adv(t_p[1])
    slope_three(1)
    adv(t_p[1])
    y_copy.wait_recv()
    fin(t_p[0])

    sub = lax.broadcasted_iota(jnp.int32, (64, 128), 0)

    def error(r):
        for h in range(4 // NROW):
            q = (4 // NROW) * r + h
            ls = slice(h * 128, (h + 1) * 128)
            want = pick(yf, yr, q)
            own_n = jnp.broadcast_to(mine, (64, 128))
            pair_n = jnp.broadcast_to(theirs, (64, 128))
            live = (own_n > float(q)) | (4.0 + float(q) - own_n < pair_n)
            predicted = psum[r, :, ls].astype(f32)
            for k in range(3):
                predicted = predicted + pr[r, k, :, ls].astype(f32)
            value = jnp.broadcast_to(scale, (64, 128)) * (predicted - want)
            value = jnp.where(live & (sub < 53), value, 0.0)
            et[:, q * 128:(q + 1) * 128] = value.astype(bf16)
            tall = jnp.concatenate([jnp.zeros((64, 128), f32), value], axis=0)
            erow[q * 128:(q + 1) * 128] = jnp.transpose(tall).astype(bf16)

    def delta_three(r):
        d3[rows_of(r)] = (dot(erow[rows_of(r)], tm, 1, 1) * a3[rows_of(r)]).astype(bf16)

    s2_d, s2_s = ([{} for _ in range(NROW)] for _ in range(2))

    def s2_part(r):
        dv = d3[rows_of(r)]
        for own, pair in ((False, (2, 1)), (False, (3, 0)), (True, (2, 1)), (True, (3, 0))):
            zs = [ring(z, k) for k in pair]
            cs = [zz * 2 + (core if own else 1 - core) for zz in zs]
            both = [dot(dv, w3b[:, :, c].reshape(256, 256), 1, 1).astype(bf16) for c in cs]
            for c, b in zip(cs, both):
                s2b[c, rows_of(r)] = b
            for k, zz, c in zip(pair, zs, cs):
                if not own:
                    s2_d[r][k] = send(s2b.at[c, rows_of(r)], s2p.at[zz, rows_of(r)], partner)

    s2_a = [{}, {}]

    def s2_half(r, k):
        lo = r * ROWS + (0 if k == 1 else ROWS // 2)
        return slice(lo, lo + ROWS // 2)

    def s2_join(r):
        rr = rows_of(r)
        for k in (2, 1, 3):
            s2_d[r][k].wait_recv()
            zz = ring(z, k)
            c = zz * 2 + core
            s2b[c, rr] = (s2b[c, rr].astype(f32) + s2p[zz, rr].astype(f32)).astype(bf16)
            if k == 2:
                for j in (1, 3):
                    hh = s2_half(r, j)
                    s2_a[r][j] = send(s2b.at[c, hh], s2z.at[2, hh], zdev[j])

    def s2_relay(r):
        for k in (1, 3):
            s2_a[r][k].wait_recv()
            c, hh = ring(z, k) * 2 + core, s2_half(r, k)
            s2b[c, hh] = (s2b[c, hh].astype(f32) + s2z[2, hh].astype(f32)).astype(bf16)
            s2_s[r][k] = send(s2b.at[c, rows_of(r)], s2z.at[k // 2, rows_of(r)], zdev[k])

    def s2_end(r):
        rr = rows_of(r)
        s2_d[r][0].wait_recv()
        total = s2b[m, rr].astype(f32) + s2p[z, rr].astype(f32)
        for k in (1, 3):
            s2_s[r][k].wait_recv()
            total = total + s2z[k // 2, rr].astype(f32)
        a2[rr] = total * a2[rr]
        d2[rr] = a2[rr].astype(bf16)
        d2t[:, rr] = jnp.transpose(a2[rr]).astype(bf16)

    error(0)
    delta_three(0)
    s2_part(0)
    s2_join(0)
    fin(t_p[1])
    error(1)
    delta_three(1)
    s2_part(1)
    s2_join(1)

    def grad_three(k, carry):
        g3b[:, :, k] = dot(h2f[k], d3[...], 0, 0).astype(bf16).reshape(4, 4, 16, 256)
        return carry

    def finish_three(lo, total):
        g3_ref[lo * 16:(lo + 4) * 16] = total.reshape(64, 256)

    t_g3 = [scatter(g3b, p, g3a, g3x, finish_three) for p in range(2)]
    lax.fori_loop(0, 4, grad_three, 0)
    s2_relay(0)
    adv(t_g3[0])
    lax.fori_loop(4, 8, grad_three, 0)
    adv(t_g3[1])
    g4 = dot(et[...], h3[...], 1, 0)
    s2_relay(1)

    def finish_two(lo, total):
        g2b[x, y, lo:lo + 4] = total.astype(bf16)
        for o in range(lo, lo + 4):
            send(g2b.at[x, y, o], z2.at[m, 0], mp_dev(o), zsem.at[4 * m], o)

    t_g2 = [scatter(g2b, p, g2a, None, finish_two, True) for p in range(2)]

    upper, lower = slice(0, 256), slice(256, 512)

    def grad_two_a(i, carry):
        g2f[2 * i], g2f[2 * i + 1] = [
            dot(d2t[:, upper], h1[k, upper], 1, 0) for k in (2 * i, 2 * i + 1)
        ]
        return carry

    def grad_two_b(i, carry):
        pair = (2 * i, 2 * i + 1)
        both = [dot(d2t[:, lower], h1[k, lower], 1, 0) for k in pair]
        both = [(g2f[k] + b).astype(bf16) for b, k in zip(both, pair)]
        for b, k in zip(both, pair):
            g2b[:, :, k] = b.reshape(4, 4, 16, 256)
        return carry

    def grad_one(pair, half):
        back = [dot(d2[half], cw[:, :, k].reshape(256, 256), 1, 0) for k in pair]
        back = [(b * a1[k, half]).astype(bf16) for b, k in zip(back, pair)]
        return [dot(xtb[:, half], b, 1, 0) for b in back]

    def delta_one_a(i, carry):
        g1f[2 * i], g1f[2 * i + 1] = grad_one((2 * i, 2 * i + 1), upper)
        return carry

    def delta_one_b(zz):
        pair = (2 * zz, 2 * zz + 1)
        for side, (k, low) in enumerate(zip(pair, grad_one(pair, lower))):
            own = jnp.where(jnp.full((64, 256), k, jnp.int32) == m, g4, 0.0)
            tall = jnp.transpose(jnp.concatenate([g1f[k] + low, own], axis=0))
            gtb[zz, side] = tall.astype(bf16).reshape(4, 4, 16, 128)

    s2_end(0)
    lax.fori_loop(0, 4, grad_two_a, 0)
    lax.fori_loop(0, 2, delta_one_a, 0)
    s2_end(1)
    lax.fori_loop(0, 2, grad_two_b, 0)
    adv(t_g2[0])
    lax.fori_loop(2, 4, grad_two_b, 0)
    adv(t_g2[1])
    for _ in range(3):
        adv(*t_g3)
    lax.fori_loop(2, 4, delta_one_a, 0)
    gt_d, gt_z = {}, {}

    def gt_join(k):
        zz = ring(z, k)
        gt_d[k].wait_recv()
        gtb[zz, core] = (gtb[zz, core].astype(f32) + gtp[zz].astype(f32)).astype(bf16)
        gt_z[k] = send(gtb.at[zz, core], gtz.at[k - 1], zdev[k])

    for n, k in enumerate((2, 1, 3, 0)):
        zz = ring(z, k)
        delta_one_b(zz)
        gt_d[k] = send(gtb.at[zz, 1 - core], gtp.at[zz], partner)
        if n >= 2:
            gt_join((2, 1)[n - 2])
    gt_join(3)
    gt_d[0].wait_recv()
    total = gtb[z, core].astype(f32) + gtp[z].astype(f32)
    for _ in range(2):
        adv(*t_g2)
    for k in (1, 3, 2):
        gt_z[k].wait_recv()
        total = total + gtz[k - 1].astype(f32)
    gto[...] = total.astype(bf16)
    gt_x = [
        send(gto.at[ring(x, i), ring(y, j)], gtx.at[n], dp_dev(ring(x, i), ring(y, j)))
        for n, (i, j) in enumerate(plane)
    ]
    adv(*t_g2)
    fin(*t_g2)
    fin(*t_g3)
    z2[m, 0] = g2b[x, y, m]
    small = gto[x, y].astype(f32)
    for n, c in enumerate(gt_x):
        c.wait_recv()
        small = small + gtx[n].astype(f32)
    gs_ref[...] = small
    for o in range(8):
        for j in range(4):
            arrived(z2.at[o, j], zsem.at[4 * o + j], None if j else o)
    g2_ref[...] = jnp.transpose(jnp.sum(z2[...].astype(f32), axis=1).reshape(128, 256))
    for c, skip in sent:
        if skip is None:
            c.wait_send()
        else:
            pl.when(m != skip)(c.wait_send)


def run_kernel(*args):
    vm = pltpu.VMEM
    grad = [
        vm((4, 4, 8, 16, 256), bf16), vm((2, 3, 4, 4, 16, 256), bf16), vm((2, 3, 4, 16, 256), bf16),
    ]
    scratch = [
        vm((8, 128, 128), f32), vm((8, 64, 128), f32), vm((3, 64, 128), bf16),
        vm((3, 64, 128), bf16), vm((3, 64, 128), bf16), vm((3, 64, 128), bf16),
        vm((2, 16, 128), f32), vm((8, 16, 256), bf16),
        vm((4, 4, 8, 16, 256), bf16), vm((8, 4, 4, 16, 128), bf16), vm((4, 4, 8, 16, 256), bf16),
        vm((512, 128), bf16), vm((64, 512), bf16),
        vm((8, 512, 256), bf16), vm((8, 512, 256), f32),
        vm((512, 256), f32), vm((512, 256), f32),
        vm((8, 512, 256), bf16), vm((512, 256), bf16), vm((512, 256), bf16),
        vm((512, 256), bf16), vm((256, 512), bf16),
        *[vm((NROW, 64, ROWS), bf16)] * 3, vm((NROW, 3, 64, ROWS), bf16), vm((64, 512), bf16), vm((512, 128), bf16),
        vm((8, 512, 256), bf16), vm((4, 512, 256), bf16), vm((3, 512, 256), bf16),
        *grad, *grad[:2], vm((8, 256, 256), f32), vm((8, 64, 256), f32),
        vm((4, 2, 4, 4, 16, 128), bf16), vm((4, 4, 4, 16, 128), bf16), vm((3, 4, 4, 16, 128), bf16),
        vm((4, 4, 16, 128), bf16), vm((15, 16, 128), bf16), vm((8, 4, 16, 256), bf16),
        pltpu.SemaphoreType.DMA((NSEM,)), pltpu.SemaphoreType.DMA((NSEM,)),
        pltpu.SemaphoreType.DMA((32,)), pltpu.SemaphoreType.DMA((32,)),
    ]
    spec = pl.BlockSpec(memory_space=pltpu.VMEM)
    return pl.pallas_call(
        kernel,
        out_shape=(
            jax.ShapeDtypeStruct((256, 128), f32),
            jax.ShapeDtypeStruct((128, 256), f32),
            jax.ShapeDtypeStruct((16, 128), f32),
        ),
        in_specs=[spec] * 2 + [pl.BlockSpec(memory_space=pltpu.SMEM)] + [spec] * 4,
        out_specs=[spec] * 3,
        scratch_shapes=scratch,
        compiler_params=pltpu.CompilerParams(
            collective_id=0, has_side_effects=True, vmem_limit_bytes=60 * 1024 * 1024
        ),
        name="train_step",
    )(*args)


def update_kernel(
    g2, g3, gs, w_in, w_mid, w_top, w_out, m_in, m_mid, m_top, m_out,
    nw_in, nw_mid, nw_top, nw_out, nm_in, nm_mid, nm_top, nm_out,
):
    small = gs[...]
    grads = (small[:, 0:55], g2[...], g3[...], pltpu.roll(small, 64, 1)[:, 0:53])
    for grad, w, mo, nw, nm in zip(
        grads, (w_in, w_mid, w_top, w_out), (m_in, m_mid, m_top, m_out),
        (nw_in, nw_mid, nw_top, nw_out), (nm_in, nm_mid, nm_top, nm_out),
    ):
        value = momentum_decay * mo[...] + grad
        nm[...] = value
        nw[...] = w[...] - learn_rate * value


def on_device(
    samples, targets, counts,
    weight_in, weight_mid, weight_top, weight_out,
    moment_in, moment_mid, moment_top, moment_out,
):
    g_mid, g_top, g_small = run_kernel(
        jnp.transpose(samples, (1, 0, 2)), jnp.transpose(targets, (1, 0, 2)), counts,
        weight_in.T, weight_mid, weight_top, weight_out,
    )
    spec = pl.BlockSpec(memory_space=pltpu.VMEM)
    shapes = [(16, 55), (256, 128), (128, 256), (16, 53)] * 2
    out = pl.pallas_call(
        update_kernel,
        out_shape=[jax.ShapeDtypeStruct(s, f32) for s in shapes],
        in_specs=[spec] * 11,
        out_specs=[spec] * 8,
        name="update",
    )(
        g_mid, g_top, g_small, weight_in.T, weight_mid, weight_top, weight_out,
        moment_in.T, moment_mid, moment_top, moment_out,
    )
    return (out[0].T, *out[1:4], out[4].T, *out[5:])


def solution(mesh):
    weights = (P(None, ("mp", "dp")), P("mp", "dp"), P("dp", "mp"), P(("mp", "dp"), None))
    in_specs = (P("dp", None, None), P("dp", None, None), P("dp")) + weights + weights
    return jax.shard_map(
        on_device, mesh=mesh, in_specs=in_specs, out_specs=weights + weights, check_vma=False
    )
```
